32 devices in a mesh: wide: 8 (over z, y), narrow: 4 (over x, core).
Axes of the slice: x: 2, y: 2, z: 4, core: 2. Of those that a mesh axis runs over, the one named last changes fastest.
Arguments:
- inputs: bfloat16 [16, 512, 1536], P('wide'), may hold values from -6 to 6
- out_grad: bfloat16 [16, 512, 1536], P('wide'), may hold values from -6 to 6
- norm_gain: bfloat16 [1536], replicated, may hold values from 0.5 to 1.5
- query_weight: bfloat16 [1536, 1536], P(None, 'narrow'), may hold values from -0.15625 to 0.15625
- query_bias: bfloat16 [1536], P('narrow'), may hold values from -3 to 3
- key_weight: bfloat16 [1536, 256], P(None, 'narrow'), may hold values from -0.15625 to 0.15625
- key_bias: bfloat16 [256], P('narrow'), may hold values from -3 to 3
- value_weight: bfloat16 [1536, 256], P(None, 'narrow'), may hold values from -0.15625 to 0.15625
- value_bias: bfloat16 [256], P('narrow'), may hold values from -3 to 3
- output_weight: bfloat16 [1536, 1536], P('narrow'), may hold values from -0.875 to 0.875
- ffn_gain: bfloat16 [1536], replicated, may hold values from 0.5 to 1.5
- gate_weight: bfloat16 [1536, 8960], P(None, 'narrow'), may hold values from -0.15625 to 0.15625
- up_weight: bfloat16 [1536, 8960], P(None, 'narrow'), may hold values from -0.15625 to 0.15625
- down_weight: bfloat16 [8960, 1536], P('narrow'), may hold values from -0.125 to 0.125
- lengths: int32 [16], P('wide'), may hold values from 256 to 512, as said below
- segments: int32 [16, 512], P('wide'), may hold values from 0 to 3, as said below
- positions: int32 [16, 512], P('wide'), may hold values from 0 to 511, as said below
Outputs:
- result: bfloat16 [16, 512, 1536], P('wide')
- input_grad: bfloat16 [16, 512, 1536], P('wide')
- norm_gain_grad: float32 [1536], replicated
- query_weight_grad: float32 [1536, 1536], P('wide', 'narrow')
- query_bias_grad: float32 [1536], P('narrow')
- key_weight_grad: float32 [1536, 256], P('wide', 'narrow')
- key_bias_grad: float32 [256], P('narrow')
- value_weight_grad: float32 [1536, 256], P('wide', 'narrow')
- value_bias_grad: float32 [256], P('narrow')
- output_weight_grad: float32 [1536, 1536], P('narrow', 'wide')
- ffn_gain_grad: float32 [1536], replicated
- gate_weight_grad: float32 [1536, 8960], P('wide', 'narrow')
- up_weight_grad: float32 [1536, 8960], P('wide', 'narrow')
- down_weight_grad: float32 [8960, 1536], P('narrow', 'wide')
The draws below stay inside these ranges and needn't reach their ends.
Inputs may be any that keep to these rules, and one draw needn't show every extreme that they name: `lengths`: the first row of the whole batch has all 512 tokens valid and the second row has 256. `segments`: document ids of a row start at 0 and never fall along the row; a row holds at most 4 documents. `positions`: A token's position within its document: 0 at the document's first token, rising by one.
All inputs are finite; a program needn't handle non-finite values.
Results may differ from the reference program's by a relative error of at most 0.018.
Values may be sent and summed in bfloat16 or wider, within the bound.
No kernel may reach another device: no remote copies, remote signals or barrier semaphores. Data moves between devices by JAX's collectives and lax.ppermute only.
A program may use at most 256 MiB of HBM per device.

```python
import jax
import jax.numpy as jnp
from jax import lax

D = 1536
H = 12
KVH = 2
HD = 128
FF = 8960
SEQ = 512
CUTS = 3
ROWS = 16


def document_layout(key):
    cut_key = jax.random.fold_in(key, 11)
    length_key = jax.random.fold_in(key, 12)
    cuts = jax.random.randint(cut_key, (ROWS, CUTS), 1, SEQ)
    cuts = cuts.at[0].set(SEQ)
    row_lengths = jax.random.randint(length_key, (ROWS,), SEQ // 2, SEQ + 1)
    row_lengths = row_lengths.at[0].set(SEQ).at[1].set(SEQ // 2)
    col_ids = jnp.arange(SEQ, dtype=jnp.int32)
    passed = cuts[:, None, :] <= col_ids[None, :, None]
    doc_ids = jnp.sum(passed.astype(jnp.int32), axis=-1)
    doc_start = jnp.max(jnp.where(passed, cuts[:, None, :], 0), axis=-1)
    doc_positions = col_ids[None, :] - doc_start
    return (row_lengths.astype(jnp.int32), doc_ids.astype(jnp.int32), doc_positions.astype(jnp.int32))


def draw_lengths(key, part):
    return document_layout(key)[0]


def draw_segments(key, part):
    return document_layout(key)[1]


def draw_positions(key, part):
    return document_layout(key)[2]


def shard_levels(stream_key, dims, shards, low, top_value):
    level, own = 1.0, jax.random.fold_in(stream_key, 6)
    for position, shards_of in shards:
        steps = jnp.exp(jax.random.uniform(jax.random.fold_in(own, position), (shards_of,), jnp.float32, low / len(shards), top_value / len(shards)))
        level = level * jnp.repeat(steps, dims[position] // shards_of).reshape([-1 if axis == position else 1 for axis in range(len(dims))])
    return level


def bell_draw(stream_key, shape, width, bound, pieces=(), held_as=jnp.bfloat16):
    entries = jax.random.normal(stream_key, shape, jnp.float32) * width
    if len(pieces) > 0:
        entries = shard_levels(stream_key, shape, pieces, -0.22, 0.18) * entries
    return jnp.clip(entries, min=-bound, max=bound).astype(held_as)


def setup_inputs(seed: int = 0) -> dict:
    streams_of = jax.random.split(jax.random.key(seed), 18)
    return {
        "inputs": bell_draw(streams_of[0], (ROWS, SEQ, D), 1.0, 6.0, ((0, 8),)),
        "out_grad": bell_draw(streams_of[1], (ROWS, SEQ, D), 1.0, 6.0, ((0, 8),)),
        "norm_gain": jnp.clip(1.0 + 0.1 * jax.random.normal(streams_of[2], (D,), jnp.float32), 0.5, 1.5).astype(jnp.bfloat16),
        "query_weight": bell_draw(streams_of[3], (D, H * HD), D ** -0.5, 0.15625, ((1, 4),)),
        "query_bias": bell_draw(streams_of[4], (H * HD,), 0.5, 3.0, ((0, 4),)),
        "key_weight": bell_draw(streams_of[5], (D, KVH * HD), D ** -0.5, 0.15625, ((1, 4),)),
        "key_bias": bell_draw(streams_of[6], (KVH * HD,), 0.5, 3.0, ((0, 4),)),
        "value_weight": bell_draw(streams_of[7], (D, KVH * HD), D ** -0.5, 0.15625, ((1, 4),)),
        "value_bias": bell_draw(streams_of[8], (KVH * HD,), 0.5, 3.0, ((0, 4),)),
        "output_weight": bell_draw(streams_of[9], (H * HD, D), (H * HD // 32) ** -0.5, 0.875, ((0, 4),)),
        "ffn_gain": jnp.clip(1.0 + 0.1 * jax.random.normal(streams_of[10], (D,), jnp.float32), 0.5, 1.5).astype(jnp.bfloat16),
        "gate_weight": bell_draw(streams_of[11], (D, FF), D ** -0.5, 0.15625, ((1, 4),)),
        "up_weight": bell_draw(streams_of[12], (D, FF), D ** -0.5, 0.15625, ((1, 4),)),
        "down_weight": bell_draw(streams_of[13], (FF, D), (FF // 4) ** -0.5, 0.125, ((0, 4),)),
        "lengths": draw_lengths(jax.random.fold_in(streams_of[17], 71), 0),
        "segments": draw_segments(jax.random.fold_in(streams_of[17], 71), 0),
        "positions": draw_positions(jax.random.fold_in(streams_of[17], 71), 0),
    }


@jax.custom_vjp
def low(v):
    return lax.optimization_barrier(v.astype(jnp.bfloat16)).astype(jnp.float32)

@jax.custom_vjp
def low_back(v):
    return v

def low_keep(v):
    return (low(v), None)

def low_pass(kept, grad):
    return (grad,)

def back_keep(v):
    return (v, None)

def back_low(kept, grad):
    return (low(grad),)
low.defvjp(low_keep, low_pass)
low_back.defvjp(back_keep, back_low)
NORM_EPS = 1e-06
ROPE_BASE = 10000.0
NEG_FILL = -1e+30

def matmul(left, right):
    return jnp.dot(left, right, precision=lax.Precision.HIGHEST, preferred_element_type=jnp.float32)

def rms_norm(values, gain):
    return values * lax.rsqrt(lax.optimization_barrier(jnp.mean(values * values, axis=-1, keepdims=True)) + NORM_EPS) * gain

def rope_tables(positions):
    half_dim = HD // 2
    inverse_freq = ROPE_BASE ** (-(jnp.arange(half_dim, dtype=jnp.float32) * (2.0 / HD)))
    angles = positions.astype(jnp.float32)[:, None] * inverse_freq[None, :]
    cosine = jnp.concatenate([jnp.cos(angles), jnp.cos(angles)], axis=-1)
    sine_table = jnp.concatenate([jnp.sin(angles), jnp.sin(angles)], axis=-1)
    return (cosine[:, None, :], sine_table[:, None, :])

def rotate(values, cosine, sine_table):
    half_dim = values.shape[-1] // 2
    turned = jnp.concatenate([-values[..., half_dim:], values[..., :half_dim]], axis=-1)
    return values * cosine + turned * sine_table

def attend_row(packed):
    queries, keys, values, seg_row, length = packed
    score_scale = HD ** (-0.5)
    scores = jnp.einsum('sgkd,tgd->gkst', queries, keys, precision=lax.Precision.HIGHEST) * score_scale
    scores = low_back(scores)
    row_ids = jnp.arange(SEQ, dtype=jnp.int32)
    allowed = (row_ids[None, :] <= row_ids[:, None]) & (seg_row[:, None] == seg_row[None, :])
    allowed = allowed & ((row_ids[None, :] < length) | (row_ids[None, :] == row_ids[:, None]))
    scores = jnp.where(allowed, scores, NEG_FILL)
    weights = low(jax.nn.softmax(scores, axis=-1))
    return jnp.einsum('gkst,tgd->sgkd', weights, values, precision=lax.Precision.HIGHEST)

def layer(inputs, norm_gain, query_weight, query_bias, key_weight, key_bias, value_weight, value_bias, output_weight, ffn_gain, gate_weight, up_weight, down_weight, lengths, segments, positions):
    tokens = ROWS * SEQ
    flat = inputs.reshape(tokens, D)
    normed_one = low(rms_norm(flat, norm_gain))
    cosine, sine_table = rope_tables(positions.reshape(tokens))
    query_lin = low_back(matmul(normed_one, query_weight) + query_bias)
    key_lin = low_back(matmul(normed_one, key_weight) + key_bias)
    value_all = low(low_back(matmul(normed_one, value_weight) + value_bias))
    query_rot = low(rotate(query_lin.reshape(tokens, H, HD), cosine, sine_table))
    key_rot = low(rotate(key_lin.reshape(tokens, KVH, HD), cosine, sine_table))
    attended = lax.map(jax.checkpoint(attend_row), (query_rot.reshape(ROWS, SEQ, KVH, H // KVH, HD), key_rot.reshape(ROWS, SEQ, KVH, HD), value_all.reshape(ROWS, SEQ, KVH, HD), segments, lengths))
    mixed = low(low_back(attended.reshape(tokens, H * HD)))
    branch = low_back(matmul(mixed, output_weight))
    hidden_state = flat + branch
    normed_two = low(rms_norm(hidden_state, ffn_gain))
    gate = low_back(matmul(normed_two, gate_weight))
    upper = low_back(matmul(normed_two, up_weight))
    activated = low(jax.nn.silu(gate) * upper)
    ffn_out = low_back(matmul(activated, down_weight))
    return (hidden_state + ffn_out).reshape(ROWS, SEQ, D)

def reference(inputs, out_grad, norm_gain, query_weight, query_bias, key_weight, key_bias, value_weight, value_bias, output_weight, ffn_gain, gate_weight, up_weight, down_weight, lengths, segments, positions):
    floats = tuple((array_in.astype(jnp.float32) for array_in in (inputs, norm_gain, query_weight, query_bias, key_weight, key_bias, value_weight, value_bias, output_weight, ffn_gain, gate_weight, up_weight, down_weight)))

    def run(*params):
        return layer(*params, lengths, segments, positions)
    output_value, pullback = jax.vjp(run, *floats)
    grads = pullback(out_grad.astype(jnp.float32))
    return (output_value.astype(jnp.bfloat16), grads[0].astype(jnp.bfloat16), grads[1], grads[2], grads[3], grads[4], grads[5], grads[6], grads[7], grads[8], grads[9], grads[10], grads[11], grads[12])
```

```python
import jax
import jax.numpy as jnp
from jax import lax
from jax.sharding import PartitionSpec as P

HD = 128


NORM_EPS = 1e-06
ROPE_BASE = 10000.0
NEG_FILL = -1e30


def swap(value, axis, mask):
    pairs = [(source, source ^ mask) for source in range(lax.axis_size(axis))]
    return lax.ppermute(value, axis, pairs)


def masks_of(axis):
    return [1 << bit for bit in range(lax.axis_size(axis).bit_length() - 1)]


def block_order(masks):
    order = [0]
    for mask in reversed(masks):
        order = [mask ^ block for block in order] + order
    return order


def level_blocks(matrix, position, masks):
    turned = matrix.T
    count = 1 << len(masks)
    rows = turned.shape[0] // count
    order = block_order(masks)
    levels = []
    start = 0
    sizes = [count >> (level + 1) for level in range(len(masks))] + [1]
    for size in sizes:
        pieces = [
            lax.dynamic_slice_in_dim(turned, (position ^ block) * rows, rows, 0)
            for block in order[start : start + size]
        ]
        levels.append(jnp.concatenate(pieces, axis=0))
        start += size
    return levels


def halving_sum(levels, right, axis, masks):
    received = []
    for left, mask in zip(levels, masks):
        rows = left.shape[0]
        part = jnp.dot(left, right, preferred_element_type=jnp.float32)
        for piece in received:
            part = part + piece[:rows].astype(jnp.float32)
        received = [piece[rows:] for piece in received]
        received.append(swap(part.astype(jnp.bfloat16), axis, mask))
    part = jnp.dot(levels[-1], right, preferred_element_type=jnp.float32)
    for piece in received:
        part = part + piece.astype(jnp.float32)
    return part


def doubling_sum(value, axis, masks):
    for mask in masks:
        value = value + swap(value, axis, mask)
    return value


def pair_sum(own, other):
    got = swap(other.astype(jnp.bfloat16), "narrow", 1)
    total = (own + got.astype(jnp.float32)).astype(jnp.bfloat16)
    for mask in masks_of("narrow")[1:]:
        total = total.astype(jnp.float32) + swap(total, "narrow", mask).astype(jnp.float32)
        if mask != masks_of("narrow")[-1]:
            total = total.astype(jnp.bfloat16)
    return total


def split_tokens(value, core, micro):
    halves = value.reshape((micro, 2, -1) + value.shape[1:])
    own = lax.dynamic_index_in_dim(halves, core, 1, keepdims=False)
    other = lax.dynamic_index_in_dim(halves, 1 - core, 1, keepdims=False)
    return (own.reshape((-1,) + value.shape[1:]), other.reshape((-1,) + value.shape[1:]))


def join_tokens(own, other, first, micro):
    own = own.reshape((micro, 1, -1) + own.shape[1:])
    other = other.reshape((micro, 1, -1) + other.shape[1:])
    left = jnp.where(first, own, other)
    right = jnp.where(first, other, own)
    joined = jnp.concatenate([left, right], axis=1)
    return joined.reshape((-1,) + own.shape[3:])


def inner(left, right):
    return lax.dot_general(
        left, right, (((0,), (0,)), ((), ())), preferred_element_type=jnp.float32
    )


def outer_back(left, right):
    return lax.dot_general(
        left, right, (((1,), (1,)), ((), ())), preferred_element_type=jnp.float32
    )


def rope_tables(positions, head_dim):
    half_dim = head_dim // 2
    inverse_freq = ROPE_BASE ** (-(jnp.arange(half_dim, dtype=jnp.float32) * (2.0 / head_dim)))
    angles = positions.astype(jnp.float32)[:, None] * inverse_freq[None, :]
    cosine = jnp.concatenate([jnp.cos(angles), jnp.cos(angles)], axis=-1)
    sine_table = jnp.concatenate([jnp.sin(angles), jnp.sin(angles)], axis=-1)
    return (cosine[:, None, :], sine_table[:, None, :])


def rotate(values, cosine, sine_table):
    half_dim = values.shape[-1] // 2
    turned = jnp.concatenate([-values[..., half_dim:], values[..., :half_dim]], axis=-1)
    return values * cosine + turned * sine_table


def unrotate(grads, cosine, sine_table):
    half_dim = grads.shape[-1] // 2
    sined = grads * sine_table
    return grads * cosine + jnp.concatenate(
        [sined[..., half_dim:], -sined[..., :half_dim]], axis=-1
    )


def norm_forward(values, gain):
    inverse = lax.rsqrt(jnp.mean(values * values, axis=-1, keepdims=True) + NORM_EPS)
    unit_values = values * inverse
    return (unit_values * gain.astype(jnp.float32), unit_values, inverse)


def norm_backward(grad_out, unit_values, inverse, gain):
    grad_unit = grad_out * gain.astype(jnp.float32)
    grad_in = inverse * (
        grad_unit - unit_values * jnp.mean(grad_unit * unit_values, axis=-1, keepdims=True)
    )
    return (grad_in, jnp.sum(grad_out * unit_values, axis=0))


def block_scores(query_block, keys, block_start, seg_row, length):
    score_scale = query_block.shape[-1] ** (-0.5)
    block_rows = query_block.shape[0]
    scores = (
        jnp.einsum("qhd,td->hqt", query_block, keys, preferred_element_type=jnp.float32)
        * score_scale
    )
    row_ids = block_start + jnp.arange(block_rows, dtype=jnp.int32)
    col_ids = jnp.arange(seg_row.shape[0], dtype=jnp.int32)
    allowed = (col_ids[None, :] <= row_ids[:, None]) & (seg_row[:, None] == seg_row[None, :])
    allowed = allowed & ((col_ids[None, :] < length) | (col_ids[None, :] == row_ids[:, None]))
    return (jnp.where(allowed[None], scores, NEG_FILL), score_scale)


def attend_forward(queries, keys, values, seg_row, length):
    seq_len, heads, head_dim = queries.shape
    block_count = seq_len // seq_len
    query_blocks = queries.reshape(block_count, seq_len, heads, head_dim)
    block_starts = jnp.arange(block_count, dtype=jnp.int32) * seq_len

    def one_block(packed):
        query_block, block_start = packed
        scores, score_scale = block_scores(query_block, keys, block_start, seg_row, length)
        row_max = jnp.max(scores, axis=-1, keepdims=True)
        exp_scores = jnp.exp(scores - row_max)
        row_total = jnp.sum(exp_scores, axis=-1, keepdims=True)
        weights = (exp_scores / row_total).astype(jnp.bfloat16)
        out_block = jnp.einsum("hqt,td->qhd", weights, values, preferred_element_type=jnp.float32)
        return (out_block, (row_max + jnp.log(row_total))[..., 0])

    out_blocks, log_totals = lax.map(one_block, (query_blocks, block_starts))
    return (out_blocks.reshape(seq_len, heads * head_dim), log_totals)


def attend_backward(queries, keys, values, seg_row, length, grad_out, log_totals):
    seq_len, heads, head_dim = queries.shape
    block_count = seq_len // seq_len
    query_blocks = queries.reshape(block_count, seq_len, heads, head_dim)
    grad_blocks = grad_out.reshape(block_count, seq_len, heads, head_dim)
    block_starts = jnp.arange(block_count, dtype=jnp.int32) * seq_len

    def one_block(carry, packed):
        key_acc, value_acc = carry
        query_block, grad_block, log_block, block_start = packed
        scores, score_scale = block_scores(query_block, keys, block_start, seg_row, length)
        weights = jnp.exp(scores - log_block[..., None])
        weight_grad = jnp.einsum(
            "qhd,td->hqt", grad_block, values, preferred_element_type=jnp.float32
        )
        delta = jnp.sum(weights * weight_grad, axis=-1, keepdims=True)
        score_grad = (weights * (weight_grad - delta)).astype(jnp.bfloat16)
        query_grad = (
            jnp.einsum("hqt,td->qhd", score_grad, keys, preferred_element_type=jnp.float32)
            * score_scale
        )
        key_acc = (
            key_acc
            + jnp.einsum("hqt,qhd->td", score_grad, query_block, preferred_element_type=jnp.float32)
            * score_scale
        )
        value_acc = value_acc + jnp.einsum(
            "hqt,qhd->td",
            weights.astype(jnp.bfloat16),
            grad_block,
            preferred_element_type=jnp.float32,
        )
        return ((key_acc, value_acc), query_grad)

    zero_rows = jnp.zeros((seq_len, head_dim), jnp.float32)
    (key_grad, value_grad), query_grads = lax.scan(
        one_block, (zero_rows, zero_rows), (query_blocks, grad_blocks, log_totals, block_starts)
    )
    return (query_grads.reshape(seq_len, heads, head_dim), key_grad, value_grad)


def body(
    inputs,
    out_grad,
    norm_gain,
    query_weight,
    query_bias,
    key_weight,
    key_bias,
    value_weight,
    value_bias,
    output_weight,
    ffn_gain,
    gate_weight,
    up_weight,
    down_weight,
    lengths,
    segments,
    positions,
):
    micro, seq_len, width = inputs.shape
    tokens = micro * seq_len
    head_dim = HD
    half_dim = head_dim // 2
    local_heads = query_weight.shape[1] // head_dim
    query_cols = local_heads * head_dim
    wide_pos = lax.axis_index("wide")
    core = lax.axis_index("narrow") % 2
    is_even = core == 0
    wide_masks = masks_of("wide")
    own_kv = jnp.concatenate([key_weight, value_weight], axis=1)
    own_kv_bias = jnp.concatenate([key_bias, value_bias])
    other_kv = swap(own_kv, "narrow", 1)
    other_kv_bias = swap(own_kv_bias, "narrow", 1)
    flat_in = inputs.reshape(tokens, width)
    flat = flat_in.astype(jnp.float32)
    scaled_one, _, _ = norm_forward(flat, norm_gain)
    normed_one = scaled_one.astype(jnp.bfloat16)
    cosine, sine_table = rope_tables(positions.reshape(tokens), head_dim)
    query_lin = jnp.dot(
        normed_one, query_weight, preferred_element_type=jnp.float32
    ) + query_bias.astype(jnp.float32)
    own_lin = jnp.dot(normed_one, own_kv, preferred_element_type=jnp.float32) + own_kv_bias.astype(
        jnp.float32
    )
    other_lin = jnp.dot(
        normed_one, other_kv, preferred_element_type=jnp.float32
    ) + other_kv_bias.astype(jnp.float32)
    left_lin = jnp.where(is_even, own_lin, other_lin)
    right_lin = jnp.where(is_even, other_lin, own_lin)
    key_lin = jnp.concatenate([left_lin[:, :half_dim], right_lin[:, :half_dim]], axis=1)
    value_rows = jnp.concatenate(
        [left_lin[:, half_dim:], right_lin[:, half_dim:]], axis=1
    ).astype(jnp.bfloat16)
    query_rot = rotate(query_lin.reshape(tokens, local_heads, head_dim), cosine, sine_table).astype(
        jnp.bfloat16
    )
    key_rot = rotate(key_lin.reshape(tokens, 1, head_dim), cosine, sine_table)[:, 0].astype(
        jnp.bfloat16
    )
    mixed_parts = []
    log_parts = []
    for row_index in range(micro):
        row_span = slice(row_index * seq_len, (row_index + 1) * seq_len)
        out_row, log_row = attend_forward(
            query_rot[row_span],
            key_rot[row_span],
            value_rows[row_span],
            segments[row_index],
            lengths[row_index],
        )
        mixed_parts.append(out_row)
        log_parts.append(log_row)
    mixed = jnp.concatenate(mixed_parts, axis=0).astype(jnp.bfloat16)
    mixed_own, mixed_other = split_tokens(mixed, core, micro)
    branch = pair_sum(
        jnp.dot(mixed_own, output_weight, preferred_element_type=jnp.float32),
        jnp.dot(mixed_other, output_weight, preferred_element_type=jnp.float32),
    )
    flat_own, _ = split_tokens(flat_in, core, micro)
    flat_own = flat_own.astype(jnp.float32)
    grad_own, grad_other = split_tokens(out_grad.reshape(tokens, width), core, micro)
    grad_pair = jnp.concatenate([grad_own, grad_other], axis=0)
    hidden_own = flat_own + branch
    scaled_two, unit_two, inverse_two = norm_forward(hidden_own, ffn_gain)
    normed_two_own = scaled_two.astype(jnp.bfloat16)
    normed_two = jnp.concatenate([normed_two_own, swap(normed_two_own, "narrow", 1)], axis=0)
    act_grad = outer_back(grad_pair, down_weight)
    gate = jnp.dot(normed_two, gate_weight, preferred_element_type=jnp.float32)
    upper = jnp.dot(normed_two, up_weight, preferred_element_type=jnp.float32)
    gate_sig = jax.nn.sigmoid(gate)
    silu_value = gate * gate_sig
    activated = (silu_value * upper).astype(jnp.bfloat16)
    gate_grad = (act_grad * upper * gate_sig * (1.0 + gate * (1.0 - gate_sig))).astype(jnp.bfloat16)
    up_grad = (act_grad * silu_value).astype(jnp.bfloat16)
    down_out = halving_sum(level_blocks(grad_pair, wide_pos, wide_masks), activated, "wide", wide_masks).T
    two_levels = level_blocks(normed_two, wide_pos, wide_masks)
    gate_out = halving_sum(two_levels, gate_grad, "wide", wide_masks)
    other_masks = [wide_masks[1], wide_masks[0]] + wide_masks[2:]
    up_out = halving_sum(level_blocks(normed_two, wide_pos, other_masks), up_grad, "wide", other_masks)
    half = tokens // 2
    two_grad = pair_sum(
        outer_back(gate_grad[:half], gate_weight) + outer_back(up_grad[:half], up_weight),
        outer_back(gate_grad[half:], gate_weight) + outer_back(up_grad[half:], up_weight),
    )
    ffn_own = pair_sum(
        jnp.dot(activated[:half], down_weight, preferred_element_type=jnp.float32),
        jnp.dot(activated[half:], down_weight, preferred_element_type=jnp.float32),
    )
    result_own = (hidden_own + ffn_own).astype(jnp.bfloat16)
    result = join_tokens(result_own, swap(result_own, "narrow", 1), is_even, micro)
    hidden_extra, ffn_gain_grad = norm_backward(two_grad, unit_two, inverse_two, ffn_gain)
    hidden_grad = grad_own.astype(jnp.float32) + hidden_extra
    branch_grad_own = hidden_grad.astype(jnp.bfloat16)
    branch_grad_other = swap(branch_grad_own, "narrow", 1)
    branch_grad = jnp.concatenate([branch_grad_own, branch_grad_other], axis=0)
    output_out = halving_sum(
        level_blocks(branch_grad, wide_pos, wide_masks),
        jnp.concatenate([mixed_own, mixed_other], axis=0),
        "wide",
        wide_masks,
    ).T
    mixed_grad = join_tokens(
        outer_back(branch_grad_own, output_weight).astype(jnp.bfloat16),
        outer_back(branch_grad_other, output_weight).astype(jnp.bfloat16),
        is_even,
        micro,
    )
    query_parts = []
    key_parts = []
    value_parts = []
    for row_index in range(micro):
        row_span = slice(row_index * seq_len, (row_index + 1) * seq_len)
        query_part, key_part, value_part = attend_backward(
            query_rot[row_span],
            key_rot[row_span],
            value_rows[row_span],
            segments[row_index],
            lengths[row_index],
            mixed_grad[row_span].reshape(seq_len, local_heads, head_dim),
            log_parts[row_index],
        )
        query_parts.append(query_part)
        key_parts.append(key_part)
        value_parts.append(value_part)
    query_rot_grad = jnp.concatenate(query_parts, axis=0)
    kv_local = jnp.stack([jnp.concatenate(key_parts, axis=0), jnp.concatenate(value_parts, axis=0)])
    kv_total = kv_local + swap(kv_local, "narrow", 1)
    key_lin_grad = unrotate(kv_total[0][:, None, :], cosine, sine_table)[:, 0].astype(jnp.bfloat16)
    value_lin_grad = kv_total[1].astype(jnp.bfloat16)
    query_lin_grad = (
        unrotate(query_rot_grad, cosine, sine_table).reshape(tokens, query_cols).astype(jnp.bfloat16)
    )
    key_own = jnp.where(is_even, key_lin_grad[:, :half_dim], key_lin_grad[:, half_dim:])
    value_own = jnp.where(is_even, value_lin_grad[:, :half_dim], value_lin_grad[:, half_dim:])
    lin_grad = jnp.concatenate([query_lin_grad, key_own, value_own], axis=1)
    lin_weight = jnp.concatenate([query_weight, own_kv], axis=1)
    lin_own, lin_other = split_tokens(lin_grad, core, micro)
    one_grad = pair_sum(outer_back(lin_own, lin_weight), outer_back(lin_other, lin_weight))
    _, unit_one, inverse_one = norm_forward(flat_own, norm_gain)
    input_extra, norm_gain_grad = norm_backward(one_grad, unit_one, inverse_one, norm_gain)
    input_own = (hidden_grad + input_extra).astype(jnp.bfloat16)
    input_grad = join_tokens(input_own, swap(input_own, "narrow", 1), is_even, micro)
    lin_out = halving_sum(
        level_blocks(normed_one, wide_pos, wide_masks), lin_grad, "wide", wide_masks
    )
    bias_grad = jnp.sum(lin_grad.astype(jnp.float32), axis=0)
    gain_grad = jnp.concatenate([norm_gain_grad, ffn_gain_grad])
    gain_grad = gain_grad + swap(gain_grad, "narrow", 1)
    small = doubling_sum(jnp.concatenate([bias_grad, gain_grad]), "wide", wide_masks)
    split_at = [query_cols, query_cols + half_dim, query_cols + 2 * half_dim]
    query_out, key_out, value_out = jnp.split(lin_out, split_at[:2], axis=1)
    query_bias_out, key_bias_out, value_bias_out, gain_out = jnp.split(small, split_at)
    return (
        result.reshape(micro, seq_len, width),
        input_grad.reshape(micro, seq_len, width),
        gain_out[:width],
        query_out,
        query_bias_out,
        key_out,
        key_bias_out,
        value_out,
        value_bias_out,
        output_out,
        gain_out[width:],
        gate_out,
        up_out,
        down_out,
    )


def solution(mesh):
    placed = (
        P("wide", None, None),
        P("wide", None, None),
        P(),
        P(None, "narrow"),
        P("narrow"),
        P(None, "narrow"),
        P("narrow"),
        P(None, "narrow"),
        P("narrow"),
        P("narrow", None),
        P(),
        P(None, "narrow"),
        P(None, "narrow"),
        P("narrow", None),
        P("wide"),
        P("wide", None),
        P("wide", None),
    )
    return jax.shard_map(
        body,
        mesh=mesh,
        in_specs=placed,
        out_specs=(
            P("wide", None, None),
            P("wide", None, None),
            P(),
            P("wide", "narrow"),
            P("narrow"),
            P("wide", "narrow"),
            P("narrow"),
            P("wide", "narrow"),
            P("narrow"),
            P("narrow", "wide"),
            P(),
            P("wide", "narrow"),
            P("wide", "narrow"),
            P("narrow", "wide"),
        ),
        check_vma=False,
    )
```

```python
import functools

import jax
import jax.numpy as jnp
from jax import lax
from jax.experimental import pallas as pl
from jax.experimental.pallas import tpu as pltpu
from jax.sharding import PartitionSpec as P

HD = 128


NORM_EPS = 1e-06
ROPE_BASE = 10000.0
NEG_FILL = -1e30
F32 = jnp.float32
BF16 = jnp.bfloat16
TILE = 256
VMEM_LIMIT = 64 << 20


def swap(value, axis, mask):
    pairs = [(source, source ^ mask) for source in range(lax.axis_size(axis))]
    return lax.ppermute(value, axis, pairs)


def pair_exchange(value):
    size = lax.axis_size("narrow")
    pairs = [[first, first + 1] for first in range(0, size, 2)]
    return lax.all_to_all(value, "narrow", 0, 0, axis_index_groups=pairs, tiled=True)


def share_wide(value):
    count = lax.axis_size("wide")
    spread = jnp.broadcast_to(value, (count,) + value.shape[1:])
    return jnp.sum(lax.all_to_all(spread, "wide", 0, 0, tiled=True), axis=0, keepdims=True)


def swap_pieces(value, mask, count):
    return [swap(piece, "narrow", mask) for piece in jnp.split(value, count, axis=0)]


def swap_in_turn(value, axis, mask, sizes):
    if len(sizes) == 1:
        return swap(value, axis, mask)
    arrived = []
    last = 0
    for size in sizes:
        first, last = last, last + size
        piece = value[first:last]
        if arrived:
            arrived[-1], piece = lax.optimization_barrier((arrived[-1], piece))
        arrived.append(swap(piece, axis, mask))
    return jnp.concatenate(arrived, axis=0)


def masks_of(axis):
    return [1 << bit for bit in range(lax.axis_size(axis).bit_length() - 1)]


def block_order(masks):
    order = [0]
    for mask in reversed(masks):
        order = [mask ^ block for block in order] + order
    return order


def dot(left, right):
    return jnp.dot(left, right, preferred_element_type=F32)


def outer_back(left, right):
    return lax.dot_general(left, right, (((1,), (1,)), ((), ())), preferred_element_type=F32)


def inner(left, right):
    return lax.dot_general(left, right, (((0,), (0,)), ((), ())), preferred_element_type=F32)


def whole(*shape):
    return pl.BlockSpec(shape, lambda *_: (0,) * len(shape))


ANYWHERE = pl.BlockSpec(memory_space=pl.ANY)


class Chain:
    def __init__(self, scalars):
        self.scalars = scalars
        self.token = None

    def hold(self, *values):
        self.token, *held = lax.optimization_barrier((self.token, *values))
        return held

    def run(self, body, name, grid, ins, outs, scratch=(), into=(), after=(), flops=1):
        extra = list(into) + ([] if self.token is None else [self.token]) + list(after)
        count, given, made = len(self.scalars), len(ins), len(outs)

        def kernel(*refs):
            scalars = refs[:count]
            used = refs[count : count + given]
            results = refs[count + given + len(extra) :]
            results[made][...] = jnp.zeros_like(results[made])
            body(scalars, used, results[:made], results[made + 1 :])

        results = pl.pallas_call(
            kernel,
            out_shape=[jax.ShapeDtypeStruct(shape, dtype) for shape, dtype, _ in outs]
            + [jax.ShapeDtypeStruct((8, 128), F32)],
            grid_spec=pltpu.PrefetchScalarGridSpec(
                num_scalar_prefetch=count,
                grid=grid,
                in_specs=[spec for _, spec in ins] + [ANYWHERE] * len(extra),
                out_specs=[spec for _, _, spec in outs] + [whole(8, 128)],
                scratch_shapes=list(scratch),
            ),
            input_output_aliases={count + given + index: index for index in range(len(into))},
            compiler_params=pltpu.CompilerParams(
                dimension_semantics=("arbitrary",) * len(grid), vmem_limit_bytes=VMEM_LIMIT
            ),
            cost_estimate=pl.CostEstimate(
                flops=flops, bytes_accessed=1, transcendentals=0
            ),
            name=name,
        )(*self.scalars, *[array for array, _ in ins], *extra)
        self.token = results[-1]
        return results[:-1]


def copies(pairs, sems):
    started = []
    for index, (source, target) in enumerate(pairs):
        copy = pltpu.make_async_copy(source, target, sems.at[index])
        copy.start()
        started.append(copy)
    return started


class Tiles:
    def __init__(self, source, target, sems, total, tile):
        self.source, self.target, self.sems, self.tile = source, target, sems, tile
        self.full, self.rest = divmod(total, tile)

    def make(self, index, size):
        at = pl.multiple_of(index * self.tile, self.tile)
        return pltpu.make_async_copy(
            self.source.at[pl.ds(at, size)], self.target.at[index, pl.ds(0, size)], self.sems.at[index]
        )

    def start(self):
        for index in range(self.full):
            self.make(index, self.tile).start()
        if self.rest:
            self.make(self.full, self.rest).start()

    def wait(self, index):
        if not self.rest:
            self.make(index, self.tile).wait()
            return

        @pl.when(index < self.full)
        def _():
            self.make(index, self.tile).wait()

        @pl.when(index == self.full)
        def _():
            self.make(self.full, self.rest).wait()


def each(count, body):
    def run(index, carry):
        body(index)
        return carry

    lax.fori_loop(0, count, run, 0)


def unit_rows(values):
    inverse = lax.rsqrt(jnp.mean(values * values, axis=-1, keepdims=True) + NORM_EPS)
    return values * inverse, inverse


def norm_back(grad, unit, inverse, gain):
    grown = grad * gain
    return inverse * (grown - unit * jnp.mean(grown * unit, axis=-1, keepdims=True))


def rotate(values, cosine, sine):
    return values * cosine + pltpu.roll(values, HD // 2, 1) * sine


def unrotate(grads, cosine, sine):
    return grads * cosine + pltpu.roll(grads * sine, HD // 2, 1)


def down_rows(row, count):
    return jnp.broadcast_to(row, (128, count)).T


def allowed_pairs(seg_row, length, first, count, keys):
    turned = down_rows(seg_row[:, first : first + count], count)
    own = jnp.concatenate([turned] * (keys // 128), axis=1)
    rows = lax.broadcasted_iota(jnp.int32, (count, keys), 0) + first
    cols = lax.broadcasted_iota(jnp.int32, (count, keys), 1)
    same = own == jnp.broadcast_to(seg_row[:, :keys], (count, keys))
    return same & (cols <= rows) & ((cols < length) | (cols == rows))


def softmax_block(query, keys, allowed):
    scores = jnp.where(allowed, outer_back(query, keys) * (HD**-0.5), NEG_FILL)
    top = jnp.max(scores, axis=1, keepdims=True)
    grown = jnp.exp(scores - top)
    return grown * (1.0 / jnp.sum(grown, axis=1, keepdims=True))


class Layer:
    def __init__(self, inputs, cols, hidden):
        self.micro, self.seq_len, self.width = inputs.shape
        self.half = self.seq_len // 2
        self.tokens = self.micro * self.seq_len
        self.cols = cols
        self.hidden = hidden
        self.core = lax.axis_index("narrow") % 2
        self.even = self.core == 0
        self.narrow_masks = masks_of("narrow")
        self.chain = None

    def gain_of(self, small_ref, index):
        return small_ref[:, index * self.width : (index + 1) * self.width]

    def halves(self, value):
        return value.reshape(self.micro, 2, self.half, self.width)

    def across(self, parts, count=1, sizes=None):
        got = pair_exchange(parts)
        total = (got[0].astype(F32) + got[1].astype(F32)).astype(BF16)
        for mask in self.narrow_masks[1:-1]:
            total = (total.astype(F32) + swap(total, "narrow", mask).astype(F32)).astype(BF16)
        (total,) = self.chain.hold(total)
        if sizes is not None:
            return total, swap_in_turn(total, "narrow", self.narrow_masks[-1], sizes)
        return total, swap_pieces(total, self.narrow_masks[-1], count)

    def join(self, own, other):
        half, width, seq_len = self.half, self.width, self.seq_len
        block = pl.BlockSpec((half, width), lambda j, *_: (j, 0))

        def body(scalars, ins, outs, scratch):
            core = scalars[0][0]
            outs[0][pl.ds(pl.multiple_of(core * half, half), half), :] = ins[0][...]
            outs[0][pl.ds(pl.multiple_of((1 - core) * half, half), half), :] = ins[1][...]

        return self.chain.run(
            body,
            "join_tokens",
            (self.micro,),
            [(own, block), (other, block)],
            [
                (
                    (self.micro, seq_len, width),
                    BF16,
                    pl.BlockSpec((None, seq_len, width), lambda j, *_: (j, 0, 0)),
                )
            ],
        )[0]

    def front(self, inputs, small, small_oth, wq, kv, segments, positions, wo):
        seq_len, width, cols, half = self.seq_len, self.width, self.cols, self.half
        bias_at = 2 * width
        step = 128
        half_dim = HD // 2

        def body(scalars, ins, outs, scratch):
            x_ref, small_ref, oth_ref, wq_ref, wk_own, wv_own, wk_oth, wv_oth, seg_ref, pos_ref, wo_ref = ins
            mixed_out, q_out, k_out, v_out, cos_out, sin_out, parts = outs
            normed, mixed_all = scratch
            core = scalars[0][0]
            length = scalars[1][pl.program_id(0)]
            even = core == 0
            gain = self.gain_of(small_ref, 0)

            def norm_rows(index, carry):
                span = pl.ds(pl.multiple_of(index * step, step), step)
                unit, _ = unit_rows(x_ref[span, :].astype(F32))
                normed[span, :] = (unit * gain).astype(BF16)
                return carry

            lax.fori_loop(0, seq_len // step, norm_rows, 0)
            lane = lax.broadcasted_iota(jnp.int32, (1, HD), 1)
            exponent = jnp.where(lane < half_dim, lane, lane - half_dim).astype(F32) * (2.0 / HD)
            freq = jnp.exp(exponent * (-jnp.log(F32(ROPE_BASE))))
            place = down_rows(pos_ref[...].astype(F32), seq_len)
            angle = place * freq
            cosine = jnp.cos(angle)
            sine = jnp.where(lane < half_dim, -1.0, 1.0) * jnp.sin(angle)
            cos_out[...] = cosine
            sin_out[...] = sine
            rows = normed[...]
            first_k = jnp.where(even, wk_own[...], wk_oth[...])
            second_k = jnp.where(even, wk_oth[...], wk_own[...])
            first_v = jnp.where(even, wv_own[...], wv_oth[...])
            second_v = jnp.where(even, wv_oth[...], wv_own[...])
            kv = jnp.concatenate([first_k, second_k, first_v, second_v], axis=0)
            lin = outer_back(rows, kv)
            own_bias = small_ref[:, bias_at + cols : bias_at + cols + HD]
            oth_bias = oth_ref[:, bias_at + cols : bias_at + cols + HD]
            left = jnp.where(even, own_bias, oth_bias)
            right = jnp.where(even, oth_bias, own_bias)
            key_bias = jnp.where(lane < half_dim, left, pltpu.roll(right, half_dim, 1))
            value_bias = jnp.where(lane < half_dim, pltpu.roll(left, half_dim, 1), right)
            key = rotate(lin[:, :HD] + key_bias, cosine, sine).astype(BF16)
            value = (lin[:, HD:] + value_bias).astype(BF16)
            k_out[...] = key
            v_out[...] = value
            query_lin = dot(rows, wq_ref[...]) + small_ref[:, bias_at : bias_at + cols]
            seg_row = seg_ref[...].astype(F32)
            masks = [allowed_pairs(seg_row, length, at, half, at + half) for at in (0, half)]
            for head in range(cols // HD):
                span = slice(head * HD, (head + 1) * HD)
                query = rotate(query_lin[:, span], cosine, sine).astype(BF16)
                q_out[:, span] = query
                for part, allowed in enumerate(masks):
                    at = part * half
                    keys = at + half
                    weights = softmax_block(query[at:keys], key[:keys], allowed).astype(BF16)
                    mixed_all[at:keys, span] = dot(weights, value[:keys]).astype(BF16)
            for side in range(2):
                some = mixed_all[side * half : (side + 1) * half, :]
                mixed_out[side] = some
                parts[side] = dot(some, wo_ref[...]).astype(BF16)

        small_size = small.shape[1]
        kv_rows = kv[0].shape[0]
        return self.chain.run(
            body,
            "attention_front",
            (self.micro,),
            [
                (inputs, pl.BlockSpec((None, seq_len, width), lambda j, *_: (j, 0, 0))),
                (small, whole(1, small_size)),
                (small_oth, whole(1, small_size)),
                (wq, whole(width, cols)),
            ]
            + [(piece, whole(kv_rows, width)) for piece in kv]
            + [
                (segments[:, None, :], pl.BlockSpec((None, 1, seq_len), lambda j, *_: (j, 0, 0))),
                (positions[:, None, :], pl.BlockSpec((None, 1, seq_len), lambda j, *_: (j, 0, 0))),
                (wo, whole(cols, width)),
            ],
            [
                ((2, self.micro * half, cols), BF16, pl.BlockSpec((2, half, cols), lambda j, *_: (0, j, 0))),
                ((self.tokens, cols), BF16, pl.BlockSpec((seq_len, cols), lambda j, *_: (j, 0))),
                ((self.tokens, HD), BF16, pl.BlockSpec((seq_len, HD), lambda j, *_: (j, 0))),
                ((self.tokens, HD), BF16, pl.BlockSpec((seq_len, HD), lambda j, *_: (j, 0))),
                ((self.tokens, HD), F32, pl.BlockSpec((seq_len, HD), lambda j, *_: (j, 0))),
                ((self.tokens, HD), F32, pl.BlockSpec((seq_len, HD), lambda j, *_: (j, 0))),
                ((2, self.micro * half, width), BF16, pl.BlockSpec((2, half, width), lambda j, *_: (0, j, 0))),
            ],
            [pltpu.VMEM((seq_len, width), BF16), pltpu.VMEM((seq_len, cols), BF16)],
        )

    def act_grad(self, grad, wd):
        tokens, width, half, micro = self.tokens, self.width, self.half, self.micro
        hidden = self.hidden
        tiles = pl.cdiv(hidden, TILE)

        def body(scalars, ins, outs, scratch):
            grad_ref, wd_ref = ins
            rows, weights, made, row_sems, in_sems, out_sems = scratch
            lines = copies(
                [
                    (grad_ref.at[row, side], rows.at[pl.ds((side * micro + row) * half, half)])
                    for side in range(2)
                    for row in range(micro)
                ],
                row_sems,
            )
            loads = Tiles(wd_ref, weights, in_sems, hidden, TILE)
            loads.start()
            for copy in lines:
                copy.wait()

            def store(index):
                return pltpu.make_async_copy(made.at[index], outs[0].at[index], out_sems.at[index])

            def one(index):
                loads.wait(index)
                made[index] = outer_back(rows[...], weights[index]).astype(BF16)
                store(index).start()

            each(tiles, one)
            each(tiles, lambda index: store(index).wait())

        return self.chain.run(
            body,
            "activation_grad",
            (1,),
            [(self.halves(grad), ANYWHERE), (wd, ANYWHERE)],
            [((tiles, tokens, TILE), BF16, ANYWHERE)],
            [
                pltpu.VMEM((tokens, width), BF16),
                pltpu.VMEM((tiles, TILE, width), BF16),
                pltpu.VMEM((tiles, tokens, TILE), BF16),
                pltpu.SemaphoreType.DMA((2 * micro,)),
                pltpu.SemaphoreType.DMA((tiles,)),
                pltpu.SemaphoreType.DMA((tiles,)),
            ],
        )[0]

    def hidden_state(self, inputs, small, own, got):
        half, width = self.half, self.width
        step = 128
        count = half // step
        rows = self.micro * half

        def body(scalars, ins, outs, scratch):
            x_ref, small_ref, own_ref, got_ref = ins
            branch = own_ref[...].astype(F32) + got_ref[...].astype(F32)
            state = x_ref[...].astype(F32) + branch
            outs[0][...] = state
            unit, _ = unit_rows(state)
            scaled = (unit * self.gain_of(small_ref, 1)).astype(BF16)
            outs[1][0] = scaled
            outs[1][1] = scaled

        part = pl.BlockSpec((step, width), lambda j, *_: (j, 0))
        return self.chain.run(
            body,
            "hidden_norm",
            (rows // step,),
            [
                (
                    self.halves(inputs),
                    pl.BlockSpec(
                        (None, None, step, width), lambda j, place, *_: (j // count, place[0], j % count, 0)
                    ),
                ),
                (small, whole(1, small.shape[1])),
                (own, part),
                (got, part),
            ],
            [
                ((rows, width), F32, part),
                ((2, rows, width), BF16, pl.BlockSpec((2, step, width), lambda j, *_: (0, j, 0))),
            ],
        )

    def expand(self, rows_in, wg, wu, act_grad):
        width, hidden, tokens = self.width, self.hidden, self.tokens
        tiles = pl.cdiv(hidden, TILE)

        def body(scalars, ins, outs, scratch):
            *row_refs, wg_ref, wu_ref, grad_ref = ins
            rows, gates, ups, grads, made, row_sems, gate_sems, up_sems, grad_sems, out_sems = scratch
            spots = []
            at = 0
            for ref in row_refs:
                spots.append((ref, rows.at[pl.ds(at, ref.shape[0])]))
                at += ref.shape[0]
            sides = copies(spots, row_sems)
            first = Tiles(wg_ref, gates, gate_sems, hidden, TILE)
            second = Tiles(wu_ref, ups, up_sems, hidden, TILE)
            first.start()
            second.start()

            def grad_loads(index):
                return [pltpu.make_async_copy(grad_ref.at[index], grads.at[index], grad_sems.at[index])]

            def store(index, kind):
                return pltpu.make_async_copy(
                    made.at[index % 2, kind], outs[kind].at[index], out_sems.at[index % 2, kind]
                )

            def begin(index):
                for copy in grad_loads(index):
                    copy.start()

            each(tiles, begin)
            for copy in sides:
                copy.wait()
            lane = lax.broadcasted_iota(jnp.int32, (1, TILE), 1)

            def one(index):
                first.wait(index)
                second.wait(index)
                for copy in grad_loads(index):
                    copy.wait()

                @pl.when(index >= 2)
                def _():
                    for kind in range(3):
                        store(index - 2, kind).wait()

                def part(number):
                    span = slice(number, tokens)
                    gate = outer_back(rows[span, :], gates[index])
                    upper = outer_back(rows[span, :], ups[index])
                    grad = grads[index, span, :].astype(F32)
                    sig = 0.5 * jnp.tanh(0.5 * gate) + 0.5
                    silu = gate * sig
                    slot = index % 2
                    made[slot, 0, span, :] = (silu * upper).astype(BF16)
                    made[slot, 1, span, :] = (grad * upper * (sig + silu * (1.0 - sig))).astype(BF16)
                    made[slot, 2, span, :] = (grad * silu).astype(BF16)

                part(0)
                if hidden % TILE:

                    @pl.when(index == tiles - 1)
                    def _():
                        slot = (tiles - 1) % 2
                        blank = jnp.zeros((3, tokens, TILE // 2), BF16)
                        spare = lane[:, TILE // 2 :] < hidden % TILE
                        if hidden % TILE <= TILE // 2:
                            made[slot, :, :, TILE // 2 :] = blank
                            spare = lane[:, : TILE // 2] < hidden % TILE
                            made[slot, :, :, : TILE // 2] = jnp.where(
                                spare, made[slot, :, :, : TILE // 2], blank
                            )
                        else:
                            made[slot, :, :, TILE // 2 :] = jnp.where(
                                spare, made[slot, :, :, TILE // 2 :], blank
                            )

                for kind in range(3):
                    store(index, kind).start()

            each(tiles, one)
            for index in range(max(tiles - 2, 0), tiles):
                for kind in range(3):
                    store(index, kind).wait()

        return self.chain.run(
            body,
            "ffn_expand",
            (1,),
            [(piece, ANYWHERE) for piece in rows_in]
            + [(wg, ANYWHERE), (wu, ANYWHERE), (act_grad, ANYWHERE)],
            [((tiles, tokens, TILE), BF16, ANYWHERE)] * 3,
            [
                pltpu.VMEM((tokens, width), BF16),
                pltpu.VMEM((tiles, TILE, width), BF16),
                pltpu.VMEM((tiles, TILE, width), BF16),
                pltpu.VMEM((tiles, tokens, TILE), BF16),
                pltpu.VMEM((2, 3, tokens, TILE), BF16),
                pltpu.SemaphoreType.DMA((len(rows_in),)),
                pltpu.SemaphoreType.DMA((tiles,)),
                pltpu.SemaphoreType.DMA((tiles,)),
                pltpu.SemaphoreType.DMA((tiles,)),
                pltpu.SemaphoreType.DMA((2, 3)),
            ],
        )

    def turn(self, blocks, orders, small=None):
        width = self.width
        arrays = [entry[:2] for entry in blocks]
        steps = self.tokens // TILE
        count = len(orders[0])
        rows = width // count

        def body(scalars, ins, outs, scratch):
            turned = scratch[0]
            if small is not None:
                unit, _ = unit_rows(ins[0][...].astype(F32))
                turned[...] = (unit * self.gain_of(ins[1], 0)).astype(BF16).T
            elif len(ins) == 1:
                turned[...] = ins[0][...].T
            else:
                for index, ref in enumerate(ins):
                    @pl.when((pl.program_id(0) >= blocks[index][2]) & (pl.program_id(0) < blocks[index][3]))
                    def _():
                        turned[...] = ref[...].T
            place = scalars[0][1]
            for order, out in zip(orders, outs):
                for index, block in enumerate(order):
                    source = pl.multiple_of((place ^ block) * rows, rows)
                    out[0, index * rows : (index + 1) * rows, :] = turned[pl.ds(source, rows), :]

        ins = arrays + ([] if small is None else [(small, whole(1, small.shape[1]))])
        return self.chain.run(
            body,
            "turn_blocks",
            (steps,),
            ins,
            [((steps, width, TILE), BF16, pl.BlockSpec((1, width, TILE), lambda j, *_: (j, 0, 0)))] * len(orders),
            [pltpu.VMEM((width, TILE), BF16)],
        )

    def turn_pieces(self, pieces, orders):
        width, tokens = self.width, self.tokens
        steps = tokens // TILE
        count = len(orders[0])
        rows = width // count

        def body(scalars, ins, outs, scratch):
            stacked, turned, made, in_sems, out_sems = scratch
            at = 0
            pairs = []
            for ref in ins:
                pairs.append((ref, stacked.at[pl.ds(at, ref.shape[0])]))
                at += ref.shape[0]
            for copy in copies(pairs, in_sems):
                copy.wait()
            place = scalars[0][1]

            def store(step, number):
                return pltpu.make_async_copy(
                    made.at[number, step], outs[number].at[step], out_sems.at[number, step]
                )

            def one(step):
                turned[...] = stacked[pl.ds(pl.multiple_of(step * TILE, TILE), TILE), :].T
                for number, order in enumerate(orders):
                    for index, block in enumerate(order):
                        source = pl.multiple_of((place ^ block) * rows, rows)
                        made[number, step, index * rows : (index + 1) * rows, :] = turned[
                            pl.ds(source, rows), :
                        ]
                    store(step, number).start()

            each(steps, one)
            for number in range(len(orders)):
                each(steps, lambda step: store(step, number).wait())

        return self.chain.run(
            body,
            "turn_pieces",
            (1,),
            [(piece, ANYWHERE) for piece in pieces],
            [((steps, width, TILE), BF16, ANYWHERE)] * len(orders),
            [
                pltpu.VMEM((tokens, width), BF16),
                pltpu.VMEM((width, TILE), BF16),
                pltpu.VMEM((len(orders), steps, width, TILE), BF16),
                pltpu.SemaphoreType.DMA((len(pieces),)),
                pltpu.SemaphoreType.DMA((len(orders), steps)),
            ],
        )

    def shrink(self, pairs):
        tiles, rows, _ = pairs[0][0].shape
        width, hidden = self.width, self.hidden
        count = len(pairs)
        full = hidden // TILE
        lead = 2 * TILE

        def body(scalars, ins, outs, scratch):
            values, weights, acc, value_sems, weight_sems = scratch

            def loads(index, size):
                found = []
                for pair in range(count):
                    at = pl.multiple_of((pair * tiles + index) * TILE, TILE)
                    found.append(
                        pltpu.make_async_copy(
                            ins[2 * pair].at[index],
                            values.at[:, pl.ds(at, TILE)],
                            value_sems.at[index, pair],
                        )
                    )
                    found.append(
                        pltpu.make_async_copy(
                            ins[2 * pair + 1].at[pl.ds(pl.multiple_of(index * TILE, TILE), size)],
                            weights.at[pl.ds(at, size)],
                            weight_sems.at[index, pair],
                        )
                    )
                return found

            def begin(index):
                for copy in loads(index, TILE):
                    copy.start()

            each(full, begin)
            if full < tiles:
                rest = hidden - full * TILE
                for copy in loads(full, rest):
                    copy.start()
                for pair in range(count):
                    at = (pair * tiles + full) * TILE
                    weights[at + rest : at + TILE] = jnp.zeros((TILE - rest, width), BF16)
            acc[...] = jnp.zeros_like(acc)

            def add(index):
                for pair in range(count):
                    at = pl.ds(pl.multiple_of((pair * tiles + index) * TILE, TILE), TILE)
                    acc[...] += dot(values[:, at], weights[at, :lead])

            def one(index):
                for copy in loads(index, TILE):
                    copy.wait()
                add(index)

            each(full, one)
            if full < tiles:
                for copy in loads(full, hidden - full * TILE):
                    copy.wait()
                add(full)

            def put(value, at):
                for side in range(2):
                    outs[0][side, :, at] = value[side * (rows // 2) : (side + 1) * (rows // 2)].astype(BF16)

            put(acc, slice(0, lead))

            def wide(number):
                at = pl.ds(pl.multiple_of(lead + number * TILE, TILE), TILE)
                put(dot(values[...], weights[:, at]), at)

            each((width - lead) // TILE, wide)

        ins = []
        for value, weight in pairs:
            ins += [(value, ANYWHERE), (weight, ANYWHERE)]
        return self.chain.run(
            body,
            "ffn_shrink",
            (1,),
            ins,
            [((2, rows // 2, width), BF16, whole(2, rows // 2, width))],
            [
                pltpu.VMEM((rows, count * tiles * TILE), BF16),
                pltpu.VMEM((count * tiles * TILE, width), BF16),
                pltpu.VMEM((rows, lead), F32),
                pltpu.SemaphoreType.DMA((tiles, count)),
                pltpu.SemaphoreType.DMA((tiles, count)),
            ],
        )[0]

    def middle(self, hidden, own, gots, grad, small):
        half, width = self.half, self.width
        step = 128
        count = half // step
        rows = self.micro * half

        def body(scalars, ins, outs, scratch):
            state_ref, own_ref, *got_refs, grad_ref, small_ref = ins
            per = rows // step // len(gots)
            for index, ref in enumerate(got_refs):

                @pl.when(pl.program_id(0) // per == index)
                def _():
                    outs[0][...] = own_ref[...].astype(F32) + ref[...].astype(F32)

            incoming = outs[0][...]
            unit, inverse = unit_rows(state_ref[...])
            back = grad_ref[...].astype(F32) + norm_back(incoming, unit, inverse, self.gain_of(small_ref, 1))
            outs[0][...] = back
            outs[1][0] = back.astype(BF16)
            outs[1][1] = back.astype(BF16)
            part = jnp.sum(incoming * unit, axis=0, keepdims=True)

            @pl.when(pl.program_id(0) == 0)
            def _():
                outs[2][...] = part

            @pl.when(pl.program_id(0) > 0)
            def _():
                outs[2][...] += part

        block = pl.BlockSpec((step, width), lambda j, *_: (j, 0))
        return self.chain.run(
            body,
            "norm_two_back",
            (rows // step,),
            [
                (hidden, block),
                (own, block),
            ]
            + [
                (
                    got,
                    pl.BlockSpec(
                        (step, width),
                        lambda j, *_, index=index: (
                            jnp.clip(j - index * (rows // step // len(gots)), 0, rows // step // len(gots) - 1),
                            0,
                        ),
                    ),
                )
                for index, got in enumerate(gots)
            ]
            + [
                (
                    self.halves(grad),
                    pl.BlockSpec(
                        (None, None, step, width),
                        lambda j, place, *_: (j // count, place[0], j % count, 0),
                    ),
                ),
                (small, whole(1, small.shape[1])),
            ],
            [
                ((rows, width), F32, block),
                ((2, rows, width), BF16, pl.BlockSpec((2, step, width), lambda j, *_: (0, j, 0))),
                ((1, width), F32, whole(1, width)),
            ],
        )

    def back(self, front, segments, both, wo):
        seq_len, width, cols, half = self.seq_len, self.width, self.cols, self.half

        def body(scalars, ins, outs, scratch):
            q_ref, k_ref, v_ref, cos_ref, sin_ref, seg_ref, both_ref, wo_ref = ins
            dq_out, dkv_out = outs
            grad_all, dk_all, dv_all = scratch
            row = pl.program_id(0)
            length = scalars[1][row]
            for side in range(2):
                grad_all[side * half : (side + 1) * half, :] = outer_back(
                    both_ref[side], wo_ref[...]
                ).astype(BF16)
            seg_row = seg_ref[...].astype(F32)
            dk_all[...] = jnp.zeros_like(dk_all)
            dv_all[...] = jnp.zeros_like(dv_all)
            for part in (0, 1):
                at = part * half
                keys = at + half
                allowed = allowed_pairs(seg_row, length, at, half, keys)
                key, value = k_ref[:keys], v_ref[:keys]
                for head in range(cols // HD):
                    span = slice(head * HD, (head + 1) * HD)
                    query = q_ref[at:keys, span]
                    grad = grad_all[at:keys, span]
                    weights = softmax_block(query, key, allowed)
                    weight_grad = outer_back(grad, value)
                    delta = jnp.sum(weights * weight_grad, axis=1, keepdims=True)
                    score_grad = (weights * (weight_grad - delta)).astype(BF16)
                    dq = dot(score_grad, key) * (HD**-0.5)
                    dq_out[at:keys, span] = unrotate(dq, cos_ref[at:keys], sin_ref[at:keys]).astype(BF16)
                    dk_all[:keys] += inner(score_grad, query)
                    dv_all[:keys] += inner(weights.astype(BF16), grad)
            for side in range(2):
                dkv_out[side, :, :HD] = (dk_all[...] * (HD**-0.5)).astype(BF16)
                dkv_out[side, :, HD:] = dv_all[...].astype(BF16)

        _, query, key, value, cosine, sine = front[:6]
        head = pl.BlockSpec((seq_len, HD), lambda j, *_: (j, 0))
        heads = pl.BlockSpec((seq_len, cols), lambda j, *_: (j, 0))
        return self.chain.run(
            body,
            "attention_back",
            (self.micro,),
            [
                (query, heads),
                (key, head),
                (value, head),
                (cosine, head),
                (sine, head),
                (segments[:, None, :], pl.BlockSpec((None, 1, seq_len), lambda j, *_: (j, 0, 0))),
                (both, pl.BlockSpec((2, half, width), lambda j, *_: (0, j, 0))),
                (wo, whole(cols, width)),
            ],
            [
                ((self.tokens, cols), BF16, heads),
                ((2, self.tokens, 2 * HD), BF16, pl.BlockSpec((2, seq_len, 2 * HD), lambda j, *_: (0, j, 0))),
            ],
            [
                pltpu.VMEM((seq_len, cols), BF16),
                pltpu.VMEM((seq_len, HD), F32),
                pltpu.VMEM((seq_len, HD), F32),
            ],
        )

    def linear_back(self, front, dq, dkv, wq, wk, wv):
        seq_len, width, cols, half = self.seq_len, self.width, self.cols, self.half
        half_dim = HD // 2
        total = cols + HD

        def body(scalars, ins, outs, scratch):
            dq_ref, dkv_ref, cos_ref, sin_ref, wq_ref, wk_ref, wv_ref = ins
            lin_out, bias_out, parts = outs
            small_grad = scratch[0]
            core = scalars[0][0]
            both = dkv_ref[0].astype(F32) + dkv_ref[1].astype(F32)
            key = unrotate(both[:, :HD], cos_ref[...], sin_ref[...])
            value = both[:, HD:]
            low = lax.broadcasted_iota(jnp.int32, key.shape, 1) < half_dim
            first = jnp.where(low, key, pltpu.roll(value, half_dim, 1))
            second = jnp.where(low, pltpu.roll(key, half_dim, 1), value)
            own_kv = jnp.where(core == 0, first, second).astype(BF16)
            small_grad[...] = own_kv
            lin_out[:, :cols] = dq_ref[...]
            lin_out[:, cols:] = own_kv

            @pl.when(pl.program_id(0) == 0)
            def _():
                bias_out[...] = jnp.zeros_like(bias_out)

            bias_out[:, :cols] += jnp.sum(dq_ref[...].astype(F32), axis=0, keepdims=True)
            bias_out[:, cols:] += jnp.sum(own_kv.astype(F32), axis=0, keepdims=True)
            weight = jnp.concatenate([wk_ref[...], wv_ref[...]], axis=0)
            for side in range(2):
                span = slice(side * half, (side + 1) * half)
                piece = outer_back(dq_ref[span, :], wq_ref[...]) + dot(small_grad[span, :], weight)
                parts[side] = piece.astype(BF16)

        kv_rows = wk.shape[0]
        head = pl.BlockSpec((seq_len, HD), lambda j, *_: (j, 0))
        return self.chain.run(
            body,
            "linear_back",
            (self.micro,),
            [
                (dq, pl.BlockSpec((seq_len, cols), lambda j, *_: (j, 0))),
                (dkv, pl.BlockSpec((2, seq_len, 2 * HD), lambda j, *_: (0, j, 0))),
                (front[4], head),
                (front[5], head),
                (wq, whole(width, cols)),
                (wk, whole(kv_rows, width)),
                (wv, whole(kv_rows, width)),
            ],
            [
                ((self.tokens, total), BF16, pl.BlockSpec((seq_len, total), lambda j, *_: (j, 0))),
                ((1, total), F32, whole(1, total)),
                (
                    (2, self.micro * half, width),
                    BF16,
                    pl.BlockSpec((2, half, width), lambda j, *_: (0, j, 0)),
                ),
            ],
            [pltpu.VMEM((seq_len, HD), BF16)],
        )

    def last(self, inputs, own, got, hidden_grad, small):
        half, width = self.half, self.width
        step = 128
        count = half // step
        rows = self.micro * half

        def body(scalars, ins, outs, scratch):
            x_ref, own_ref, got_ref, grad_ref, small_ref = ins
            incoming = own_ref[...].astype(F32) + got_ref[...].astype(F32)
            unit, inverse = unit_rows(x_ref[...].astype(F32))
            back = grad_ref[...] + norm_back(incoming, unit, inverse, self.gain_of(small_ref, 0))
            outs[0][...] = back.astype(BF16)
            part = jnp.sum(incoming * unit, axis=0, keepdims=True)

            @pl.when(pl.program_id(0) == 0)
            def _():
                outs[1][...] = part

            @pl.when(pl.program_id(0) > 0)
            def _():
                outs[1][...] += part

        block = pl.BlockSpec((step, width), lambda j, *_: (j, 0))
        return self.chain.run(
            body,
            "norm_one_back",
            (rows // step,),
            [
                (
                    self.halves(inputs),
                    pl.BlockSpec(
                        (None, None, step, width),
                        lambda j, place, *_: (j // count, place[0], j % count, 0),
                    ),
                ),
                (own, block),
                (got, block),
                (hidden_grad, block),
                (small, whole(1, small.shape[1])),
            ],
            [((rows, width), BF16, block), ((1, width), F32, whole(1, width))],
        )

    def result(self, state, own, got):
        rows, width = state.shape
        step = 128
        block = pl.BlockSpec((step, width), lambda j, *_: (j, 0))

        def body(scalars, ins, outs, scratch):
            value = ins[0][...] + ins[1][...].astype(F32) + ins[2][...].astype(F32)
            outs[0][...] = value.astype(BF16)

        return self.chain.run(
            body,
            "result",
            (rows // step,),
            [(state, block), (own, block), (got, block)],
            [((rows, width), BF16, block)],
        )[0]


class Halving:
    def __init__(self, chain, left, right, masks, cols, columns=None, at=0):
        self.chain, self.left, self.right, self.masks, self.cols = chain, left, right, masks, cols
        total = left.shape[1]
        levels = len(masks)
        self.sizes = [total >> (level + 1) for level in range(levels)] + [total >> levels]
        self.starts = [total - (total >> level) for level in range(levels + 1)]
        self.parts = []
        self.columns = right.shape[2] if columns is None else columns
        self.at = at
        self.level = 0
        self.received = []
        self.result = None

    def product(self, first, last, into=()):
        parts, _, span = self.left.shape
        tiles, tokens, tile = self.right.shape
        sizes = self.sizes[first:last]
        offset = self.starts[first]
        rows = sum(sizes)
        column, columns = self.at, self.columns

        def body(scalars, refs, outs, scratch):
            left, right, made, left_sems, in_sems, out_sems = scratch
            lefts = copies(
                [
                    (refs[0].at[part, pl.ds(offset, rows)], left.at[:, pl.ds(part * span, span)])
                    for part in range(parts)
                ],
                left_sems,
            )

            def load(index):
                return pltpu.make_async_copy(refs[1].at[index], right.at[index], in_sems.at[index])

            def stores(index):
                at = 0
                found = []
                for number, size in enumerate(sizes):
                    found.append(
                        pltpu.make_async_copy(
                            made.at[index, pl.ds(at, size)],
                            outs[number].at[index, :, pl.ds(column, tile)],
                            out_sems.at[index, number],
                        )
                    )
                    at += size
                return found

            each(tiles, lambda index: load(index).start())
            for copy in lefts:
                copy.wait()

            def one(index):
                load(index).wait()

                made[index] = dot(left[...], right[index]).astype(BF16)
                for store in stores(index):
                    store.start()

            each(tiles, one)

            def end(index):
                for store in stores(index):
                    store.wait()

            each(tiles, end)

        self.parts += self.chain.run(
            body,
            "gradient_product",
            (1,),
            [(self.left, ANYWHERE), (self.right, ANYWHERE)],
            [((tiles, size, columns), BF16, ANYWHERE) for size in sizes],
            [
                pltpu.VMEM((rows, tokens), BF16),
                pltpu.VMEM((tiles, tokens, tile), BF16),
                pltpu.VMEM((tiles, rows, tile), BF16),
                pltpu.SemaphoreType.DMA((parts,)),
                pltpu.SemaphoreType.DMA((tiles,)),
                pltpu.SemaphoreType.DMA((tiles, len(sizes))),
            ],
            into=into,
        )
        return self

    def send(self):
        if self.level == len(self.masks):
            return self
        value = self.parts[self.level]
        if self.received:
            tiles, size, tile = value.shape
            start = self.starts[self.level]
            ins = [(value, whole(tiles, size, tile))]
            for piece, base in self.received:
                at = (start - base) // size
                ins.append((piece, pl.BlockSpec((tiles, size, tile), lambda *_, at=at: (0, at, 0))))

            def body(scalars, refs, outs, scratch):
                def one(index):
                    total = refs[0][index].astype(F32)
                    for ref in refs[1:]:
                        total = total + ref[index].astype(F32)
                    outs[0][index] = total.astype(BF16)

                each(tiles, one)

            (value,) = self.chain.run(
                body, "gradient_add", (1,), ins, [((tiles, size, tile), BF16, whole(tiles, size, tile))]
            )
        after = self.starts[self.level + 1]
        self.received.append((swap(value, "wide", self.masks[self.level]), after))
        self.level += 1
        return self

    def total(self):
        if self.result is not None:
            return self.result
        while self.level < len(self.masks):
            self.send()
        rows, start = self.sizes[-1], self.starts[-1]
        tiles, tile = self.right.shape[0], self.columns
        cols = self.cols
        ins = [(self.parts[-1], whole(tiles, rows, tile))]
        for piece, base in self.received:
            at = (start - base) // rows
            ins.append((piece, pl.BlockSpec((tiles, rows, tile), lambda *_, at=at: (0, at, 0))))

        def body(scalars, refs, outs, scratch):
            for index in range(tiles):
                value = refs[0][index].astype(F32)
                for ref in refs[1:]:
                    value = value + ref[index].astype(F32)
                size = min(tile, cols - index * tile)
                outs[0][:, index * tile : index * tile + size] = value[:, :size]

        (self.result,) = self.chain.run(
            body, "gradient_total", (1,), ins, [((rows, cols), F32, whole(rows, cols))]
        )
        return self.result


def doubling_sum(value, axis, masks):
    for mask in masks:
        value = value + swap(value, axis, mask)
    return value


def body(
    inputs,
    out_grad,
    norm_gain,
    query_weight,
    query_bias,
    key_weight,
    key_bias,
    value_weight,
    value_bias,
    output_weight,
    ffn_gain,
    gate_weight,
    up_weight,
    down_weight,
    lengths,
    segments,
    positions,
):
    micro, seq_len, width = inputs.shape
    cols = query_weight.shape[1]
    hidden_units = gate_weight.shape[1]
    layer = Layer(inputs, cols, hidden_units)
    half, tokens = layer.half, layer.tokens
    place = jnp.stack([layer.core, lax.axis_index("wide")]).astype(jnp.int32)
    chain = Chain([place, lengths])
    layer.chain = chain
    wide_masks = masks_of("wide")
    late_masks = [wide_masks[1], wide_masks[0]] + wide_masks[2:]
    early, late = block_order(wide_masks), block_order(late_masks)
    key_rows, value_rows = key_weight.T, value_weight.T
    gate_rows, up_rows = gate_weight.T, up_weight.T
    small = jnp.concatenate([norm_gain, ffn_gain, query_bias, key_bias, value_bias]).astype(F32)[None]
    small_oth = swap(small, "narrow", 1)
    kv = (key_rows, value_rows, swap(key_rows, "narrow", 1), swap(value_rows, "narrow", 1))
    grad_flat = out_grad.reshape(tokens, width)
    halves_grad = layer.halves(out_grad)
    front = layer.front(inputs, small, small_oth, query_weight, kv, segments, positions, output_weight)
    one_own, one_got = layer.across(front[6], sizes=(micro * half,))
    mixed = front[0]
    (grad_turned,) = layer.turn(
        [
            (
                halves_grad,
                pl.BlockSpec((None, None, TILE, width), lambda j, *_: (j % micro, j // micro, 0, 0)),
            )
        ],
        (early,),
    )
    act_grad = layer.act_grad(out_grad, down_weight)
    (one_turned,) = layer.turn(
        [(inputs.reshape(tokens, width), pl.BlockSpec((TILE, width), lambda j, *_: (j, 0)))], (early,), small
    )
    state, normed = layer.hidden_state(inputs, small, one_own, one_got)
    normed = pair_exchange(normed).reshape(tokens, width)
    act, dgate, dup = layer.expand([normed], gate_rows, up_rows, act_grad)
    levels = len(wide_masks)
    down = Halving(chain, grad_turned, act, wide_masks, hidden_units).product(0, 1).send()
    two_early, two_late = layer.turn_pieces([normed], (early, late))
    up = Halving(chain, two_late, dup, late_masks, hidden_units).product(0, levels + 1).send()
    two_sum = layer.across(layer.shrink([(dgate, gate_rows), (dup, up_rows)]))
    gate = Halving(chain, two_early, dgate, wide_masks, hidden_units).product(0, levels + 1).send()
    down.product(1, levels + 1)
    ffn_parts = layer.shrink([(act, down_weight)])
    down.send()
    ffn_sum = layer.across(ffn_parts)
    hidden_grad, branch_grad, ffn_gain_grad = layer.middle(state, *two_sum, out_grad, small)
    branch_both = pair_exchange(branch_grad)
    up.send()
    dq, dkv = layer.back(front, segments, branch_both, output_weight)
    down.send()
    lin_grad, bias, parts = layer.linear_back(
        front, dq, pair_exchange(dkv), query_weight, key_rows, value_rows
    )
    one_sum = layer.across(parts)
    gate.send()
    lin_cols = cols + HD
    lin = Halving(chain, one_turned, lin_grad[None], wide_masks, lin_cols + cols, lin_cols + cols)
    lin.product(0, levels + 1)
    (branch_turned,) = layer.turn_pieces([branch_both.reshape(tokens, width)], (early,))
    out = Halving(
        chain, branch_turned, mixed.reshape(1, tokens, cols), wide_masks, lin_cols + cols, lin_cols + cols, lin_cols
    )
    out.product(0, levels + 1, tuple(lin.parts)).send()
    up.send()
    result_own = layer.result(state, ffn_sum[0], ffn_sum[1][0])
    result_oth = swap(result_own, "narrow", 1)
    down_out = down.total()
    input_own, norm_gain_grad = layer.last(inputs, one_sum[0], one_sum[1][0], hidden_grad, small)
    input_oth = swap(input_own, "narrow", 1)
    result = layer.join(result_own, result_oth)
    gate.send()
    out.send()
    input_grad = layer.join(input_own, input_oth)
    out.send()
    up_out = up.total()
    gate_out = gate.total()
    joint = out.total()
    lin_out, output_out = joint[:, :lin_cols], joint[:, lin_cols:]
    packed = jnp.concatenate([bias, norm_gain_grad, ffn_gain_grad], axis=1) + chain.token[:1, :1]
    packed = share_wide(packed)
    gain_both = pair_exchange(jnp.broadcast_to(packed[:, cols + HD :], (2, 2 * width)))
    gain_out = gain_both[0] + gain_both[1]
    part = HD // 2
    query_out, key_out, value_out = jnp.split(lin_out, [cols, cols + part], axis=1)
    query_bias_out, key_bias_out, value_bias_out, _ = jnp.split(
        packed[0], [cols, cols + part, cols + 2 * part]
    )
    norm_gain_out, ffn_gain_out = gain_out[:width], gain_out[width:]
    return (
        result,
        input_grad,
        norm_gain_out,
        query_out,
        query_bias_out,
        key_out,
        key_bias_out,
        value_out,
        value_bias_out,
        output_out.T,
        ffn_gain_out,
        gate_out,
        up_out,
        down_out.T,
    )


def solution(mesh):
    placed = (
        P("wide", None, None),
        P("wide", None, None),
        P(),
        P(None, "narrow"),
        P("narrow"),
        P(None, "narrow"),
        P("narrow"),
        P(None, "narrow"),
        P("narrow"),
        P("narrow", None),
        P(),
        P(None, "narrow"),
        P(None, "narrow"),
        P("narrow", None),
        P("wide"),
        P("wide", None),
        P("wide", None),
    )
    return jax.shard_map(
        body,
        mesh=mesh,
        in_specs=placed,
        out_specs=(
            P("wide", None, None),
            P("wide", None, None),
            P(),
            P("wide", "narrow"),
            P("narrow"),
            P("wide", "narrow"),
            P("narrow"),
            P("wide", "narrow"),
            P("narrow"),
            P("narrow", "wide"),
            P(),
            P("wide", "narrow"),
            P("wide", "narrow"),
            P("narrow", "wide"),
        ),
        check_vma=False,
    )
```

```python
import functools

import jax
import jax.numpy as jnp
from jax import lax
from jax.experimental import pallas as pl
from jax.experimental.pallas import tpu as pltpu
from jax.sharding import PartitionSpec as P

HD = 128


NORM_EPS = 1e-06
ROPE_BASE = 10000.0
NEG_FILL = -1e30
F32 = jnp.float32
BF16 = jnp.bfloat16
TILE = 256
VMEM_LIMIT = 64 << 20
ORDER = (
    "pd1 tn pu s2",
    "pg pdr mid ad",
    "sF au bk ad",
    "ln plo c4 ag",
    "ta pout td au",
    "res last ag jr",
    "al ji tu al",
    "tg pk tl",
)
MASKS = "012 102 012 012"
DIRECT = ""


def swap(value, axis, mask):
    pairs = [(source, source ^ mask) for source in range(lax.axis_size(axis))]
    return lax.ppermute(value, axis, pairs)


def pair_exchange(value):
    size = lax.axis_size("narrow")
    pairs = [[first, first + 1] for first in range(0, size, 2)]
    return lax.all_to_all(value, "narrow", 0, 0, axis_index_groups=pairs, tiled=True)


def share_wide(value):
    count = lax.axis_size("wide")
    spread = jnp.broadcast_to(value, (count,) + value.shape[1:])
    return jnp.sum(lax.all_to_all(spread, "wide", 0, 0, tiled=True), axis=0, keepdims=True)


def swap_pieces(value, mask, count):
    return [swap(piece, "narrow", mask) for piece in jnp.split(value, count, axis=0)]


def swap_in_turn(value, axis, mask, sizes):
    if len(sizes) == 1:
        return swap(value, axis, mask)
    arrived = []
    last = 0
    for size in sizes:
        first, last = last, last + size
        piece = value[first:last]
        if arrived:
            arrived[-1], piece = lax.optimization_barrier((arrived[-1], piece))
        arrived.append(swap(piece, axis, mask))
    return jnp.concatenate(arrived, axis=0)


def masks_of(axis):
    return [1 << bit for bit in range(lax.axis_size(axis).bit_length() - 1)]


def block_order(masks):
    order = [0]
    for mask in reversed(masks):
        order = [mask ^ block for block in order] + order
    return order


def dot(left, right):
    return jnp.dot(left, right, preferred_element_type=F32)


def outer_back(left, right):
    return lax.dot_general(left, right, (((1,), (1,)), ((), ())), preferred_element_type=F32)


def inner(left, right):
    return lax.dot_general(left, right, (((0,), (0,)), ((), ())), preferred_element_type=F32)


def whole(*shape):
    return pl.BlockSpec(shape, lambda *_: (0,) * len(shape))


ANYWHERE = pl.BlockSpec(memory_space=pl.ANY)


TIMES = {
    "attention_back": 13,
    "linear_back": 7,
    "ffn_shrink": 13,
    "gradient_product": 8,
    "turn_pieces": 6,
    "norm_two_back": 8,
    "norm_one_back": 6,
    "gradient_add": 4,
    "gradient_total": 4,
    "result": 5,
    "join_tokens": 4,
}


class Chain:
    def __init__(self, scalars):
        self.scalars = scalars
        self.token = None
        self.scale = 0.0

    def hold(self, *values):
        self.token, *held = lax.optimization_barrier((self.token, *values))
        return held

    def run(self, body, name, grid, ins, outs, scratch=(), into=(), after=(), flops=1):
        extra = list(into) + ([] if self.token is None else [self.token]) + list(after)
        count, given, made = len(self.scalars), len(ins), len(outs)

        def kernel(*refs):
            scalars = refs[:count]
            used = refs[count : count + given]
            results = refs[count + given + len(extra) :]
            results[made][...] = jnp.zeros_like(results[made])
            body(scalars, used, results[:made], results[made + 1 :])

        results = pl.pallas_call(
            kernel,
            out_shape=[jax.ShapeDtypeStruct(shape, dtype) for shape, dtype, _ in outs]
            + [jax.ShapeDtypeStruct((8, 128), F32)],
            grid_spec=pltpu.PrefetchScalarGridSpec(
                num_scalar_prefetch=count,
                grid=grid,
                in_specs=[spec for _, spec in ins] + [ANYWHERE] * len(extra),
                out_specs=[spec for _, _, spec in outs] + [whole(8, 128)],
                scratch_shapes=list(scratch),
            ),
            input_output_aliases={count + given + index: index for index in range(len(into))},
            compiler_params=pltpu.CompilerParams(
                dimension_semantics=("arbitrary",) * len(grid), vmem_limit_bytes=VMEM_LIMIT
            ),
            cost_estimate=pl.CostEstimate(
                flops=int(self.scale * TIMES.get(name, 5)) + 1, bytes_accessed=1, transcendentals=0
            ),
            name=name,
        )(*self.scalars, *[array for array, _ in ins], *extra)
        self.token = results[-1]
        return results[:-1]


def copies(pairs, sems):
    started = []
    for index, (source, target) in enumerate(pairs):
        copy = pltpu.make_async_copy(source, target, sems.at[index])
        copy.start()
        started.append(copy)
    return started


class Tiles:
    def __init__(self, source, target, sems, total, tile):
        self.source, self.target, self.sems, self.tile = source, target, sems, tile
        self.full, self.rest = divmod(total, tile)

    def make(self, index, size):
        at = pl.multiple_of(index * self.tile, self.tile)
        return pltpu.make_async_copy(
            self.source.at[pl.ds(at, size)], self.target.at[index, pl.ds(0, size)], self.sems.at[index]
        )

    def start(self):
        for index in range(self.full):
            self.make(index, self.tile).start()
        if self.rest:
            self.make(self.full, self.rest).start()

    def wait(self, index):
        if not self.rest:
            self.make(index, self.tile).wait()
            return

        @pl.when(index < self.full)
        def _():
            self.make(index, self.tile).wait()

        @pl.when(index == self.full)
        def _():
            self.make(self.full, self.rest).wait()


def each(count, body):
    def run(index, carry):
        body(index)
        return carry

    lax.fori_loop(0, count, run, 0)


def unit_rows(values):
    inverse = lax.rsqrt(jnp.mean(values * values, axis=-1, keepdims=True) + NORM_EPS)
    return values * inverse, inverse


def norm_back(grad, unit, inverse, gain):
    grown = grad * gain
    return inverse * (grown - unit * jnp.mean(grown * unit, axis=-1, keepdims=True))


def rotate(values, cosine, sine):
    return values * cosine + pltpu.roll(values, HD // 2, 1) * sine


def unrotate(grads, cosine, sine):
    return grads * cosine + pltpu.roll(grads * sine, HD // 2, 1)


def down_rows(row, count):
    return jnp.broadcast_to(row, (128, count)).T


def allowed_pairs(seg_row, length, first, count, keys):
    turned = down_rows(seg_row[:, first : first + count], count)
    own = jnp.concatenate([turned] * (keys // 128), axis=1)
    rows = lax.broadcasted_iota(jnp.int32, (count, keys), 0) + first
    cols = lax.broadcasted_iota(jnp.int32, (count, keys), 1)
    same = own == jnp.broadcast_to(seg_row[:, :keys], (count, keys))
    return same & (cols <= rows) & ((cols < length) | (cols == rows))


def softmax_block(query, keys, allowed):
    scores = jnp.where(allowed, outer_back(query, keys) * (HD**-0.5), NEG_FILL)
    top = jnp.max(scores, axis=1, keepdims=True)
    grown = jnp.exp(scores - top)
    return grown * (1.0 / jnp.sum(grown, axis=1, keepdims=True))


class Layer:
    def __init__(self, inputs, cols, hidden):
        self.micro, self.seq_len, self.width = inputs.shape
        self.half = self.seq_len // 2
        self.tokens = self.micro * self.seq_len
        self.cols = cols
        self.hidden = hidden
        self.core = lax.axis_index("narrow") % 2
        self.even = self.core == 0
        self.narrow_masks = masks_of("narrow")
        self.chain = None

    def gain_of(self, small_ref, index):
        return small_ref[:, index * self.width : (index + 1) * self.width]

    def halves(self, value):
        return value.reshape(self.micro, 2, self.half, self.width)

    def across(self, parts, count=1, sizes=None):
        return self.to_other_chip(pair_exchange(parts), count, sizes)

    def to_other_chip(self, got, count=1, sizes=None):
        total = (got[0].astype(F32) + got[1].astype(F32)).astype(BF16)
        for mask in self.narrow_masks[1:-1]:
            total = (total.astype(F32) + swap(total, "narrow", mask).astype(F32)).astype(BF16)
        (total,) = self.chain.hold(total)
        if sizes is not None:
            return total, swap_in_turn(total, "narrow", self.narrow_masks[-1], sizes)
        return total, swap_pieces(total, self.narrow_masks[-1], count)

    def join(self, own, other):
        half, width, seq_len = self.half, self.width, self.seq_len
        block = pl.BlockSpec((half, width), lambda j, *_: (j, 0))

        def body(scalars, ins, outs, scratch):
            core = scalars[0][0]
            outs[0][pl.ds(pl.multiple_of(core * half, half), half), :] = ins[0][...]
            outs[0][pl.ds(pl.multiple_of((1 - core) * half, half), half), :] = ins[1][...]

        return self.chain.run(
            body,
            "join_tokens",
            (self.micro,),
            [(own, block), (other, block)],
            [
                (
                    (self.micro, seq_len, width),
                    BF16,
                    pl.BlockSpec((None, seq_len, width), lambda j, *_: (j, 0, 0)),
                )
            ],
        )[0]

    def front(self, inputs, small, small_oth, wq, kv, segments, positions, wo):
        seq_len, width, cols, half = self.seq_len, self.width, self.cols, self.half
        bias_at = 2 * width
        step = 128
        half_dim = HD // 2

        def body(scalars, ins, outs, scratch):
            x_ref, small_ref, oth_ref, wq_ref, wk_own, wv_own, wk_oth, wv_oth, seg_ref, pos_ref, wo_ref = ins
            mixed_out, q_out, k_out, v_out, cos_out, sin_out, part_own, part_oth = outs
            normed, mixed_all = scratch
            core = scalars[0][0]
            length = scalars[1][pl.program_id(0)]
            even = core == 0
            gain = self.gain_of(small_ref, 0)

            def norm_rows(index, carry):
                span = pl.ds(pl.multiple_of(index * step, step), step)
                unit, _ = unit_rows(x_ref[span, :].astype(F32))
                normed[span, :] = (unit * gain).astype(BF16)
                return carry

            lax.fori_loop(0, seq_len // step, norm_rows, 0)
            lane = lax.broadcasted_iota(jnp.int32, (1, HD), 1)
            exponent = jnp.where(lane < half_dim, lane, lane - half_dim).astype(F32) * (2.0 / HD)
            freq = jnp.exp(exponent * (-jnp.log(F32(ROPE_BASE))))
            place = down_rows(pos_ref[pl.ds(pl.program_id(0), 1), :].astype(F32), seq_len)
            angle = place * freq
            cosine = jnp.cos(angle)
            sine = jnp.where(lane < half_dim, -1.0, 1.0) * jnp.sin(angle)
            cos_out[...] = cosine
            sin_out[...] = sine
            rows = normed[...]
            first_k = jnp.where(even, wk_own[...], wk_oth[...])
            second_k = jnp.where(even, wk_oth[...], wk_own[...])
            first_v = jnp.where(even, wv_own[...], wv_oth[...])
            second_v = jnp.where(even, wv_oth[...], wv_own[...])
            kv = jnp.concatenate([first_k, second_k, first_v, second_v], axis=0)
            lin = outer_back(rows, kv)
            own_bias = small_ref[:, bias_at + cols : bias_at + cols + HD]
            oth_bias = oth_ref[:, bias_at + cols : bias_at + cols + HD]
            left = jnp.where(even, own_bias, oth_bias)
            right = jnp.where(even, oth_bias, own_bias)
            key_bias = jnp.where(lane < half_dim, left, pltpu.roll(right, half_dim, 1))
            value_bias = jnp.where(lane < half_dim, pltpu.roll(left, half_dim, 1), right)
            key = rotate(lin[:, :HD] + key_bias, cosine, sine).astype(BF16)
            value = (lin[:, HD:] + value_bias).astype(BF16)
            k_out[...] = key
            v_out[...] = value
            query_lin = dot(rows, wq_ref[...]) + small_ref[:, bias_at : bias_at + cols]
            seg_row = seg_ref[pl.ds(pl.program_id(0), 1), :].astype(F32)
            masks = [allowed_pairs(seg_row, length, at, half, at + half) for at in (0, half)]
            for head in range(cols // HD):
                span = slice(head * HD, (head + 1) * HD)
                query = rotate(query_lin[:, span], cosine, sine).astype(BF16)
                q_out[:, span] = query
                for part, allowed in enumerate(masks):
                    at = part * half
                    keys = at + half
                    weights = softmax_block(query[at:keys], key[:keys], allowed).astype(BF16)
                    mixed_all[at:keys, span] = dot(weights, value[:keys]).astype(BF16)
            for side in range(2):
                mixed_out[side] = mixed_all[side * half : (side + 1) * half, :]
            for side, part in ((core, part_own), (1 - core, part_oth)):
                some = mixed_all[pl.ds(pl.multiple_of(side * half, half), half), :]
                part[...] = dot(some, wo_ref[...]).astype(BF16)

        small_size = small.shape[1]
        kv_rows = kv[0].shape[0]
        return self.chain.run(
            body,
            "attention_front",
            (self.micro,),
            [
                (inputs, pl.BlockSpec((None, seq_len, width), lambda j, *_: (j, 0, 0))),
                (small, whole(1, small_size)),
                (small_oth, whole(1, small_size)),
                (wq, whole(width, cols)),
            ]
            + [(piece, whole(kv_rows, width)) for piece in kv]
            + [
                (segments, whole(*segments.shape)),
                (positions, whole(*positions.shape)),
                (wo, whole(cols, width)),
            ],
            [
                ((2, self.micro * half, cols), BF16, pl.BlockSpec((2, half, cols), lambda j, *_: (0, j, 0))),
                ((self.tokens, cols), BF16, pl.BlockSpec((seq_len, cols), lambda j, *_: (j, 0))),
                ((self.tokens, HD), BF16, pl.BlockSpec((seq_len, HD), lambda j, *_: (j, 0))),
                ((self.tokens, HD), BF16, pl.BlockSpec((seq_len, HD), lambda j, *_: (j, 0))),
                ((self.tokens, HD), F32, pl.BlockSpec((seq_len, HD), lambda j, *_: (j, 0))),
                ((self.tokens, HD), F32, pl.BlockSpec((seq_len, HD), lambda j, *_: (j, 0))),
                ((self.micro * half, width), BF16, pl.BlockSpec((half, width), lambda j, *_: (j, 0))),
                ((self.micro * half, width), BF16, pl.BlockSpec((half, width), lambda j, *_: (j, 0))),
            ],
            [pltpu.VMEM((seq_len, width), BF16), pltpu.VMEM((seq_len, cols), BF16)],
        )

    def act_grad(self, grad, wd):
        tokens, width, half, micro = self.tokens, self.width, self.half, self.micro
        hidden = self.hidden
        tiles = pl.cdiv(hidden, TILE)

        def body(scalars, ins, outs, scratch):
            grad_ref, wd_ref = ins
            rows, weights, made, row_sems, in_sems, out_sems = scratch
            lines = copies(
                [
                    (grad_ref.at[row, side], rows.at[pl.ds((side * micro + row) * half, half)])
                    for side in range(2)
                    for row in range(micro)
                ],
                row_sems,
            )
            loads = Tiles(wd_ref, weights, in_sems, hidden, TILE)
            loads.start()
            for copy in lines:
                copy.wait()

            def store(index):
                return pltpu.make_async_copy(made.at[index], outs[0].at[index], out_sems.at[index])

            def one(index):
                loads.wait(index)
                made[index] = outer_back(rows[...], weights[index]).astype(BF16)
                store(index).start()

            each(tiles, one)
            each(tiles, lambda index: store(index).wait())

        return self.chain.run(
            body,
            "activation_grad",
            (1,),
            [(self.halves(grad), ANYWHERE), (wd, ANYWHERE)],
            [((tiles, tokens, TILE), BF16, ANYWHERE)],
            [
                pltpu.VMEM((tokens, width), BF16),
                pltpu.VMEM((tiles, TILE, width), BF16),
                pltpu.VMEM((tiles, tokens, TILE), BF16),
                pltpu.SemaphoreType.DMA((2 * micro,)),
                pltpu.SemaphoreType.DMA((tiles,)),
                pltpu.SemaphoreType.DMA((tiles,)),
            ],
        )[0]

    def hidden_state(self, inputs, small, own, got):
        half, width = self.half, self.width
        step = 128
        count = half // step
        rows = self.micro * half

        def body(scalars, ins, outs, scratch):
            x_ref, small_ref, own_ref, got_ref = ins
            branch = own_ref[...].astype(F32) + got_ref[...].astype(F32)
            state = x_ref[...].astype(F32) + branch
            outs[0][...] = state
            unit, _ = unit_rows(state)
            outs[1][...] = (unit * self.gain_of(small_ref, 1)).astype(BF16)

        part = pl.BlockSpec((step, width), lambda j, *_: (j, 0))
        return self.chain.run(
            body,
            "hidden_norm",
            (rows // step,),
            [
                (
                    self.halves(inputs),
                    pl.BlockSpec(
                        (None, None, step, width), lambda j, place, *_: (j // count, place[0], j % count, 0)
                    ),
                ),
                (small, whole(1, small.shape[1])),
                (own, part),
                (got, part),
            ],
            [((rows, width), F32, part), ((rows, width), BF16, part)],
        )

    def placed(self, scalars, refs, target):
        core = scalars[0][0]
        rows = refs[0].shape[0]
        if len(refs) == 1:
            return [(refs[0], target)]
        spots = [pl.multiple_of(side * rows, rows) for side in (core, 1 - core)]
        return [(ref, target.at[pl.ds(spot, rows)]) for ref, spot in zip(refs, spots)]

    def expand(self, rows_in, wg, wu, act_grad):
        width, hidden, tokens = self.width, self.hidden, self.tokens
        tiles = pl.cdiv(hidden, TILE)

        def body(scalars, ins, outs, scratch):
            *row_refs, wg_ref, wu_ref, grad_ref = ins
            rows, gates, ups, grads, made, row_sems, gate_sems, up_sems, grad_sems, out_sems = scratch
            sides = copies(self.placed(scalars, row_refs, rows), row_sems)
            first = Tiles(wg_ref, gates, gate_sems, hidden, TILE)
            second = Tiles(wu_ref, ups, up_sems, hidden, TILE)
            first.start()
            second.start()

            def grad_loads(index):
                return [pltpu.make_async_copy(grad_ref.at[index], grads.at[index], grad_sems.at[index])]

            def store(index, kind):
                return pltpu.make_async_copy(
                    made.at[index % 2, kind], outs[kind].at[index], out_sems.at[index % 2, kind]
                )

            def begin(index):
                for copy in grad_loads(index):
                    copy.start()

            each(tiles, begin)
            for copy in sides:
                copy.wait()
            lane = lax.broadcasted_iota(jnp.int32, (1, TILE), 1)

            def one(index):
                first.wait(index)
                second.wait(index)
                for copy in grad_loads(index):
                    copy.wait()

                @pl.when(index >= 2)
                def _():
                    for kind in range(3):
                        store(index - 2, kind).wait()

                def part(number):
                    span = slice(number, tokens)
                    gate = outer_back(rows[span, :], gates[index])
                    upper = outer_back(rows[span, :], ups[index])
                    grad = grads[index, span, :].astype(F32)
                    sig = 0.5 * jnp.tanh(0.5 * gate) + 0.5
                    silu = gate * sig
                    slot = index % 2
                    made[slot, 0, span, :] = (silu * upper).astype(BF16)
                    made[slot, 1, span, :] = (grad * upper * (sig + silu * (1.0 - sig))).astype(BF16)
                    made[slot, 2, span, :] = (grad * silu).astype(BF16)

                part(0)
                if hidden % TILE:

                    @pl.when(index == tiles - 1)
                    def _():
                        slot = (tiles - 1) % 2
                        blank = jnp.zeros((3, tokens, TILE // 2), BF16)
                        spare = lane[:, TILE // 2 :] < hidden % TILE
                        if hidden % TILE <= TILE // 2:
                            made[slot, :, :, TILE // 2 :] = blank
                            spare = lane[:, : TILE // 2] < hidden % TILE
                            made[slot, :, :, : TILE // 2] = jnp.where(
                                spare, made[slot, :, :, : TILE // 2], blank
                            )
                        else:
                            made[slot, :, :, TILE // 2 :] = jnp.where(
                                spare, made[slot, :, :, TILE // 2 :], blank
                            )

                for kind in range(3):
                    store(index, kind).start()

            each(tiles, one)
            for index in range(max(tiles - 2, 0), tiles):
                for kind in range(3):
                    store(index, kind).wait()

        return self.chain.run(
            body,
            "ffn_expand",
            (1,),
            [(piece, ANYWHERE) for piece in rows_in]
            + [(wg, ANYWHERE), (wu, ANYWHERE), (act_grad, ANYWHERE)],
            [((tiles, tokens, TILE), BF16, ANYWHERE)] * 3,
            [
                pltpu.VMEM((tokens, width), BF16),
                pltpu.VMEM((tiles, TILE, width), BF16),
                pltpu.VMEM((tiles, TILE, width), BF16),
                pltpu.VMEM((tiles, tokens, TILE), BF16),
                pltpu.VMEM((2, 3, tokens, TILE), BF16),
                pltpu.SemaphoreType.DMA((len(rows_in),)),
                pltpu.SemaphoreType.DMA((tiles,)),
                pltpu.SemaphoreType.DMA((tiles,)),
                pltpu.SemaphoreType.DMA((tiles,)),
                pltpu.SemaphoreType.DMA((2, 3)),
            ],
        )

    def turn(self, blocks, orders, small=None):
        width = self.width
        arrays = [entry[:2] for entry in blocks]
        steps = self.tokens // TILE
        count = len(orders[0])
        rows = width // count

        def body(scalars, ins, outs, scratch):
            turned = scratch[0]
            if small is not None:
                unit, _ = unit_rows(ins[0][...].astype(F32))
                turned[...] = (unit * self.gain_of(ins[1], 0)).astype(BF16).T
            elif len(ins) == 1:
                turned[...] = ins[0][...].T
            else:
                for index, ref in enumerate(ins):
                    @pl.when((pl.program_id(0) >= blocks[index][2]) & (pl.program_id(0) < blocks[index][3]))
                    def _():
                        turned[...] = ref[...].T
            place = scalars[0][1]
            for order, out in zip(orders, outs):
                for index, block in enumerate(order):
                    source = pl.multiple_of((place ^ block) * rows, rows)
                    out[0, index * rows : (index + 1) * rows, :] = turned[pl.ds(source, rows), :]

        ins = arrays + ([] if small is None else [(small, whole(1, small.shape[1]))])
        return self.chain.run(
            body,
            "turn_blocks",
            (steps,),
            ins,
            [((steps, width, TILE), BF16, pl.BlockSpec((1, width, TILE), lambda j, *_: (j, 0, 0)))] * len(orders),
            [pltpu.VMEM((width, TILE), BF16)],
        )

    def turn_pieces(self, pieces, orders):
        width, tokens = self.width, self.tokens
        steps = tokens // TILE
        count = len(orders[0])
        rows = width // count

        def body(scalars, ins, outs, scratch):
            stacked, turned, made, in_sems, out_sems = scratch
            for copy in copies(self.placed(scalars, ins, stacked), in_sems):
                copy.wait()
            place = scalars[0][1]

            def store(step, number):
                return pltpu.make_async_copy(
                    made.at[number, step], outs[number].at[step], out_sems.at[number, step]
                )

            def one(step):
                turned[...] = stacked[pl.ds(pl.multiple_of(step * TILE, TILE), TILE), :].T
                for number, order in enumerate(orders):
                    for index, block in enumerate(order):
                        source = pl.multiple_of((place ^ block) * rows, rows)
                        made[number, step, index * rows : (index + 1) * rows, :] = turned[
                            pl.ds(source, rows), :
                        ]
                    store(step, number).start()

            each(steps, one)
            for number in range(len(orders)):
                each(steps, lambda step: store(step, number).wait())

        return self.chain.run(
            body,
            "turn_pieces",
            (1,),
            [(piece, ANYWHERE) for piece in pieces],
            [((steps, width, TILE), BF16, ANYWHERE)] * len(orders),
            [
                pltpu.VMEM((tokens, width), BF16),
                pltpu.VMEM((width, TILE), BF16),
                pltpu.VMEM((len(orders), steps, width, TILE), BF16),
                pltpu.SemaphoreType.DMA((len(pieces),)),
                pltpu.SemaphoreType.DMA((len(orders), steps)),
            ],
        )

    def shrink(self, pairs):
        tiles, rows, _ = pairs[0][0].shape
        width, hidden = self.width, self.hidden
        count = len(pairs)
        full = hidden // TILE
        lead = 2 * TILE

        def body(scalars, ins, outs, scratch):
            values, weights, acc, value_sems, weight_sems = scratch

            def loads(index, size):
                found = []
                for pair in range(count):
                    at = pl.multiple_of((pair * tiles + index) * TILE, TILE)
                    found.append(
                        pltpu.make_async_copy(
                            ins[2 * pair].at[index],
                            values.at[:, pl.ds(at, TILE)],
                            value_sems.at[index, pair],
                        )
                    )
                    found.append(
                        pltpu.make_async_copy(
                            ins[2 * pair + 1].at[pl.ds(pl.multiple_of(index * TILE, TILE), size)],
                            weights.at[pl.ds(at, size)],
                            weight_sems.at[index, pair],
                        )
                    )
                return found

            def begin(index):
                for copy in loads(index, TILE):
                    copy.start()

            each(full, begin)
            if full < tiles:
                rest = hidden - full * TILE
                for copy in loads(full, rest):
                    copy.start()
                for pair in range(count):
                    at = (pair * tiles + full) * TILE
                    weights[at + rest : at + TILE] = jnp.zeros((TILE - rest, width), BF16)
            acc[...] = jnp.zeros_like(acc)

            def add(index):
                for pair in range(count):
                    at = pl.ds(pl.multiple_of((pair * tiles + index) * TILE, TILE), TILE)
                    acc[...] += dot(values[:, at], weights[at, :lead])

            def one(index):
                for copy in loads(index, TILE):
                    copy.wait()
                add(index)

            each(full, one)
            if full < tiles:
                for copy in loads(full, hidden - full * TILE):
                    copy.wait()
                add(full)

            def put(value, at):
                for side in range(2):
                    outs[0][side, :, at] = value[side * (rows // 2) : (side + 1) * (rows // 2)].astype(BF16)

            put(acc, slice(0, lead))

            def wide(number):
                at = pl.ds(pl.multiple_of(lead + number * TILE, TILE), TILE)
                put(dot(values[...], weights[:, at]), at)

            each((width - lead) // TILE, wide)

        ins = []
        for value, weight in pairs:
            ins += [(value, ANYWHERE), (weight, ANYWHERE)]
        return self.chain.run(
            body,
            "ffn_shrink",
            (1,),
            ins,
            [((2, rows // 2, width), BF16, whole(2, rows // 2, width))],
            [
                pltpu.VMEM((rows, count * tiles * TILE), BF16),
                pltpu.VMEM((count * tiles * TILE, width), BF16),
                pltpu.VMEM((rows, lead), F32),
                pltpu.SemaphoreType.DMA((tiles, count)),
                pltpu.SemaphoreType.DMA((tiles, count)),
            ],
        )[0]

    def middle(self, hidden, own, gots, grad, small):
        half, width = self.half, self.width
        step = 128
        count = half // step
        rows = self.micro * half

        def body(scalars, ins, outs, scratch):
            state_ref, own_ref, *got_refs, grad_ref, small_ref = ins
            per = rows // step // len(gots)
            for index, ref in enumerate(got_refs):

                @pl.when(pl.program_id(0) // per == index)
                def _():
                    outs[0][...] = own_ref[...].astype(F32) + ref[...].astype(F32)

            incoming = outs[0][...]
            unit, inverse = unit_rows(state_ref[...])
            back = grad_ref[...].astype(F32) + norm_back(incoming, unit, inverse, self.gain_of(small_ref, 1))
            outs[0][...] = back
            outs[1][0] = back.astype(BF16)
            outs[1][1] = back.astype(BF16)
            part = jnp.sum(incoming * unit, axis=0, keepdims=True)

            @pl.when(pl.program_id(0) == 0)
            def _():
                outs[2][...] = part

            @pl.when(pl.program_id(0) > 0)
            def _():
                outs[2][...] += part

        block = pl.BlockSpec((step, width), lambda j, *_: (j, 0))
        return self.chain.run(
            body,
            "norm_two_back",
            (rows // step,),
            [
                (hidden, block),
                (own, block),
            ]
            + [
                (
                    got,
                    pl.BlockSpec(
                        (step, width),
                        lambda j, *_, index=index: (
                            jnp.clip(j - index * (rows // step // len(gots)), 0, rows // step // len(gots) - 1),
                            0,
                        ),
                    ),
                )
                for index, got in enumerate(gots)
            ]
            + [
                (
                    self.halves(grad),
                    pl.BlockSpec(
                        (None, None, step, width),
                        lambda j, place, *_: (j // count, place[0], j % count, 0),
                    ),
                ),
                (small, whole(1, small.shape[1])),
            ],
            [
                ((rows, width), F32, block),
                ((2, rows, width), BF16, pl.BlockSpec((2, step, width), lambda j, *_: (0, j, 0))),
                ((1, width), F32, whole(1, width)),
            ],
        )

    def back(self, front, segments, both, wo):
        seq_len, width, cols, half = self.seq_len, self.width, self.cols, self.half

        def body(scalars, ins, outs, scratch):
            q_ref, k_ref, v_ref, cos_ref, sin_ref, seg_ref, both_ref, wo_ref = ins
            dq_out, dkv_out = outs
            grad_all, dk_all, dv_all = scratch
            row = pl.program_id(0)
            length = scalars[1][row]
            for side in range(2):
                grad_all[side * half : (side + 1) * half, :] = outer_back(
                    both_ref[side], wo_ref[...]
                ).astype(BF16)
            seg_row = seg_ref[pl.ds(row, 1), :].astype(F32)
            dk_all[...] = jnp.zeros_like(dk_all)
            dv_all[...] = jnp.zeros_like(dv_all)
            for part in (0, 1):
                at = part * half
                keys = at + half
                allowed = allowed_pairs(seg_row, length, at, half, keys)
                key, value = k_ref[:keys], v_ref[:keys]
                for head in range(cols // HD):
                    span = slice(head * HD, (head + 1) * HD)
                    query = q_ref[at:keys, span]
                    grad = grad_all[at:keys, span]
                    weights = softmax_block(query, key, allowed)
                    weight_grad = outer_back(grad, value)
                    delta = jnp.sum(weights * weight_grad, axis=1, keepdims=True)
                    score_grad = (weights * (weight_grad - delta)).astype(BF16)
                    dq = dot(score_grad, key) * (HD**-0.5)
                    dq_out[at:keys, span] = unrotate(dq, cos_ref[at:keys], sin_ref[at:keys]).astype(BF16)
                    dk_all[:keys] += inner(score_grad, query)
                    dv_all[:keys] += inner(weights.astype(BF16), grad)
            for side in range(2):
                dkv_out[side, :, :HD] = (dk_all[...] * (HD**-0.5)).astype(BF16)
                dkv_out[side, :, HD:] = dv_all[...].astype(BF16)

        _, query, key, value, cosine, sine = front[:6]
        head = pl.BlockSpec((seq_len, HD), lambda j, *_: (j, 0))
        heads = pl.BlockSpec((seq_len, cols), lambda j, *_: (j, 0))
        return self.chain.run(
            body,
            "attention_back",
            (self.micro,),
            [
                (query, heads),
                (key, head),
                (value, head),
                (cosine, head),
                (sine, head),
                (segments, whole(*segments.shape)),
                (both, pl.BlockSpec((2, half, width), lambda j, *_: (0, j, 0))),
                (wo, whole(cols, width)),
            ],
            [
                ((self.tokens, cols), BF16, heads),
                ((2, self.tokens, 2 * HD), BF16, pl.BlockSpec((2, seq_len, 2 * HD), lambda j, *_: (0, j, 0))),
            ],
            [
                pltpu.VMEM((seq_len, cols), BF16),
                pltpu.VMEM((seq_len, HD), F32),
                pltpu.VMEM((seq_len, HD), F32),
            ],
        )

    def linear_back(self, front, dq, dkv, wq, wk, wv):
        seq_len, width, cols, half = self.seq_len, self.width, self.cols, self.half
        half_dim = HD // 2
        total = cols + HD

        def body(scalars, ins, outs, scratch):
            dq_ref, dkv_ref, cos_ref, sin_ref, wq_ref, wk_ref, wv_ref = ins
            lin_out, bias_out, parts = outs
            small_grad = scratch[0]
            core = scalars[0][0]
            both = dkv_ref[0].astype(F32) + dkv_ref[1].astype(F32)
            key = unrotate(both[:, :HD], cos_ref[...], sin_ref[...])
            value = both[:, HD:]
            low = lax.broadcasted_iota(jnp.int32, key.shape, 1) < half_dim
            first = jnp.where(low, key, pltpu.roll(value, half_dim, 1))
            second = jnp.where(low, pltpu.roll(key, half_dim, 1), value)
            own_kv = jnp.where(core == 0, first, second).astype(BF16)
            small_grad[...] = own_kv
            lin_out[:, :cols] = dq_ref[...]
            lin_out[:, cols:] = own_kv

            @pl.when(pl.program_id(0) == 0)
            def _():
                bias_out[...] = jnp.zeros_like(bias_out)

            bias_out[:, :cols] += jnp.sum(dq_ref[...].astype(F32), axis=0, keepdims=True)
            bias_out[:, cols:] += jnp.sum(own_kv.astype(F32), axis=0, keepdims=True)
            weight = jnp.concatenate([wk_ref[...], wv_ref[...]], axis=0)
            for side in range(2):
                span = slice(side * half, (side + 1) * half)
                piece = outer_back(dq_ref[span, :], wq_ref[...]) + dot(small_grad[span, :], weight)
                parts[side] = piece.astype(BF16)

        kv_rows = wk.shape[0]
        head = pl.BlockSpec((seq_len, HD), lambda j, *_: (j, 0))
        return self.chain.run(
            body,
            "linear_back",
            (self.micro,),
            [
                (dq, pl.BlockSpec((seq_len, cols), lambda j, *_: (j, 0))),
                (dkv, pl.BlockSpec((2, seq_len, 2 * HD), lambda j, *_: (0, j, 0))),
                (front[4], head),
                (front[5], head),
                (wq, whole(width, cols)),
                (wk, whole(kv_rows, width)),
                (wv, whole(kv_rows, width)),
            ],
            [
                ((self.tokens, total), BF16, pl.BlockSpec((seq_len, total), lambda j, *_: (j, 0))),
                ((1, total), F32, whole(1, total)),
                (
                    (2, self.micro * half, width),
                    BF16,
                    pl.BlockSpec((2, half, width), lambda j, *_: (0, j, 0)),
                ),
            ],
            [pltpu.VMEM((seq_len, HD), BF16)],
        )

    def last(self, inputs, own, got, hidden_grad, small):
        half, width = self.half, self.width
        step = 128
        count = half // step
        rows = self.micro * half

        def body(scalars, ins, outs, scratch):
            x_ref, own_ref, got_ref, grad_ref, small_ref = ins
            incoming = own_ref[...].astype(F32) + got_ref[...].astype(F32)
            unit, inverse = unit_rows(x_ref[...].astype(F32))
            back = grad_ref[...] + norm_back(incoming, unit, inverse, self.gain_of(small_ref, 0))
            outs[0][...] = back.astype(BF16)
            part = jnp.sum(incoming * unit, axis=0, keepdims=True)

            @pl.when(pl.program_id(0) == 0)
            def _():
                outs[1][...] = part

            @pl.when(pl.program_id(0) > 0)
            def _():
                outs[1][...] += part

        block = pl.BlockSpec((step, width), lambda j, *_: (j, 0))
        return self.chain.run(
            body,
            "norm_one_back",
            (rows // step,),
            [
                (
                    self.halves(inputs),
                    pl.BlockSpec(
                        (None, None, step, width),
                        lambda j, place, *_: (j // count, place[0], j % count, 0),
                    ),
                ),
                (own, block),
                (got, block),
                (hidden_grad, block),
                (small, whole(1, small.shape[1])),
            ],
            [((rows, width), BF16, block), ((1, width), F32, whole(1, width))],
        )

    def result(self, state, own, got):
        rows, width = state.shape
        step = 128
        block = pl.BlockSpec((step, width), lambda j, *_: (j, 0))

        def body(scalars, ins, outs, scratch):
            value = ins[0][...] + ins[1][...].astype(F32) + ins[2][...].astype(F32)
            outs[0][...] = value.astype(BF16)

        return self.chain.run(
            body,
            "result",
            (rows // step,),
            [(state, block), (own, block), (got, block)],
            [((rows, width), BF16, block)],
        )[0]


class Halving:
    def __init__(self, chain, left, right, masks, cols, columns=None, at=0, direct=False):
        self.chain, self.left, self.right, self.masks, self.cols = chain, left, right, masks, cols
        total = left.shape[1]
        levels = len(masks)
        self.sizes = [total >> (level + 1) for level in range(levels)] + [total >> levels]
        self.starts = [total - (total >> level) for level in range(levels + 1)]
        self.parts = []
        self.columns = right.shape[2] if columns is None else columns
        self.at = at
        self.direct = direct
        self.level = 0
        self.received = []
        self.result = None

    def product(self, first, last, into=()):
        parts, _, span = self.left.shape
        tiles, tokens, tile = self.right.shape
        sizes = self.sizes[first:last]
        offset = self.starts[first]
        rows = sum(sizes)
        column, columns = self.at, self.columns

        def body(scalars, refs, outs, scratch):
            left, right, made, left_sems, in_sems, out_sems = scratch
            lefts = copies(
                [
                    (refs[0].at[part, pl.ds(offset, rows)], left.at[:, pl.ds(part * span, span)])
                    for part in range(parts)
                ],
                left_sems,
            )

            def load(index):
                return pltpu.make_async_copy(refs[1].at[index], right.at[index], in_sems.at[index])

            def stores(index):
                at = 0
                found = []
                for number, size in enumerate(sizes):
                    found.append(
                        pltpu.make_async_copy(
                            made.at[index, pl.ds(at, size)],
                            outs[number].at[index, :, pl.ds(column, tile)],
                            out_sems.at[index, number],
                        )
                    )
                    at += size
                return found

            each(tiles, lambda index: load(index).start())
            for copy in lefts:
                copy.wait()

            def one(index):
                load(index).wait()

                made[index] = dot(left[...], right[index]).astype(BF16)
                for store in stores(index):
                    store.start()

            each(tiles, one)

            def end(index):
                for store in stores(index):
                    store.wait()

            each(tiles, end)

        self.parts += self.chain.run(
            body,
            "gradient_product",
            (1,),
            [(self.left, ANYWHERE), (self.right, ANYWHERE)],
            [((tiles, size, columns), BF16, ANYWHERE) for size in sizes],
            [
                pltpu.VMEM((rows, tokens), BF16),
                pltpu.VMEM((tiles, tokens, tile), BF16),
                pltpu.VMEM((tiles, rows, tile), BF16),
                pltpu.SemaphoreType.DMA((parts,)),
                pltpu.SemaphoreType.DMA((tiles,)),
                pltpu.SemaphoreType.DMA((tiles, len(sizes))),
            ],
            into=into,
        )
        return self

    def send(self):
        if self.level == len(self.masks):
            return self
        if self.direct and self.level == len(self.masks) - 2:
            return self.send_direct()
        value = self.parts[self.level]
        if self.received:
            tiles, size, tile = value.shape
            start = self.starts[self.level]
            ins = [(value, whole(tiles, size, tile))]
            for piece, base in self.received:
                at = (start - base) // size
                ins.append((piece, pl.BlockSpec((tiles, size, tile), lambda *_, at=at: (0, at, 0))))

            def body(scalars, refs, outs, scratch):
                def one(index):
                    total = refs[0][index].astype(F32)
                    for ref in refs[1:]:
                        total = total + ref[index].astype(F32)
                    outs[0][index] = total.astype(BF16)

                each(tiles, one)

            (value,) = self.chain.run(
                body, "gradient_add", (1,), ins, [((tiles, size, tile), BF16, whole(tiles, size, tile))]
            )
        after = self.starts[self.level + 1]
        self.received.append((swap(value, "wide", self.masks[self.level]), after))
        self.level += 1
        return self

    def send_direct(self):
        first, second = self.masks[-2:]
        pair, single = self.parts[self.level], self.parts[self.level + 1]
        tiles, rows, tile = single.shape
        start = self.starts[self.level]
        ins = [(pair, whole(tiles, 2 * rows, tile)), (single, whole(tiles, rows, tile))]
        for piece, base in self.received:
            for index in range(3):
                at = (start - base) // rows + index
                ins.append((piece, pl.BlockSpec((tiles, rows, tile), lambda *_, at=at: (0, at, 0))))

        def body(scalars, refs, outs, scratch):
            def one(index):
                for block in range(3):
                    if block < 2:
                        total = refs[0][index, block * rows : (block + 1) * rows].astype(F32)
                    else:
                        total = refs[1][index].astype(F32)
                    for ref in refs[2 + block :: 3]:
                        total = total + ref[index].astype(F32)
                    outs[block][index] = total.astype(BF16)

            each(tiles, one)

        shape = (tiles, rows, tile)
        values = self.chain.run(body, "gradient_add", (1,), ins, [(shape, BF16, whole(*shape))] * 3)
        for value, mask in zip(values, (first ^ second, first, second)):
            self.received.append((swap(value, "wide", mask), self.starts[-1]))
        self.level = len(self.masks)
        return self

    def total(self):
        if self.result is not None:
            return self.result
        while self.level < len(self.masks):
            self.send()
        rows, start = self.sizes[-1], self.starts[-1]
        tiles, tile = self.right.shape[0], self.columns
        cols = self.cols
        ins = [(self.parts[-1], whole(tiles, rows, tile))]
        for piece, base in self.received:
            at = (start - base) // rows
            ins.append((piece, pl.BlockSpec((tiles, rows, tile), lambda *_, at=at: (0, at, 0))))

        def body(scalars, refs, outs, scratch):
            for index in range(tiles):
                value = refs[0][index].astype(F32)
                for ref in refs[1:]:
                    value = value + ref[index].astype(F32)
                size = min(tile, cols - index * tile)
                outs[0][:, index * tile : index * tile + size] = value[:, :size]

        (self.result,) = self.chain.run(
            body, "gradient_total", (1,), ins, [((rows, cols), F32, whole(rows, cols))]
        )
        return self.result


def doubling_sum(value, axis, masks):
    for mask in masks:
        value = value + swap(value, axis, mask)
    return value


def body(
    inputs,
    out_grad,
    norm_gain,
    query_weight,
    query_bias,
    key_weight,
    key_bias,
    value_weight,
    value_bias,
    output_weight,
    ffn_gain,
    gate_weight,
    up_weight,
    down_weight,
    lengths,
    segments,
    positions,
):
    micro, seq_len, width = inputs.shape
    cols = query_weight.shape[1]
    hidden_units = gate_weight.shape[1]
    layer = Layer(inputs, cols, hidden_units)
    half, tokens = layer.half, layer.tokens
    place = jnp.stack([layer.core, lax.axis_index("wide")]).astype(jnp.int32)
    chain = Chain([place, lengths])
    layer.chain = chain
    wide_masks = masks_of("wide")
    down_masks, up_masks, gate_masks, joint_masks = [
        [wide_masks[int(place)] for place in places] + wide_masks[3:] for places in MASKS.split()
    ]
    key_rows, value_rows = key_weight.T, value_weight.T
    gate_rows, up_rows = gate_weight.T, up_weight.T
    small = jnp.concatenate([norm_gain, ffn_gain, query_bias, key_bias, value_bias]).astype(F32)[None]
    small_oth = swap(small, "narrow", 1)
    kv = (key_rows, value_rows, swap(key_rows, "narrow", 1), swap(value_rows, "narrow", 1))
    grad_flat = out_grad.reshape(tokens, width)
    halves_grad = layer.halves(out_grad)
    front = layer.front(inputs, small, small_oth, query_weight, kv, segments, positions, output_weight)
    pair = (front[6], swap(front[7], "narrow", 1))
    one_own, one_got = layer.to_other_chip(pair, sizes=(micro * half,))
    mixed = front[0]
    (grad_turned,) = layer.turn(
        [
            (
                halves_grad,
                pl.BlockSpec((None, None, TILE, width), lambda j, *_: (j % micro, j // micro, 0, 0)),
            )
        ],
        (block_order(down_masks),),
    )
    act_grad = layer.act_grad(out_grad, down_weight)
    (one_turned,) = layer.turn(
        [(inputs.reshape(tokens, width), pl.BlockSpec((TILE, width), lambda j, *_: (j, 0)))], (block_order(joint_masks),), small
    )
    state, normed = layer.hidden_state(inputs, small, one_own, one_got)
    normed = [normed, swap(normed, "narrow", 1)]
    act, dgate, dup = layer.expand(normed, gate_rows, up_rows, act_grad)
    levels = len(wide_masks)
    lin_cols = cols + HD
    made = {}
    down = Halving(chain, grad_turned, act, down_masks, hidden_units, direct="d" in DIRECT)

    def turn_two():
        made["two"] = layer.turn_pieces(normed, (block_order(gate_masks), block_order(up_masks)))

    def up_product():
        made["up"] = Halving(chain, made["two"][1], dup, up_masks, hidden_units, direct="u" in DIRECT).product(0, levels + 1)
        made["up"].send()

    def gate_product():
        made["gate"] = Halving(chain, made["two"][0], dgate, gate_masks, hidden_units, direct="g" in DIRECT).product(0, levels + 1)
        made["gate"].send()

    def shrink_two():
        made["two_sum"] = layer.across(layer.shrink([(dgate, gate_rows), (dup, up_rows)]))

    def shrink_ffn():
        made["ffn_sum"] = layer.across(layer.shrink([(act, down_weight)]))

    def middle():
        made["hidden_grad"], branch, made["ffn_gain"] = layer.middle(state, *made["two_sum"], out_grad, small)
        made["branch"] = pair_exchange(branch)

    def back():
        made["dq"], made["dkv"] = layer.back(front, segments, made["branch"], output_weight)

    def linear():
        made["lin_grad"], made["bias"], parts = layer.linear_back(
            front, made["dq"], pair_exchange(made["dkv"]), query_weight, key_rows, value_rows
        )
        made["one_sum"] = layer.across(parts)

    def linear_product():
        right = made["lin_grad"][None]
        made["lin"] = Halving(chain, one_turned, right, joint_masks, lin_cols + cols, lin_cols + cols)
        made["lin"].product(0, levels + 1)

    def turn_branch():
        (made["branch_turned"],) = layer.turn_pieces([made["branch"].reshape(tokens, width)], (block_order(joint_masks),))

    def output_product():
        right = mixed.reshape(1, tokens, cols)
        both = lin_cols + cols
        made["joint"] = Halving(chain, made["branch_turned"], right, joint_masks, both, both, lin_cols, "l" in DIRECT)
        made["joint"].product(0, levels + 1, tuple(made["lin"].parts)).send()

    def result():
        own = layer.result(state, made["ffn_sum"][0], made["ffn_sum"][1][0])
        made["result"] = (own, swap(own, "narrow", 1))

    def last():
        own, made["norm_gain"] = layer.last(
            inputs, made["one_sum"][0], made["one_sum"][1][0], made["hidden_grad"], small
        )
        made["input"] = (own, swap(own, "narrow", 1))

    def pack():
        packed = jnp.concatenate([made["bias"], made["norm_gain"], made["ffn_gain"]], axis=1)
        packed = share_wide(packed + chain.token[:1, :1])
        both = pair_exchange(jnp.broadcast_to(packed[:, cols + HD :], (2, 2 * width)))
        made["packed"] = chain.hold(packed, both[0] + both[1])

    def total(name):
        made[name + "_out"] = made[name].total()

    made["down"] = down
    steps = {
        "pk": pack,
        "pd1": lambda: down.product(0, 1).send(),
        "pdr": lambda: down.product(1, levels + 1),
        "tn": turn_two,
        "pu": up_product,
        "pg": gate_product,
        "s2": shrink_two,
        "sF": shrink_ffn,
        "mid": middle,
        "bk": back,
        "ln": linear,
        "plo": linear_product,
        "ta": turn_branch,
        "pout": output_product,
        "res": result,
        "last": last,
        "jr": lambda: made.update(result_out=layer.join(*made["result"])),
        "ji": lambda: made.update(input_out=layer.join(*made["input"])),
        "ad": lambda: down.send(),
        "au": lambda: made["up"].send(),
        "ag": lambda: made["gate"].send(),
        "al": lambda: made["joint"].send(),
        "td": lambda: total("down"),
        "tu": lambda: total("up"),
        "tg": lambda: total("gate"),
        "tl": lambda: total("joint"),
    }
    for name in " ".join(ORDER).split():
        if name.startswith("c"):
            chain.scale = 1e8 * int(name[1:])
        else:
            steps[name]()
    result, input_grad = made["result_out"], made["input_out"]
    down_out, up_out, gate_out = made["down_out"], made["up_out"], made["gate_out"]
    lin_out, output_out = made["joint_out"][:, :lin_cols], made["joint_out"][:, lin_cols:]
    packed, gain_out = made["packed"]
    part = HD // 2
    query_out, key_out, value_out = jnp.split(lin_out, [cols, cols + part], axis=1)
    query_bias_out, key_bias_out, value_bias_out, _ = jnp.split(
        packed[0], [cols, cols + part, cols + 2 * part]
    )
    norm_gain_out, ffn_gain_out = gain_out[:width], gain_out[width:]
    return (
        result,
        input_grad,
        norm_gain_out,
        query_out,
        query_bias_out,
        key_out,
        key_bias_out,
        value_out,
        value_bias_out,
        output_out.T,
        ffn_gain_out,
        gate_out,
        up_out,
        down_out.T,
    )


def solution(mesh):
    placed = (
        P("wide", None, None),
        P("wide", None, None),
        P(),
        P(None, "narrow"),
        P("narrow"),
        P(None, "narrow"),
        P("narrow"),
        P(None, "narrow"),
        P("narrow"),
        P("narrow", None),
        P(),
        P(None, "narrow"),
        P(None, "narrow"),
        P("narrow", None),
        P("wide"),
        P("wide", None),
        P("wide", None),
    )
    return jax.shard_map(
        body,
        mesh=mesh,
        in_specs=placed,
        out_specs=(
            P("wide", None, None),
            P("wide", None, None),
            P(),
            P("wide", "narrow"),
            P("narrow"),
            P("wide", "narrow"),
            P("narrow"),
            P("wide", "narrow"),
            P("narrow"),
            P("narrow", "wide"),
            P(),
            P("wide", "narrow"),
            P("wide", "narrow"),
            P("narrow", "wide"),
        ),
        check_vma=False,
    )
```

```python
import functools

import jax
import jax.numpy as jnp
from jax import lax
from jax.experimental import pallas as pl
from jax.experimental.pallas import tpu as pltpu
from jax.sharding import PartitionSpec as P

HD = 128


NORM_EPS = 1e-06
ROPE_BASE = 10000.0
NEG_FILL = -1e30
F32 = jnp.float32
BF16 = jnp.bfloat16
TILE = 256
VMEM_LIMIT = 64 << 20
ORDER = (
    "pd1 tn pu s2",
    "pg pdr sF mid",
    "ad au xF bk",
    "ad ln plo c4",
    "ag ta pout td",
    "au res last ag",
    "jr al ji al",
    "tu tg tl pk",
)
MASKS = "012 102 012 012"
DIRECT = ""


def swap(value, axis, mask):
    pairs = [(source, source ^ mask) for source in range(lax.axis_size(axis))]
    return lax.ppermute(value, axis, pairs)


def pair_exchange(value):
    size = lax.axis_size("narrow")
    pairs = [[first, first + 1] for first in range(0, size, 2)]
    return lax.all_to_all(value, "narrow", 0, 0, axis_index_groups=pairs, tiled=True)


def share_wide(value):
    count = lax.axis_size("wide")
    spread = jnp.broadcast_to(value, (count,) + value.shape[1:])
    return jnp.sum(lax.all_to_all(spread, "wide", 0, 0, tiled=True), axis=0, keepdims=True)


def swap_pieces(value, mask, count):
    return [swap(piece, "narrow", mask) for piece in jnp.split(value, count, axis=0)]


def swap_in_turn(value, axis, mask, sizes):
    if len(sizes) == 1:
        return swap(value, axis, mask)
    arrived = []
    last = 0
    for size in sizes:
        first, last = last, last + size
        piece = value[first:last]
        if arrived:
            arrived[-1], piece = lax.optimization_barrier((arrived[-1], piece))
        arrived.append(swap(piece, axis, mask))
    return jnp.concatenate(arrived, axis=0)


def masks_of(axis):
    return [1 << bit for bit in range(lax.axis_size(axis).bit_length() - 1)]


def block_order(masks):
    order = [0]
    for mask in reversed(masks):
        order = [mask ^ block for block in order] + order
    return order


def dot(left, right):
    return jnp.dot(left, right, preferred_element_type=F32)


def outer_back(left, right):
    return lax.dot_general(left, right, (((1,), (1,)), ((), ())), preferred_element_type=F32)


def inner(left, right):
    return lax.dot_general(left, right, (((0,), (0,)), ((), ())), preferred_element_type=F32)


def whole(*shape):
    return pl.BlockSpec(shape, lambda *_: (0,) * len(shape))


ANYWHERE = pl.BlockSpec(memory_space=pl.ANY)


TIMES = {
    "attention_back": 13,
    "linear_back": 7,
    "ffn_shrink": 13,
    "gradient_product": 8,
    "turn_pieces": 6,
    "norm_two_back": 8,
    "norm_one_back": 6,
    "gradient_add": 4,
    "gradient_total": 4,
    "result": 5,
    "join_tokens": 4,
}


class Chain:
    def __init__(self, scalars):
        self.scalars = scalars
        self.token = None
        self.scale = 0.0

    def hold(self, *values):
        self.token, *held = lax.optimization_barrier((self.token, *values))
        return held

    def run(self, body, name, grid, ins, outs, scratch=(), into=(), after=(), flops=1):
        extra = list(into) + ([] if self.token is None else [self.token]) + list(after)
        count, given, made = len(self.scalars), len(ins), len(outs)

        def kernel(*refs):
            scalars = refs[:count]
            used = refs[count : count + given]
            results = refs[count + given + len(extra) :]
            results[made][...] = jnp.zeros_like(results[made])
            body(scalars, used, results[:made], results[made + 1 :])

        results = pl.pallas_call(
            kernel,
            out_shape=[jax.ShapeDtypeStruct(shape, dtype) for shape, dtype, _ in outs]
            + [jax.ShapeDtypeStruct((8, 128), F32)],
            grid_spec=pltpu.PrefetchScalarGridSpec(
                num_scalar_prefetch=count,
                grid=grid,
                in_specs=[spec for _, spec in ins] + [ANYWHERE] * len(extra),
                out_specs=[spec for _, _, spec in outs] + [whole(8, 128)],
                scratch_shapes=list(scratch),
            ),
            input_output_aliases={count + given + index: index for index in range(len(into))},
            compiler_params=pltpu.CompilerParams(
                dimension_semantics=("arbitrary",) * len(grid), vmem_limit_bytes=VMEM_LIMIT
            ),
            cost_estimate=pl.CostEstimate(
                flops=int(self.scale * TIMES.get(name, 5)) + 1, bytes_accessed=1, transcendentals=0
            ),
            name=name,
        )(*self.scalars, *[array for array, _ in ins], *extra)
        self.token = results[-1]
        return results[:-1]


def copies(pairs, sems):
    started = []
    for index, (source, target) in enumerate(pairs):
        copy = pltpu.make_async_copy(source, target, sems.at[index])
        copy.start()
        started.append(copy)
    return started


class Tiles:
    def __init__(self, source, target, sems, total, tile):
        self.source, self.target, self.sems, self.tile = source, target, sems, tile
        self.full, self.rest = divmod(total, tile)

    def make(self, index, size):
        at = pl.multiple_of(index * self.tile, self.tile)
        return pltpu.make_async_copy(
            self.source.at[pl.ds(at, size)], self.target.at[index, pl.ds(0, size)], self.sems.at[index]
        )

    def start(self):
        for index in range(self.full):
            self.make(index, self.tile).start()
        if self.rest:
            self.make(self.full, self.rest).start()

    def wait(self, index):
        if not self.rest:
            self.make(index, self.tile).wait()
            return

        @pl.when(index < self.full)
        def _():
            self.make(index, self.tile).wait()

        @pl.when(index == self.full)
        def _():
            self.make(self.full, self.rest).wait()


def each(count, body):
    def run(index, carry):
        body(index)
        return carry

    lax.fori_loop(0, count, run, 0)


def unit_rows(values):
    inverse = lax.rsqrt(jnp.mean(values * values, axis=-1, keepdims=True) + NORM_EPS)
    return values * inverse, inverse


def norm_back(grad, unit, inverse, gain):
    grown = grad * gain
    return inverse * (grown - unit * jnp.mean(grown * unit, axis=-1, keepdims=True))


def rotate(values, cosine, sine):
    return values * cosine + pltpu.roll(values, HD // 2, 1) * sine


def unrotate(grads, cosine, sine):
    return grads * cosine + pltpu.roll(grads * sine, HD // 2, 1)


def down_rows(row, count):
    return jnp.broadcast_to(row, (128, count)).T


def allowed_pairs(seg_row, length, first, count, keys):
    turned = down_rows(seg_row[:, first : first + count], count)
    own = jnp.concatenate([turned] * (keys // 128), axis=1)
    rows = lax.broadcasted_iota(jnp.int32, (count, keys), 0) + first
    cols = lax.broadcasted_iota(jnp.int32, (count, keys), 1)
    same = own == jnp.broadcast_to(seg_row[:, :keys], (count, keys))
    return same & (cols <= rows) & ((cols < length) | (cols == rows))


def softmax_block(query, keys, allowed):
    scores = jnp.where(allowed, outer_back(query, keys) * (HD**-0.5), NEG_FILL)
    top = jnp.max(scores, axis=1, keepdims=True)
    grown = jnp.exp(scores - top)
    return grown * (1.0 / jnp.sum(grown, axis=1, keepdims=True))


class Layer:
    def __init__(self, inputs, cols, hidden):
        self.micro, self.seq_len, self.width = inputs.shape
        self.half = self.seq_len // 2
        self.tokens = self.micro * self.seq_len
        self.cols = cols
        self.hidden = hidden
        self.core = lax.axis_index("narrow") % 2
        self.even = self.core == 0
        self.narrow_masks = masks_of("narrow")
        self.chain = None

    def gain_of(self, small_ref, index):
        return small_ref[:, index * self.width : (index + 1) * self.width]

    def halves(self, value):
        return value.reshape(self.micro, 2, self.half, self.width)

    def across(self, parts, count=1, sizes=None):
        return self.to_other_chip(pair_exchange(parts), count, sizes)

    def to_other_chip(self, got, count=1, sizes=None):
        total = (got[0].astype(F32) + got[1].astype(F32)).astype(BF16)
        for mask in self.narrow_masks[1:-1]:
            total = (total.astype(F32) + swap(total, "narrow", mask).astype(F32)).astype(BF16)
        (total,) = self.chain.hold(total)
        if sizes is not None:
            return total, swap_in_turn(total, "narrow", self.narrow_masks[-1], sizes)
        return total, swap_pieces(total, self.narrow_masks[-1], count)

    def join(self, own, other):
        half, width, seq_len = self.half, self.width, self.seq_len
        block = pl.BlockSpec((half, width), lambda j, *_: (j, 0))

        def body(scalars, ins, outs, scratch):
            core = scalars[0][0]
            outs[0][pl.ds(pl.multiple_of(core * half, half), half), :] = ins[0][...]
            outs[0][pl.ds(pl.multiple_of((1 - core) * half, half), half), :] = ins[1][...]

        return self.chain.run(
            body,
            "join_tokens",
            (self.micro,),
            [(own, block), (other, block)],
            [
                (
                    (self.micro, seq_len, width),
                    BF16,
                    pl.BlockSpec((None, seq_len, width), lambda j, *_: (j, 0, 0)),
                )
            ],
        )[0]

    def front(self, inputs, small, small_oth, wq, kv, segments, positions, wo):
        seq_len, width, cols, half = self.seq_len, self.width, self.cols, self.half
        bias_at = 2 * width
        step = 128
        half_dim = HD // 2

        def body(scalars, ins, outs, scratch):
            x_ref, small_ref, oth_ref, wq_ref, wk_own, wv_own, wk_oth, wv_oth, seg_ref, pos_ref, wo_ref = ins
            mixed_out, q_out, k_out, v_out, cos_out, sin_out, part_own, part_oth = outs
            normed, mixed_all = scratch
            core = scalars[0][0]
            length = scalars[1][pl.program_id(0)]
            even = core == 0
            gain = self.gain_of(small_ref, 0)

            def norm_rows(index, carry):
                span = pl.ds(pl.multiple_of(index * step, step), step)
                unit, _ = unit_rows(x_ref[span, :].astype(F32))
                normed[span, :] = (unit * gain).astype(BF16)
                return carry

            lax.fori_loop(0, seq_len // step, norm_rows, 0)
            lane = lax.broadcasted_iota(jnp.int32, (1, HD), 1)
            exponent = jnp.where(lane < half_dim, lane, lane - half_dim).astype(F32) * (2.0 / HD)
            freq = jnp.exp(exponent * (-jnp.log(F32(ROPE_BASE))))
            place = down_rows(pos_ref[pl.ds(pl.program_id(0), 1), :].astype(F32), seq_len)
            angle = place * freq
            cosine = jnp.cos(angle)
            sine = jnp.where(lane < half_dim, -1.0, 1.0) * jnp.sin(angle)
            cos_out[...] = cosine
            sin_out[...] = sine
            rows = normed[...]
            first_k = jnp.where(even, wk_own[...], wk_oth[...])
            second_k = jnp.where(even, wk_oth[...], wk_own[...])
            first_v = jnp.where(even, wv_own[...], wv_oth[...])
            second_v = jnp.where(even, wv_oth[...], wv_own[...])
            kv = jnp.concatenate([first_k, second_k, first_v, second_v], axis=0)
            lin = outer_back(rows, kv)
            own_bias = small_ref[:, bias_at + cols : bias_at + cols + HD]
            oth_bias = oth_ref[:, bias_at + cols : bias_at + cols + HD]
            left = jnp.where(even, own_bias, oth_bias)
            right = jnp.where(even, oth_bias, own_bias)
            key_bias = jnp.where(lane < half_dim, left, pltpu.roll(right, half_dim, 1))
            value_bias = jnp.where(lane < half_dim, pltpu.roll(left, half_dim, 1), right)
            key = rotate(lin[:, :HD] + key_bias, cosine, sine).astype(BF16)
            value = (lin[:, HD:] + value_bias).astype(BF16)
            k_out[...] = key
            v_out[...] = value
            query_lin = dot(rows, wq_ref[...]) + small_ref[:, bias_at : bias_at + cols]
            seg_row = seg_ref[pl.ds(pl.program_id(0), 1), :].astype(F32)
            masks = [allowed_pairs(seg_row, length, at, half, at + half) for at in (0, half)]
            for head in range(cols // HD):
                span = slice(head * HD, (head + 1) * HD)
                query = rotate(query_lin[:, span], cosine, sine).astype(BF16)
                q_out[:, span] = query
                for part, allowed in enumerate(masks):
                    at = part * half
                    keys = at + half
                    weights = softmax_block(query[at:keys], key[:keys], allowed).astype(BF16)
                    mixed_all[at:keys, span] = dot(weights, value[:keys]).astype(BF16)
            for side in range(2):
                mixed_out[side] = mixed_all[side * half : (side + 1) * half, :]
            for side, part in ((core, part_own), (1 - core, part_oth)):
                some = mixed_all[pl.ds(pl.multiple_of(side * half, half), half), :]
                part[...] = dot(some, wo_ref[...]).astype(BF16)

        small_size = small.shape[1]
        kv_rows = kv[0].shape[0]
        return self.chain.run(
            body,
            "attention_front",
            (self.micro,),
            [
                (inputs, pl.BlockSpec((None, seq_len, width), lambda j, *_: (j, 0, 0))),
                (small, whole(1, small_size)),
                (small_oth, whole(1, small_size)),
                (wq, whole(width, cols)),
            ]
            + [(piece, whole(kv_rows, width)) for piece in kv]
            + [
                (segments, whole(*segments.shape)),
                (positions, whole(*positions.shape)),
                (wo, whole(cols, width)),
            ],
            [
                ((2, self.micro * half, cols), BF16, pl.BlockSpec((2, half, cols), lambda j, *_: (0, j, 0))),
                ((self.tokens, cols), BF16, pl.BlockSpec((seq_len, cols), lambda j, *_: (j, 0))),
                ((self.tokens, HD), BF16, pl.BlockSpec((seq_len, HD), lambda j, *_: (j, 0))),
                ((self.tokens, HD), BF16, pl.BlockSpec((seq_len, HD), lambda j, *_: (j, 0))),
                ((self.tokens, HD), F32, pl.BlockSpec((seq_len, HD), lambda j, *_: (j, 0))),
                ((self.tokens, HD), F32, pl.BlockSpec((seq_len, HD), lambda j, *_: (j, 0))),
                ((self.micro * half, width), BF16, pl.BlockSpec((half, width), lambda j, *_: (j, 0))),
                ((self.micro * half, width), BF16, pl.BlockSpec((half, width), lambda j, *_: (j, 0))),
            ],
            [pltpu.VMEM((seq_len, width), BF16), pltpu.VMEM((seq_len, cols), BF16)],
        )

    def act_grad(self, grad, wd):
        tokens, width, half, micro = self.tokens, self.width, self.half, self.micro
        hidden = self.hidden
        tiles = pl.cdiv(hidden, TILE)

        def body(scalars, ins, outs, scratch):
            grad_ref, wd_ref = ins
            rows, weights, made, row_sems, in_sems, out_sems = scratch
            lines = copies(
                [
                    (grad_ref.at[row, side], rows.at[pl.ds((side * micro + row) * half, half)])
                    for side in range(2)
                    for row in range(micro)
                ],
                row_sems,
            )
            loads = Tiles(wd_ref, weights, in_sems, hidden, TILE)
            loads.start()
            for copy in lines:
                copy.wait()

            def store(index):
                return pltpu.make_async_copy(made.at[index], outs[0].at[index], out_sems.at[index])

            def one(index):
                loads.wait(index)
                made[index] = outer_back(rows[...], weights[index]).astype(BF16)
                store(index).start()

            each(tiles, one)
            each(tiles, lambda index: store(index).wait())

        return self.chain.run(
            body,
            "activation_grad",
            (1,),
            [(self.halves(grad), ANYWHERE), (wd, ANYWHERE)],
            [((tiles, tokens, TILE), BF16, ANYWHERE)],
            [
                pltpu.VMEM((tokens, width), BF16),
                pltpu.VMEM((tiles, TILE, width), BF16),
                pltpu.VMEM((tiles, tokens, TILE), BF16),
                pltpu.SemaphoreType.DMA((2 * micro,)),
                pltpu.SemaphoreType.DMA((tiles,)),
                pltpu.SemaphoreType.DMA((tiles,)),
            ],
        )[0]

    def hidden_state(self, inputs, small, own, got):
        half, width = self.half, self.width
        step = 128
        count = half // step
        rows = self.micro * half

        def body(scalars, ins, outs, scratch):
            x_ref, small_ref, own_ref, got_ref = ins
            branch = own_ref[...].astype(F32) + got_ref[...].astype(F32)
            state = x_ref[...].astype(F32) + branch
            outs[0][...] = state
            unit, _ = unit_rows(state)
            outs[1][...] = (unit * self.gain_of(small_ref, 1)).astype(BF16)

        part = pl.BlockSpec((step, width), lambda j, *_: (j, 0))
        return self.chain.run(
            body,
            "hidden_norm",
            (rows // step,),
            [
                (
                    self.halves(inputs),
                    pl.BlockSpec(
                        (None, None, step, width), lambda j, place, *_: (j // count, place[0], j % count, 0)
                    ),
                ),
                (small, whole(1, small.shape[1])),
                (own, part),
                (got, part),
            ],
            [((rows, width), F32, part), ((rows, width), BF16, part)],
        )

    def placed(self, scalars, refs, target):
        core = scalars[0][0]
        rows = refs[0].shape[0]
        if len(refs) == 1:
            return [(refs[0], target)]
        spots = [pl.multiple_of(side * rows, rows) for side in (core, 1 - core)]
        return [(ref, target.at[pl.ds(spot, rows)]) for ref, spot in zip(refs, spots)]

    def expand(self, rows_in, wg, wu, act_grad):
        width, hidden, tokens = self.width, self.hidden, self.tokens
        tiles = pl.cdiv(hidden, TILE)

        def body(scalars, ins, outs, scratch):
            *row_refs, wg_ref, wu_ref, grad_ref = ins
            rows, gates, ups, grads, made, row_sems, gate_sems, up_sems, grad_sems, out_sems = scratch
            sides = copies(self.placed(scalars, row_refs, rows), row_sems)
            first = Tiles(wg_ref, gates, gate_sems, hidden, TILE)
            second = Tiles(wu_ref, ups, up_sems, hidden, TILE)
            first.start()
            second.start()

            def grad_loads(index):
                return [pltpu.make_async_copy(grad_ref.at[index], grads.at[index], grad_sems.at[index])]

            def store(index, kind):
                return pltpu.make_async_copy(
                    made.at[index % 2, kind], outs[kind].at[index], out_sems.at[index % 2, kind]
                )

            def begin(index):
                for copy in grad_loads(index):
                    copy.start()

            each(tiles, begin)
            for copy in sides:
                copy.wait()
            lane = lax.broadcasted_iota(jnp.int32, (1, TILE), 1)

            def one(index):
                first.wait(index)
                second.wait(index)
                for copy in grad_loads(index):
                    copy.wait()

                @pl.when(index >= 2)
                def _():
                    for kind in range(3):
                        store(index - 2, kind).wait()

                def part(number):
                    span = slice(number, tokens)
                    gate = outer_back(rows[span, :], gates[index])
                    upper = outer_back(rows[span, :], ups[index])
                    grad = grads[index, span, :].astype(F32)
                    sig = 0.5 * jnp.tanh(0.5 * gate) + 0.5
                    silu = gate * sig
                    slot = index % 2
                    made[slot, 0, span, :] = (silu * upper).astype(BF16)
                    made[slot, 1, span, :] = (grad * upper * (sig + silu * (1.0 - sig))).astype(BF16)
                    made[slot, 2, span, :] = (grad * silu).astype(BF16)

                part(0)
                if hidden % TILE:

                    @pl.when(index == tiles - 1)
                    def _():
                        slot = (tiles - 1) % 2
                        blank = jnp.zeros((3, tokens, TILE // 2), BF16)
                        spare = lane[:, TILE // 2 :] < hidden % TILE
                        if hidden % TILE <= TILE // 2:
                            made[slot, :, :, TILE // 2 :] = blank
                            spare = lane[:, : TILE // 2] < hidden % TILE
                            made[slot, :, :, : TILE // 2] = jnp.where(
                                spare, made[slot, :, :, : TILE // 2], blank
                            )
                        else:
                            made[slot, :, :, TILE // 2 :] = jnp.where(
                                spare, made[slot, :, :, TILE // 2 :], blank
                            )

                for kind in range(3):
                    store(index, kind).start()

            each(tiles, one)
            for index in range(max(tiles - 2, 0), tiles):
                for kind in range(3):
                    store(index, kind).wait()

        return self.chain.run(
            body,
            "ffn_expand",
            (1,),
            [(piece, ANYWHERE) for piece in rows_in]
            + [(wg, ANYWHERE), (wu, ANYWHERE), (act_grad, ANYWHERE)],
            [((tiles, tokens, TILE), BF16, ANYWHERE)] * 3,
            [
                pltpu.VMEM((tokens, width), BF16),
                pltpu.VMEM((tiles, TILE, width), BF16),
                pltpu.VMEM((tiles, TILE, width), BF16),
                pltpu.VMEM((tiles, tokens, TILE), BF16),
                pltpu.VMEM((2, 3, tokens, TILE), BF16),
                pltpu.SemaphoreType.DMA((len(rows_in),)),
                pltpu.SemaphoreType.DMA((tiles,)),
                pltpu.SemaphoreType.DMA((tiles,)),
                pltpu.SemaphoreType.DMA((tiles,)),
                pltpu.SemaphoreType.DMA((2, 3)),
            ],
        )

    def turn(self, blocks, orders, small=None):
        width = self.width
        arrays = [entry[:2] for entry in blocks]
        steps = self.tokens // TILE
        count = len(orders[0])
        rows = width // count

        def body(scalars, ins, outs, scratch):
            turned = scratch[0]
            if small is not None:
                unit, _ = unit_rows(ins[0][...].astype(F32))
                turned[...] = (unit * self.gain_of(ins[1], 0)).astype(BF16).T
            elif len(ins) == 1:
                turned[...] = ins[0][...].T
            else:
                for index, ref in enumerate(ins):
                    @pl.when((pl.program_id(0) >= blocks[index][2]) & (pl.program_id(0) < blocks[index][3]))
                    def _():
                        turned[...] = ref[...].T
            place = scalars[0][1]
            for order, out in zip(orders, outs):
                for index, block in enumerate(order):
                    source = pl.multiple_of((place ^ block) * rows, rows)
                    out[0, index * rows : (index + 1) * rows, :] = turned[pl.ds(source, rows), :]

        ins = arrays + ([] if small is None else [(small, whole(1, small.shape[1]))])
        return self.chain.run(
            body,
            "turn_blocks",
            (steps,),
            ins,
            [((steps, width, TILE), BF16, pl.BlockSpec((1, width, TILE), lambda j, *_: (j, 0, 0)))] * len(orders),
            [pltpu.VMEM((width, TILE), BF16)],
        )

    def turn_pieces(self, pieces, orders):
        width, tokens = self.width, self.tokens
        steps = tokens // TILE
        count = len(orders[0])
        rows = width // count

        def body(scalars, ins, outs, scratch):
            stacked, turned, made, in_sems, out_sems = scratch
            for copy in copies(self.placed(scalars, ins, stacked), in_sems):
                copy.wait()
            place = scalars[0][1]

            def store(step, number):
                return pltpu.make_async_copy(
                    made.at[number, step], outs[number].at[step], out_sems.at[number, step]
                )

            def one(step):
                turned[...] = stacked[pl.ds(pl.multiple_of(step * TILE, TILE), TILE), :].T
                for number, order in enumerate(orders):
                    for index, block in enumerate(order):
                        source = pl.multiple_of((place ^ block) * rows, rows)
                        made[number, step, index * rows : (index + 1) * rows, :] = turned[
                            pl.ds(source, rows), :
                        ]
                    store(step, number).start()

            each(steps, one)
            for number in range(len(orders)):
                each(steps, lambda step: store(step, number).wait())

        return self.chain.run(
            body,
            "turn_pieces",
            (1,),
            [(piece, ANYWHERE) for piece in pieces],
            [((steps, width, TILE), BF16, ANYWHERE)] * len(orders),
            [
                pltpu.VMEM((tokens, width), BF16),
                pltpu.VMEM((width, TILE), BF16),
                pltpu.VMEM((len(orders), steps, width, TILE), BF16),
                pltpu.SemaphoreType.DMA((len(pieces),)),
                pltpu.SemaphoreType.DMA((len(orders), steps)),
            ],
        )

    def shrink(self, pairs):
        tiles, rows, _ = pairs[0][0].shape
        width, hidden = self.width, self.hidden
        count = len(pairs)
        full = hidden // TILE
        lead = 2 * TILE

        def body(scalars, ins, outs, scratch):
            values, weights, acc, value_sems, weight_sems = scratch

            def loads(index, size):
                found = []
                for pair in range(count):
                    at = pl.multiple_of((pair * tiles + index) * TILE, TILE)
                    found.append(
                        pltpu.make_async_copy(
                            ins[2 * pair].at[index],
                            values.at[:, pl.ds(at, TILE)],
                            value_sems.at[index, pair],
                        )
                    )
                    found.append(
                        pltpu.make_async_copy(
                            ins[2 * pair + 1].at[pl.ds(pl.multiple_of(index * TILE, TILE), size)],
                            weights.at[pl.ds(at, size)],
                            weight_sems.at[index, pair],
                        )
                    )
                return found

            def begin(index):
                for copy in loads(index, TILE):
                    copy.start()

            each(full, begin)
            if full < tiles:
                rest = hidden - full * TILE
                for copy in loads(full, rest):
                    copy.start()
                for pair in range(count):
                    at = (pair * tiles + full) * TILE
                    weights[at + rest : at + TILE] = jnp.zeros((TILE - rest, width), BF16)
            acc[...] = jnp.zeros_like(acc)

            def add(index):
                for pair in range(count):
                    at = pl.ds(pl.multiple_of((pair * tiles + index) * TILE, TILE), TILE)
                    acc[...] += dot(values[:, at], weights[at, :lead])

            def one(index):
                for copy in loads(index, TILE):
                    copy.wait()
                add(index)

            each(full, one)
            if full < tiles:
                for copy in loads(full, hidden - full * TILE):
                    copy.wait()
                add(full)

            def put(value, at):
                for side in range(2):
                    outs[0][side, :, at] = value[side * (rows // 2) : (side + 1) * (rows // 2)].astype(BF16)

            put(acc, slice(0, lead))

            def wide(number):
                at = pl.ds(pl.multiple_of(lead + number * TILE, TILE), TILE)
                put(dot(values[...], weights[:, at]), at)

            each((width - lead) // TILE, wide)

        ins = []
        for value, weight in pairs:
            ins += [(value, ANYWHERE), (weight, ANYWHERE)]
        return self.chain.run(
            body,
            "ffn_shrink",
            (1,),
            ins,
            [((2, rows // 2, width), BF16, whole(2, rows // 2, width))],
            [
                pltpu.VMEM((rows, count * tiles * TILE), BF16),
                pltpu.VMEM((count * tiles * TILE, width), BF16),
                pltpu.VMEM((rows, lead), F32),
                pltpu.SemaphoreType.DMA((tiles, count)),
                pltpu.SemaphoreType.DMA((tiles, count)),
            ],
        )[0]

    def middle(self, hidden, own, gots, grad, small):
        half, width = self.half, self.width
        step = 128
        count = half // step
        rows = self.micro * half

        def body(scalars, ins, outs, scratch):
            state_ref, own_ref, *got_refs, grad_ref, small_ref = ins
            per = rows // step // len(gots)
            for index, ref in enumerate(got_refs):

                @pl.when(pl.program_id(0) // per == index)
                def _():
                    outs[0][...] = own_ref[...].astype(F32) + ref[...].astype(F32)

            incoming = outs[0][...]
            unit, inverse = unit_rows(state_ref[...])
            back = grad_ref[...].astype(F32) + norm_back(incoming, unit, inverse, self.gain_of(small_ref, 1))
            outs[0][...] = back
            outs[1][0] = back.astype(BF16)
            outs[1][1] = back.astype(BF16)
            part = jnp.sum(incoming * unit, axis=0, keepdims=True)

            @pl.when(pl.program_id(0) == 0)
            def _():
                outs[2][...] = part

            @pl.when(pl.program_id(0) > 0)
            def _():
                outs[2][...] += part

        block = pl.BlockSpec((step, width), lambda j, *_: (j, 0))
        return self.chain.run(
            body,
            "norm_two_back",
            (rows // step,),
            [
                (hidden, block),
                (own, block),
            ]
            + [
                (
                    got,
                    pl.BlockSpec(
                        (step, width),
                        lambda j, *_, index=index: (
                            jnp.clip(j - index * (rows // step // len(gots)), 0, rows // step // len(gots) - 1),
                            0,
                        ),
                    ),
                )
                for index, got in enumerate(gots)
            ]
            + [
                (
                    self.halves(grad),
                    pl.BlockSpec(
                        (None, None, step, width),
                        lambda j, place, *_: (j // count, place[0], j % count, 0),
                    ),
                ),
                (small, whole(1, small.shape[1])),
            ],
            [
                ((rows, width), F32, block),
                ((2, rows, width), BF16, pl.BlockSpec((2, step, width), lambda j, *_: (0, j, 0))),
                ((1, width), F32, whole(1, width)),
            ],
        )

    def back(self, front, segments, both, wo):
        seq_len, width, cols, half = self.seq_len, self.width, self.cols, self.half

        def body(scalars, ins, outs, scratch):
            q_ref, k_ref, v_ref, cos_ref, sin_ref, seg_ref, both_ref, wo_ref = ins
            dq_out, dkv_out = outs
            grad_all, dk_all, dv_all = scratch
            row = pl.program_id(0)
            length = scalars[1][row]
            for side in range(2):
                grad_all[side * half : (side + 1) * half, :] = outer_back(
                    both_ref[side], wo_ref[...]
                ).astype(BF16)
            seg_row = seg_ref[pl.ds(row, 1), :].astype(F32)
            dk_all[...] = jnp.zeros_like(dk_all)
            dv_all[...] = jnp.zeros_like(dv_all)
            for part in (0, 1):
                at = part * half
                keys = at + half
                allowed = allowed_pairs(seg_row, length, at, half, keys)
                key, value = k_ref[:keys], v_ref[:keys]
                for head in range(cols // HD):
                    span = slice(head * HD, (head + 1) * HD)
                    query = q_ref[at:keys, span]
                    grad = grad_all[at:keys, span]
                    weights = softmax_block(query, key, allowed)
                    weight_grad = outer_back(grad, value)
                    delta = jnp.sum(weights * weight_grad, axis=1, keepdims=True)
                    score_grad = (weights * (weight_grad - delta)).astype(BF16)
                    dq = dot(score_grad, key) * (HD**-0.5)
                    dq_out[at:keys, span] = unrotate(dq, cos_ref[at:keys], sin_ref[at:keys]).astype(BF16)
                    dk_all[:keys] += inner(score_grad, query)
                    dv_all[:keys] += inner(weights.astype(BF16), grad)
            for side in range(2):
                dkv_out[side, :, :HD] = (dk_all[...] * (HD**-0.5)).astype(BF16)
                dkv_out[side, :, HD:] = dv_all[...].astype(BF16)

        _, query, key, value, cosine, sine = front[:6]
        head = pl.BlockSpec((seq_len, HD), lambda j, *_: (j, 0))
        heads = pl.BlockSpec((seq_len, cols), lambda j, *_: (j, 0))
        return self.chain.run(
            body,
            "attention_back",
            (self.micro,),
            [
                (query, heads),
                (key, head),
                (value, head),
                (cosine, head),
                (sine, head),
                (segments, whole(*segments.shape)),
                (both, pl.BlockSpec((2, half, width), lambda j, *_: (0, j, 0))),
                (wo, whole(cols, width)),
            ],
            [
                ((self.tokens, cols), BF16, heads),
                ((2, self.tokens, 2 * HD), BF16, pl.BlockSpec((2, seq_len, 2 * HD), lambda j, *_: (0, j, 0))),
            ],
            [
                pltpu.VMEM((seq_len, cols), BF16),
                pltpu.VMEM((seq_len, HD), F32),
                pltpu.VMEM((seq_len, HD), F32),
            ],
        )

    def linear_back(self, front, dq, dkv, wq, wk, wv):
        seq_len, width, cols, half = self.seq_len, self.width, self.cols, self.half
        half_dim = HD // 2
        total = cols + HD

        def body(scalars, ins, outs, scratch):
            dq_ref, dkv_ref, cos_ref, sin_ref, wq_ref, wk_ref, wv_ref = ins
            lin_out, bias_out, parts = outs
            small_grad = scratch[0]
            core = scalars[0][0]
            both = dkv_ref[0].astype(F32) + dkv_ref[1].astype(F32)
            key = unrotate(both[:, :HD], cos_ref[...], sin_ref[...])
            value = both[:, HD:]
            low = lax.broadcasted_iota(jnp.int32, key.shape, 1) < half_dim
            first = jnp.where(low, key, pltpu.roll(value, half_dim, 1))
            second = jnp.where(low, pltpu.roll(key, half_dim, 1), value)
            own_kv = jnp.where(core == 0, first, second).astype(BF16)
            small_grad[...] = own_kv
            lin_out[:, :cols] = dq_ref[...]
            lin_out[:, cols:] = own_kv

            @pl.when(pl.program_id(0) == 0)
            def _():
                bias_out[...] = jnp.zeros_like(bias_out)

            bias_out[:, :cols] += jnp.sum(dq_ref[...].astype(F32), axis=0, keepdims=True)
            bias_out[:, cols:] += jnp.sum(own_kv.astype(F32), axis=0, keepdims=True)
            weight = jnp.concatenate([wk_ref[...], wv_ref[...]], axis=0)
            for side in range(2):
                span = slice(side * half, (side + 1) * half)
                piece = outer_back(dq_ref[span, :], wq_ref[...]) + dot(small_grad[span, :], weight)
                parts[side] = piece.astype(BF16)

        kv_rows = wk.shape[0]
        head = pl.BlockSpec((seq_len, HD), lambda j, *_: (j, 0))
        return self.chain.run(
            body,
            "linear_back",
            (self.micro,),
            [
                (dq, pl.BlockSpec((seq_len, cols), lambda j, *_: (j, 0))),
                (dkv, pl.BlockSpec((2, seq_len, 2 * HD), lambda j, *_: (0, j, 0))),
                (front[4], head),
                (front[5], head),
                (wq, whole(width, cols)),
                (wk, whole(kv_rows, width)),
                (wv, whole(kv_rows, width)),
            ],
            [
                ((self.tokens, total), BF16, pl.BlockSpec((seq_len, total), lambda j, *_: (j, 0))),
                ((1, total), F32, whole(1, total)),
                (
                    (2, self.micro * half, width),
                    BF16,
                    pl.BlockSpec((2, half, width), lambda j, *_: (0, j, 0)),
                ),
            ],
            [pltpu.VMEM((seq_len, HD), BF16)],
        )

    def last(self, inputs, own, got, hidden_grad, small):
        half, width = self.half, self.width
        step = 128
        count = half // step
        rows = self.micro * half

        def body(scalars, ins, outs, scratch):
            x_ref, own_ref, got_ref, grad_ref, small_ref = ins
            incoming = own_ref[...].astype(F32) + got_ref[...].astype(F32)
            unit, inverse = unit_rows(x_ref[...].astype(F32))
            back = grad_ref[...] + norm_back(incoming, unit, inverse, self.gain_of(small_ref, 0))
            outs[0][...] = back.astype(BF16)
            part = jnp.sum(incoming * unit, axis=0, keepdims=True)

            @pl.when(pl.program_id(0) == 0)
            def _():
                outs[1][...] = part

            @pl.when(pl.program_id(0) > 0)
            def _():
                outs[1][...] += part

        block = pl.BlockSpec((step, width), lambda j, *_: (j, 0))
        return self.chain.run(
            body,
            "norm_one_back",
            (rows // step,),
            [
                (
                    self.halves(inputs),
                    pl.BlockSpec(
                        (None, None, step, width),
                        lambda j, place, *_: (j // count, place[0], j % count, 0),
                    ),
                ),
                (own, block),
                (got, block),
                (hidden_grad, block),
                (small, whole(1, small.shape[1])),
            ],
            [((rows, width), BF16, block), ((1, width), F32, whole(1, width))],
        )

    def result(self, state, own, got):
        rows, width = state.shape
        step = 128
        block = pl.BlockSpec((step, width), lambda j, *_: (j, 0))

        def body(scalars, ins, outs, scratch):
            value = ins[0][...] + ins[1][...].astype(F32) + ins[2][...].astype(F32)
            outs[0][...] = value.astype(BF16)

        return self.chain.run(
            body,
            "result",
            (rows // step,),
            [(state, block), (own, block), (got, block)],
            [((rows, width), BF16, block)],
        )[0]


class Halving:
    def __init__(self, chain, left, right, masks, cols, columns=None, at=0, direct=False):
        self.chain, self.left, self.right, self.masks, self.cols = chain, left, right, masks, cols
        total = left.shape[1]
        levels = len(masks)
        self.sizes = [total >> (level + 1) for level in range(levels)] + [total >> levels]
        self.starts = [total - (total >> level) for level in range(levels + 1)]
        self.parts = []
        self.columns = right.shape[2] if columns is None else columns
        self.at = at
        self.direct = direct
        self.level = 0
        self.received = []
        self.result = None

    def product(self, first, last, into=()):
        parts, _, span = self.left.shape
        tiles, tokens, tile = self.right.shape
        sizes = self.sizes[first:last]
        offset = self.starts[first]
        rows = sum(sizes)
        column, columns = self.at, self.columns

        def body(scalars, refs, outs, scratch):
            left, right, made, left_sems, in_sems, out_sems = scratch
            lefts = copies(
                [
                    (refs[0].at[part, pl.ds(offset, rows)], left.at[:, pl.ds(part * span, span)])
                    for part in range(parts)
                ],
                left_sems,
            )

            def load(index):
                return pltpu.make_async_copy(refs[1].at[index], right.at[index], in_sems.at[index])

            def stores(index):
                at = 0
                found = []
                for number, size in enumerate(sizes):
                    found.append(
                        pltpu.make_async_copy(
                            made.at[index, pl.ds(at, size)],
                            outs[number].at[index, :, pl.ds(column, tile)],
                            out_sems.at[index, number],
                        )
                    )
                    at += size
                return found

            each(tiles, lambda index: load(index).start())
            for copy in lefts:
                copy.wait()

            def one(index):
                load(index).wait()

                made[index] = dot(left[...], right[index]).astype(BF16)
                for store in stores(index):
                    store.start()

            each(tiles, one)

            def end(index):
                for store in stores(index):
                    store.wait()

            each(tiles, end)

        self.parts += self.chain.run(
            body,
            "gradient_product",
            (1,),
            [(self.left, ANYWHERE), (self.right, ANYWHERE)],
            [((tiles, size, columns), BF16, ANYWHERE) for size in sizes],
            [
                pltpu.VMEM((rows, tokens), BF16),
                pltpu.VMEM((tiles, tokens, tile), BF16),
                pltpu.VMEM((tiles, rows, tile), BF16),
                pltpu.SemaphoreType.DMA((parts,)),
                pltpu.SemaphoreType.DMA((tiles,)),
                pltpu.SemaphoreType.DMA((tiles, len(sizes))),
            ],
            into=into,
        )
        return self

    def send(self):
        if self.level == len(self.masks):
            return self
        if self.direct and self.level == len(self.masks) - 2:
            return self.send_direct()
        value = self.parts[self.level]
        if self.received:
            tiles, size, tile = value.shape
            start = self.starts[self.level]
            ins = [(value, whole(tiles, size, tile))]
            for piece, base in self.received:
                at = (start - base) // size
                ins.append((piece, pl.BlockSpec((tiles, size, tile), lambda *_, at=at: (0, at, 0))))

            def body(scalars, refs, outs, scratch):
                def one(index):
                    total = refs[0][index].astype(F32)
                    for ref in refs[1:]:
                        total = total + ref[index].astype(F32)
                    outs[0][index] = total.astype(BF16)

                each(tiles, one)

            (value,) = self.chain.run(
                body, "gradient_add", (1,), ins, [((tiles, size, tile), BF16, whole(tiles, size, tile))]
            )
        after = self.starts[self.level + 1]
        self.received.append((swap(value, "wide", self.masks[self.level]), after))
        self.level += 1
        return self

    def send_direct(self):
        first, second = self.masks[-2:]
        pair, single = self.parts[self.level], self.parts[self.level + 1]
        tiles, rows, tile = single.shape
        start = self.starts[self.level]
        ins = [(pair, whole(tiles, 2 * rows, tile)), (single, whole(tiles, rows, tile))]
        for piece, base in self.received:
            for index in range(3):
                at = (start - base) // rows + index
                ins.append((piece, pl.BlockSpec((tiles, rows, tile), lambda *_, at=at: (0, at, 0))))

        def body(scalars, refs, outs, scratch):
            def one(index):
                for block in range(3):
                    if block < 2:
                        total = refs[0][index, block * rows : (block + 1) * rows].astype(F32)
                    else:
                        total = refs[1][index].astype(F32)
                    for ref in refs[2 + block :: 3]:
                        total = total + ref[index].astype(F32)
                    outs[block][index] = total.astype(BF16)

            each(tiles, one)

        shape = (tiles, rows, tile)
        values = self.chain.run(body, "gradient_add", (1,), ins, [(shape, BF16, whole(*shape))] * 3)
        for value, mask in zip(values, (first ^ second, first, second)):
            self.received.append((swap(value, "wide", mask), self.starts[-1]))
        self.level = len(self.masks)
        return self

    def total(self):
        if self.result is not None:
            return self.result
        while self.level < len(self.masks):
            self.send()
        rows, start = self.sizes[-1], self.starts[-1]
        tiles, tile = self.right.shape[0], self.columns
        cols = self.cols
        ins = [(self.parts[-1], whole(tiles, rows, tile))]
        for piece, base in self.received:
            at = (start - base) // rows
            ins.append((piece, pl.BlockSpec((tiles, rows, tile), lambda *_, at=at: (0, at, 0))))

        def body(scalars, refs, outs, scratch):
            for index in range(tiles):
                value = refs[0][index].astype(F32)
                for ref in refs[1:]:
                    value = value + ref[index].astype(F32)
                size = min(tile, cols - index * tile)
                outs[0][:, index * tile : index * tile + size] = value[:, :size]

        (self.result,) = self.chain.run(
            body, "gradient_total", (1,), ins, [((rows, cols), F32, whole(rows, cols))]
        )
        return self.result


def doubling_sum(value, axis, masks):
    for mask in masks:
        value = value + swap(value, axis, mask)
    return value


def body(
    inputs,
    out_grad,
    norm_gain,
    query_weight,
    query_bias,
    key_weight,
    key_bias,
    value_weight,
    value_bias,
    output_weight,
    ffn_gain,
    gate_weight,
    up_weight,
    down_weight,
    lengths,
    segments,
    positions,
):
    micro, seq_len, width = inputs.shape
    cols = query_weight.shape[1]
    hidden_units = gate_weight.shape[1]
    layer = Layer(inputs, cols, hidden_units)
    half, tokens = layer.half, layer.tokens
    place = jnp.stack([layer.core, lax.axis_index("wide")]).astype(jnp.int32)
    chain = Chain([place, lengths])
    layer.chain = chain
    wide_masks = masks_of("wide")
    down_masks, up_masks, gate_masks, joint_masks = [
        [wide_masks[int(place)] for place in places] + wide_masks[3:] for places in MASKS.split()
    ]
    key_rows, value_rows = key_weight.T, value_weight.T
    gate_rows, up_rows = gate_weight.T, up_weight.T
    small = jnp.concatenate([norm_gain, ffn_gain, query_bias, key_bias, value_bias]).astype(F32)[None]
    small_oth = swap(small, "narrow", 1)
    kv = (key_rows, value_rows, swap(key_rows, "narrow", 1), swap(value_rows, "narrow", 1))
    grad_flat = out_grad.reshape(tokens, width)
    halves_grad = layer.halves(out_grad)
    front = layer.front(inputs, small, small_oth, query_weight, kv, segments, positions, output_weight)
    pair = (front[6], swap(front[7], "narrow", 1))
    one_own, one_got = layer.to_other_chip(pair, sizes=(micro * half,))
    mixed = front[0]
    (grad_turned,) = layer.turn(
        [
            (
                halves_grad,
                pl.BlockSpec((None, None, TILE, width), lambda j, *_: (j % micro, j // micro, 0, 0)),
            )
        ],
        (block_order(down_masks),),
    )
    act_grad = layer.act_grad(out_grad, down_weight)
    (one_turned,) = layer.turn(
        [(inputs.reshape(tokens, width), pl.BlockSpec((TILE, width), lambda j, *_: (j, 0)))], (block_order(joint_masks),), small
    )
    state, normed = layer.hidden_state(inputs, small, one_own, one_got)
    normed = [normed, swap(normed, "narrow", 1)]
    act, dgate, dup = layer.expand(normed, gate_rows, up_rows, act_grad)
    levels = len(wide_masks)
    lin_cols = cols + HD
    made = {}
    down = Halving(chain, grad_turned, act, down_masks, hidden_units, direct="d" in DIRECT)

    def turn_two():
        made["two"] = layer.turn_pieces(normed, (block_order(gate_masks), block_order(up_masks)))

    def up_product():
        made["up"] = Halving(chain, made["two"][1], dup, up_masks, hidden_units, direct="u" in DIRECT).product(0, levels + 1)
        made["up"].send()

    def gate_product():
        made["gate"] = Halving(chain, made["two"][0], dgate, gate_masks, hidden_units, direct="g" in DIRECT).product(0, levels + 1)
        made["gate"].send()

    def shrink_two():
        made["two_sum"] = layer.across(layer.shrink([(dgate, gate_rows), (dup, up_rows)]))

    def shrink_ffn():
        made["ffn"] = layer.shrink([(act, down_weight)])

    def across_ffn():
        made["ffn_sum"] = layer.across(made["ffn"])

    def middle():
        made["hidden_grad"], branch, made["ffn_gain"] = layer.middle(state, *made["two_sum"], out_grad, small)
        made["branch"] = pair_exchange(branch)

    def back():
        made["dq"], made["dkv"] = layer.back(front, segments, made["branch"], output_weight)

    def linear():
        made["lin_grad"], made["bias"], parts = layer.linear_back(
            front, made["dq"], pair_exchange(made["dkv"]), query_weight, key_rows, value_rows
        )
        made["one_sum"] = layer.across(parts)

    def linear_product():
        right = made["lin_grad"][None]
        made["lin"] = Halving(chain, one_turned, right, joint_masks, lin_cols + cols, lin_cols + cols)
        made["lin"].product(0, levels + 1)

    def turn_branch():
        (made["branch_turned"],) = layer.turn_pieces([made["branch"].reshape(tokens, width)], (block_order(joint_masks),))

    def output_product():
        right = mixed.reshape(1, tokens, cols)
        both = lin_cols + cols
        made["joint"] = Halving(chain, made["branch_turned"], right, joint_masks, both, both, lin_cols, "l" in DIRECT)
        made["joint"].product(0, levels + 1, tuple(made["lin"].parts)).send()

    def result():
        own = layer.result(state, made["ffn_sum"][0], made["ffn_sum"][1][0])
        made["result"] = (own, swap(own, "narrow", 1))

    def last():
        own, made["norm_gain"] = layer.last(
            inputs, made["one_sum"][0], made["one_sum"][1][0], made["hidden_grad"], small
        )
        made["input"] = (own, swap(own, "narrow", 1))

    def pack():
        packed = jnp.concatenate([made["bias"], made["norm_gain"], made["ffn_gain"]], axis=1)
        packed = share_wide(packed + chain.token[:1, :1])
        both = pair_exchange(jnp.broadcast_to(packed[:, cols + HD :], (2, 2 * width)))
        made["packed"] = chain.hold(packed, both[0] + both[1])

    def total(name):
        made[name + "_out"] = made[name].total()

    made["down"] = down
    steps = {
        "pk": pack,
        "pd1": lambda: down.product(0, 1).send(),
        "pdr": lambda: down.product(1, levels + 1),
        "tn": turn_two,
        "pu": up_product,
        "pg": gate_product,
        "s2": shrink_two,
        "sF": shrink_ffn,
        "xF": across_ffn,
        "mid": middle,
        "bk": back,
        "ln": linear,
        "plo": linear_product,
        "ta": turn_branch,
        "pout": output_product,
        "res": result,
        "last": last,
        "jr": lambda: made.update(result_out=layer.join(*made["result"])),
        "ji": lambda: made.update(input_out=layer.join(*made["input"])),
        "ad": lambda: down.send(),
        "au": lambda: made["up"].send(),
        "ag": lambda: made["gate"].send(),
        "al": lambda: made["joint"].send(),
        "td": lambda: total("down"),
        "tu": lambda: total("up"),
        "tg": lambda: total("gate"),
        "tl": lambda: total("joint"),
    }
    for name in " ".join(ORDER).split():
        if name.startswith("c"):
            chain.scale = 1e8 * int(name[1:])
        else:
            steps[name]()
    result, input_grad = made["result_out"], made["input_out"]
    down_out, up_out, gate_out = made["down_out"], made["up_out"], made["gate_out"]
    lin_out, output_out = made["joint_out"][:, :lin_cols], made["joint_out"][:, lin_cols:]
    packed, gain_out = made["packed"]
    part = HD // 2
    query_out, key_out, value_out = jnp.split(lin_out, [cols, cols + part], axis=1)
    query_bias_out, key_bias_out, value_bias_out, _ = jnp.split(
        packed[0], [cols, cols + part, cols + 2 * part]
    )
    norm_gain_out, ffn_gain_out = gain_out[:width], gain_out[width:]
    return (
        result,
        input_grad,
        norm_gain_out,
        query_out,
        query_bias_out,
        key_out,
        key_bias_out,
        value_out,
        value_bias_out,
        output_out.T,
        ffn_gain_out,
        gate_out,
        up_out,
        down_out.T,
    )


def solution(mesh):
    placed = (
        P("wide", None, None),
        P("wide", None, None),
        P(),
        P(None, "narrow"),
        P("narrow"),
        P(None, "narrow"),
        P("narrow"),
        P(None, "narrow"),
        P("narrow"),
        P("narrow", None),
        P(),
        P(None, "narrow"),
        P(None, "narrow"),
        P("narrow", None),
        P("wide"),
        P("wide", None),
        P("wide", None),
    )
    return jax.shard_map(
        body,
        mesh=mesh,
        in_specs=placed,
        out_specs=(
            P("wide", None, None),
            P("wide", None, None),
            P(),
            P("wide", "narrow"),
            P("narrow"),
            P("wide", "narrow"),
            P("narrow"),
            P("wide", "narrow"),
            P("narrow"),
            P("narrow", "wide"),
            P(),
            P("wide", "narrow"),
            P("wide", "narrow"),
            P("narrow", "wide"),
        ),
        check_vma=False,
    )
```

```python
import functools

import jax
import jax.numpy as jnp
from jax import lax
from jax.experimental import pallas as pl
from jax.experimental.pallas import tpu as pltpu
from jax.sharding import PartitionSpec as P

HD = 128


NORM_EPS = 1e-06
ROPE_BASE = 10000.0
NEG_FILL = -1e30
F32 = jnp.float32
BF16 = jnp.bfloat16
TILE = 256
VMEM_LIMIT = 64 << 20
ORDER = (
    "pd1 tn pu s2",
    "pg pdr sF mid",
    "ad au xF bk",
    "ad ln plo c4",
    "ag ta pout td",
    "au res last ag",
    "jr al ji gp",
    "al tu tg tl",
    "pk",
)
MASKS = "012 102 012 012"
DIRECT = ""


def swap(value, axis, mask):
    pairs = [(source, source ^ mask) for source in range(lax.axis_size(axis))]
    return lax.ppermute(value, axis, pairs)


def pair_exchange(value):
    size = lax.axis_size("narrow")
    pairs = [[first, first + 1] for first in range(0, size, 2)]
    return lax.all_to_all(value, "narrow", 0, 0, axis_index_groups=pairs, tiled=True)


def share_wide(value):
    count = lax.axis_size("wide")
    spread = jnp.broadcast_to(value, (count,) + value.shape[1:])
    return jnp.sum(lax.all_to_all(spread, "wide", 0, 0, tiled=True), axis=0, keepdims=True)


def swap_pieces(value, mask, count):
    return [swap(piece, "narrow", mask) for piece in jnp.split(value, count, axis=0)]


def swap_in_turn(value, axis, mask, sizes):
    if len(sizes) == 1:
        return swap(value, axis, mask)
    arrived = []
    last = 0
    for size in sizes:
        first, last = last, last + size
        piece = value[first:last]
        if arrived:
            arrived[-1], piece = lax.optimization_barrier((arrived[-1], piece))
        arrived.append(swap(piece, axis, mask))
    return jnp.concatenate(arrived, axis=0)


def masks_of(axis):
    return [1 << bit for bit in range(lax.axis_size(axis).bit_length() - 1)]


def block_order(masks):
    order = [0]
    for mask in reversed(masks):
        order = [mask ^ block for block in order] + order
    return order


def dot(left, right):
    return jnp.dot(left, right, preferred_element_type=F32)


def outer_back(left, right):
    return lax.dot_general(left, right, (((1,), (1,)), ((), ())), preferred_element_type=F32)


def inner(left, right):
    return lax.dot_general(left, right, (((0,), (0,)), ((), ())), preferred_element_type=F32)


def whole(*shape):
    return pl.BlockSpec(shape, lambda *_: (0,) * len(shape))


ANYWHERE = pl.BlockSpec(memory_space=pl.ANY)


TIMES = {
    "attention_back": 13,
    "linear_back": 7,
    "ffn_shrink": 13,
    "gradient_product": 8,
    "turn_pieces": 6,
    "norm_two_back": 8,
    "norm_one_back": 6,
    "gradient_add": 4,
    "gradient_total": 4,
    "result": 5,
    "join_tokens": 4,
}


class Chain:
    def __init__(self, scalars):
        self.scalars = scalars
        self.token = None
        self.scale = 0.0

    def hold(self, *values):
        self.token, *held = lax.optimization_barrier((self.token, *values))
        return held

    def run(self, body, name, grid, ins, outs, scratch=(), into=(), after=(), flops=1):
        extra = list(into) + ([] if self.token is None else [self.token]) + list(after)
        count, given, made = len(self.scalars), len(ins), len(outs)

        def kernel(*refs):
            scalars = refs[:count]
            used = refs[count : count + given]
            results = refs[count + given + len(extra) :]
            results[made][...] = jnp.zeros_like(results[made])
            body(scalars, used, results[:made], results[made + 1 :])

        results = pl.pallas_call(
            kernel,
            out_shape=[jax.ShapeDtypeStruct(shape, dtype) for shape, dtype, _ in outs]
            + [jax.ShapeDtypeStruct((8, 128), F32)],
            grid_spec=pltpu.PrefetchScalarGridSpec(
                num_scalar_prefetch=count,
                grid=grid,
                in_specs=[spec for _, spec in ins] + [ANYWHERE] * len(extra),
                out_specs=[spec for _, _, spec in outs] + [whole(8, 128)],
                scratch_shapes=list(scratch),
            ),
            input_output_aliases={count + given + index: index for index in range(len(into))},
            compiler_params=pltpu.CompilerParams(
                dimension_semantics=("arbitrary",) * len(grid), vmem_limit_bytes=VMEM_LIMIT
            ),
            cost_estimate=pl.CostEstimate(
                flops=int(self.scale * TIMES.get(name, 5)) + 1, bytes_accessed=1, transcendentals=0
            ),
            name=name,
        )(*self.scalars, *[array for array, _ in ins], *extra)
        self.token = results[-1]
        return results[:-1]


def copies(pairs, sems):
    started = []
    for index, (source, target) in enumerate(pairs):
        copy = pltpu.make_async_copy(source, target, sems.at[index])
        copy.start()
        started.append(copy)
    return started


class Tiles:
    def __init__(self, source, target, sems, total, tile):
        self.source, self.target, self.sems, self.tile = source, target, sems, tile
        self.full, self.rest = divmod(total, tile)

    def make(self, index, size):
        at = pl.multiple_of(index * self.tile, self.tile)
        return pltpu.make_async_copy(
            self.source.at[pl.ds(at, size)], self.target.at[index, pl.ds(0, size)], self.sems.at[index]
        )

    def start(self):
        for index in range(self.full):
            self.make(index, self.tile).start()
        if self.rest:
            self.make(self.full, self.rest).start()

    def wait(self, index):
        if not self.rest:
            self.make(index, self.tile).wait()
            return

        @pl.when(index < self.full)
        def _():
            self.make(index, self.tile).wait()

        @pl.when(index == self.full)
        def _():
            self.make(self.full, self.rest).wait()


def each(count, body):
    def run(index, carry):
        body(index)
        return carry

    lax.fori_loop(0, count, run, 0)


def unit_rows(values):
    inverse = lax.rsqrt(jnp.mean(values * values, axis=-1, keepdims=True) + NORM_EPS)
    return values * inverse, inverse


def norm_back(grad, unit, inverse, gain):
    grown = grad * gain
    return inverse * (grown - unit * jnp.mean(grown * unit, axis=-1, keepdims=True))


def rotate(values, cosine, sine):
    return values * cosine + pltpu.roll(values, HD // 2, 1) * sine


def unrotate(grads, cosine, sine):
    return grads * cosine + pltpu.roll(grads * sine, HD // 2, 1)


def down_rows(row, count):
    return jnp.broadcast_to(row, (128, count)).T


def allowed_pairs(seg_row, length, first, count, keys):
    turned = down_rows(seg_row[:, first : first + count], count)
    own = jnp.concatenate([turned] * (keys // 128), axis=1)
    rows = lax.broadcasted_iota(jnp.int32, (count, keys), 0) + first
    cols = lax.broadcasted_iota(jnp.int32, (count, keys), 1)
    same = own == jnp.broadcast_to(seg_row[:, :keys], (count, keys))
    return same & (cols <= rows) & ((cols < length) | (cols == rows))


def softmax_block(query, keys, allowed):
    scores = jnp.where(allowed, outer_back(query, keys) * (HD**-0.5), NEG_FILL)
    top = jnp.max(scores, axis=1, keepdims=True)
    grown = jnp.exp(scores - top)
    return grown * (1.0 / jnp.sum(grown, axis=1, keepdims=True))


class Layer:
    def __init__(self, inputs, cols, hidden):
        self.micro, self.seq_len, self.width = inputs.shape
        self.half = self.seq_len // 2
        self.tokens = self.micro * self.seq_len
        self.cols = cols
        self.hidden = hidden
        self.core = lax.axis_index("narrow") % 2
        self.even = self.core == 0
        self.narrow_masks = masks_of("narrow")
        self.chain = None

    def gain_of(self, small_ref, index):
        return small_ref[:, index * self.width : (index + 1) * self.width]

    def halves(self, value):
        return value.reshape(self.micro, 2, self.half, self.width)

    def across(self, parts, count=1, sizes=None):
        return self.to_other_chip(pair_exchange(parts), count, sizes)

    def to_other_chip(self, got, count=1, sizes=None):
        total = (got[0].astype(F32) + got[1].astype(F32)).astype(BF16)
        for mask in self.narrow_masks[1:-1]:
            total = (total.astype(F32) + swap(total, "narrow", mask).astype(F32)).astype(BF16)
        (total,) = self.chain.hold(total)
        if sizes is not None:
            return total, swap_in_turn(total, "narrow", self.narrow_masks[-1], sizes)
        return total, swap_pieces(total, self.narrow_masks[-1], count)

    def join(self, own, other):
        half, width, seq_len = self.half, self.width, self.seq_len
        block = pl.BlockSpec((half, width), lambda j, *_: (j, 0))

        def body(scalars, ins, outs, scratch):
            core = scalars[0][0]
            outs[0][pl.ds(pl.multiple_of(core * half, half), half), :] = ins[0][...]
            outs[0][pl.ds(pl.multiple_of((1 - core) * half, half), half), :] = ins[1][...]

        return self.chain.run(
            body,
            "join_tokens",
            (self.micro,),
            [(own, block), (other, block)],
            [
                (
                    (self.micro, seq_len, width),
                    BF16,
                    pl.BlockSpec((None, seq_len, width), lambda j, *_: (j, 0, 0)),
                )
            ],
        )[0]

    def front(self, inputs, small, small_oth, wq, kv, segments, positions, wo):
        seq_len, width, cols, half = self.seq_len, self.width, self.cols, self.half
        bias_at = 2 * width
        step = 128
        half_dim = HD // 2

        def body(scalars, ins, outs, scratch):
            x_ref, small_ref, oth_ref, wq_ref, wk_own, wv_own, wk_oth, wv_oth, seg_ref, pos_ref, wo_ref = ins
            mixed_out, q_out, k_out, v_out, cos_out, sin_out, part_own, part_oth = outs
            normed, mixed_all = scratch
            core = scalars[0][0]
            length = scalars[1][pl.program_id(0)]
            even = core == 0
            gain = self.gain_of(small_ref, 0)

            def norm_rows(index, carry):
                span = pl.ds(pl.multiple_of(index * step, step), step)
                unit, _ = unit_rows(x_ref[span, :].astype(F32))
                normed[span, :] = (unit * gain).astype(BF16)
                return carry

            lax.fori_loop(0, seq_len // step, norm_rows, 0)
            lane = lax.broadcasted_iota(jnp.int32, (1, HD), 1)
            exponent = jnp.where(lane < half_dim, lane, lane - half_dim).astype(F32) * (2.0 / HD)
            freq = jnp.exp(exponent * (-jnp.log(F32(ROPE_BASE))))
            place = down_rows(pos_ref[pl.ds(pl.program_id(0), 1), :].astype(F32), seq_len)
            angle = place * freq
            cosine = jnp.cos(angle)
            sine = jnp.where(lane < half_dim, -1.0, 1.0) * jnp.sin(angle)
            cos_out[...] = cosine
            sin_out[...] = sine
            rows = normed[...]
            first_k = jnp.where(even, wk_own[...], wk_oth[...])
            second_k = jnp.where(even, wk_oth[...], wk_own[...])
            first_v = jnp.where(even, wv_own[...], wv_oth[...])
            second_v = jnp.where(even, wv_oth[...], wv_own[...])
            kv = jnp.concatenate([first_k, second_k, first_v, second_v], axis=0)
            lin = outer_back(rows, kv)
            own_bias = small_ref[:, bias_at + cols : bias_at + cols + HD]
            oth_bias = oth_ref[:, bias_at + cols : bias_at + cols + HD]
            left = jnp.where(even, own_bias, oth_bias)
            right = jnp.where(even, oth_bias, own_bias)
            key_bias = jnp.where(lane < half_dim, left, pltpu.roll(right, half_dim, 1))
            value_bias = jnp.where(lane < half_dim, pltpu.roll(left, half_dim, 1), right)
            key = rotate(lin[:, :HD] + key_bias, cosine, sine).astype(BF16)
            value = (lin[:, HD:] + value_bias).astype(BF16)
            k_out[...] = key
            v_out[...] = value
            query_lin = dot(rows, wq_ref[...]) + small_ref[:, bias_at : bias_at + cols]
            seg_row = seg_ref[pl.ds(pl.program_id(0), 1), :].astype(F32)
            masks = [allowed_pairs(seg_row, length, at, half, at + half) for at in (0, half)]
            for head in range(cols // HD):
                span = slice(head * HD, (head + 1) * HD)
                query = rotate(query_lin[:, span], cosine, sine).astype(BF16)
                q_out[:, span] = query
                for part, allowed in enumerate(masks):
                    at = part * half
                    keys = at + half
                    weights = softmax_block(query[at:keys], key[:keys], allowed).astype(BF16)
                    mixed_all[at:keys, span] = dot(weights, value[:keys]).astype(BF16)
            for side in range(2):
                mixed_out[side] = mixed_all[side * half : (side + 1) * half, :]
            for side, part in ((core, part_own), (1 - core, part_oth)):
                some = mixed_all[pl.ds(pl.multiple_of(side * half, half), half), :]
                part[...] = dot(some, wo_ref[...]).astype(BF16)

        small_size = small.shape[1]
        kv_rows = kv[0].shape[0]
        return self.chain.run(
            body,
            "attention_front",
            (self.micro,),
            [
                (inputs, pl.BlockSpec((None, seq_len, width), lambda j, *_: (j, 0, 0))),
                (small, whole(1, small_size)),
                (small_oth, whole(1, small_size)),
                (wq, whole(width, cols)),
            ]
            + [(piece, whole(kv_rows, width)) for piece in kv]
            + [
                (segments, whole(*segments.shape)),
                (positions, whole(*positions.shape)),
                (wo, whole(cols, width)),
            ],
            [
                ((2, self.micro * half, cols), BF16, pl.BlockSpec((2, half, cols), lambda j, *_: (0, j, 0))),
                ((self.tokens, cols), BF16, pl.BlockSpec((seq_len, cols), lambda j, *_: (j, 0))),
                ((self.tokens, HD), BF16, pl.BlockSpec((seq_len, HD), lambda j, *_: (j, 0))),
                ((self.tokens, HD), BF16, pl.BlockSpec((seq_len, HD), lambda j, *_: (j, 0))),
                ((self.tokens, HD), F32, pl.BlockSpec((seq_len, HD), lambda j, *_: (j, 0))),
                ((self.tokens, HD), F32, pl.BlockSpec((seq_len, HD), lambda j, *_: (j, 0))),
                ((self.micro * half, width), BF16, pl.BlockSpec((half, width), lambda j, *_: (j, 0))),
                ((self.micro * half, width), BF16, pl.BlockSpec((half, width), lambda j, *_: (j, 0))),
            ],
            [pltpu.VMEM((seq_len, width), BF16), pltpu.VMEM((seq_len, cols), BF16)],
        )

    def act_grad(self, grad, wd):
        tokens, width, half, micro = self.tokens, self.width, self.half, self.micro
        hidden = self.hidden
        tiles = pl.cdiv(hidden, TILE)

        def body(scalars, ins, outs, scratch):
            grad_ref, wd_ref = ins
            rows, weights, made, row_sems, in_sems, out_sems = scratch
            lines = copies(
                [
                    (grad_ref.at[row, side], rows.at[pl.ds((side * micro + row) * half, half)])
                    for side in range(2)
                    for row in range(micro)
                ],
                row_sems,
            )
            loads = Tiles(wd_ref, weights, in_sems, hidden, TILE)
            loads.start()
            for copy in lines:
                copy.wait()

            def store(index):
                return pltpu.make_async_copy(made.at[index], outs[0].at[index], out_sems.at[index])

            def one(index):
                loads.wait(index)
                made[index] = outer_back(rows[...], weights[index]).astype(BF16)
                store(index).start()

            each(tiles, one)
            each(tiles, lambda index: store(index).wait())

        return self.chain.run(
            body,
            "activation_grad",
            (1,),
            [(self.halves(grad), ANYWHERE), (wd, ANYWHERE)],
            [((tiles, tokens, TILE), BF16, ANYWHERE)],
            [
                pltpu.VMEM((tokens, width), BF16),
                pltpu.VMEM((tiles, TILE, width), BF16),
                pltpu.VMEM((tiles, tokens, TILE), BF16),
                pltpu.SemaphoreType.DMA((2 * micro,)),
                pltpu.SemaphoreType.DMA((tiles,)),
                pltpu.SemaphoreType.DMA((tiles,)),
            ],
        )[0]

    def hidden_state(self, inputs, small, own, got):
        half, width = self.half, self.width
        step = 128
        count = half // step
        rows = self.micro * half

        def body(scalars, ins, outs, scratch):
            x_ref, small_ref, own_ref, got_ref = ins
            branch = own_ref[...].astype(F32) + got_ref[...].astype(F32)
            state = x_ref[...].astype(F32) + branch
            outs[0][...] = state
            unit, _ = unit_rows(state)
            outs[1][...] = (unit * self.gain_of(small_ref, 1)).astype(BF16)

        part = pl.BlockSpec((step, width), lambda j, *_: (j, 0))
        return self.chain.run(
            body,
            "hidden_norm",
            (rows // step,),
            [
                (
                    self.halves(inputs),
                    pl.BlockSpec(
                        (None, None, step, width), lambda j, place, *_: (j // count, place[0], j % count, 0)
                    ),
                ),
                (small, whole(1, small.shape[1])),
                (own, part),
                (got, part),
            ],
            [((rows, width), F32, part), ((rows, width), BF16, part)],
        )

    def placed(self, scalars, refs, target):
        core = scalars[0][0]
        rows = refs[0].shape[0]
        if len(refs) == 1:
            return [(refs[0], target)]
        spots = [pl.multiple_of(side * rows, rows) for side in (core, 1 - core)]
        return [(ref, target.at[pl.ds(spot, rows)]) for ref, spot in zip(refs, spots)]

    def expand(self, rows_in, wg, wu, act_grad):
        width, hidden, tokens = self.width, self.hidden, self.tokens
        tiles = pl.cdiv(hidden, TILE)

        def body(scalars, ins, outs, scratch):
            *row_refs, wg_ref, wu_ref, grad_ref = ins
            rows, gates, ups, grads, made, row_sems, gate_sems, up_sems, grad_sems, out_sems = scratch
            sides = copies(self.placed(scalars, row_refs, rows), row_sems)
            first = Tiles(wg_ref, gates, gate_sems, hidden, TILE)
            second = Tiles(wu_ref, ups, up_sems, hidden, TILE)
            first.start()
            second.start()

            def grad_loads(index):
                return [pltpu.make_async_copy(grad_ref.at[index], grads.at[index], grad_sems.at[index])]

            def store(index, kind):
                return pltpu.make_async_copy(
                    made.at[index % 2, kind], outs[kind].at[index], out_sems.at[index % 2, kind]
                )

            def begin(index):
                for copy in grad_loads(index):
                    copy.start()

            each(tiles, begin)
            for copy in sides:
                copy.wait()
            lane = lax.broadcasted_iota(jnp.int32, (1, TILE), 1)

            def one(index):
                first.wait(index)
                second.wait(index)
                for copy in grad_loads(index):
                    copy.wait()

                @pl.when(index >= 2)
                def _():
                    for kind in range(3):
                        store(index - 2, kind).wait()

                def part(number):
                    span = slice(number, tokens)
                    gate = outer_back(rows[span, :], gates[index])
                    upper = outer_back(rows[span, :], ups[index])
                    grad = grads[index, span, :].astype(F32)
                    sig = 0.5 * jnp.tanh(0.5 * gate) + 0.5
                    silu = gate * sig
                    slot = index % 2
                    made[slot, 0, span, :] = (silu * upper).astype(BF16)
                    made[slot, 1, span, :] = (grad * upper * (sig + silu * (1.0 - sig))).astype(BF16)
                    made[slot, 2, span, :] = (grad * silu).astype(BF16)

                part(0)
                if hidden % TILE:

                    @pl.when(index == tiles - 1)
                    def _():
                        slot = (tiles - 1) % 2
                        blank = jnp.zeros((3, tokens, TILE // 2), BF16)
                        spare = lane[:, TILE // 2 :] < hidden % TILE
                        if hidden % TILE <= TILE // 2:
                            made[slot, :, :, TILE // 2 :] = blank
                            spare = lane[:, : TILE // 2] < hidden % TILE
                            made[slot, :, :, : TILE // 2] = jnp.where(
                                spare, made[slot, :, :, : TILE // 2], blank
                            )
                        else:
                            made[slot, :, :, TILE // 2 :] = jnp.where(
                                spare, made[slot, :, :, TILE // 2 :], blank
                            )

                for kind in range(3):
                    store(index, kind).start()

            each(tiles, one)
            for index in range(max(tiles - 2, 0), tiles):
                for kind in range(3):
                    store(index, kind).wait()

        return self.chain.run(
            body,
            "ffn_expand",
            (1,),
            [(piece, ANYWHERE) for piece in rows_in]
            + [(wg, ANYWHERE), (wu, ANYWHERE), (act_grad, ANYWHERE)],
            [((tiles, tokens, TILE), BF16, ANYWHERE)] * 3,
            [
                pltpu.VMEM((tokens, width), BF16),
                pltpu.VMEM((tiles, TILE, width), BF16),
                pltpu.VMEM((tiles, TILE, width), BF16),
                pltpu.VMEM((tiles, tokens, TILE), BF16),
                pltpu.VMEM((2, 3, tokens, TILE), BF16),
                pltpu.SemaphoreType.DMA((len(rows_in),)),
                pltpu.SemaphoreType.DMA((tiles,)),
                pltpu.SemaphoreType.DMA((tiles,)),
                pltpu.SemaphoreType.DMA((tiles,)),
                pltpu.SemaphoreType.DMA((2, 3)),
            ],
        )

    def turn(self, blocks, orders, small=None):
        width = self.width
        arrays = [entry[:2] for entry in blocks]
        steps = self.tokens // TILE
        count = len(orders[0])
        rows = width // count

        def body(scalars, ins, outs, scratch):
            turned = scratch[0]
            if small is not None:
                unit, _ = unit_rows(ins[0][...].astype(F32))
                turned[...] = (unit * self.gain_of(ins[1], 0)).astype(BF16).T
            elif len(ins) == 1:
                turned[...] = ins[0][...].T
            else:
                for index, ref in enumerate(ins):
                    @pl.when((pl.program_id(0) >= blocks[index][2]) & (pl.program_id(0) < blocks[index][3]))
                    def _():
                        turned[...] = ref[...].T
            place = scalars[0][1]
            for order, out in zip(orders, outs):
                for index, block in enumerate(order):
                    source = pl.multiple_of((place ^ block) * rows, rows)
                    out[0, index * rows : (index + 1) * rows, :] = turned[pl.ds(source, rows), :]

        ins = arrays + ([] if small is None else [(small, whole(1, small.shape[1]))])
        return self.chain.run(
            body,
            "turn_blocks",
            (steps,),
            ins,
            [((steps, width, TILE), BF16, pl.BlockSpec((1, width, TILE), lambda j, *_: (j, 0, 0)))] * len(orders),
            [pltpu.VMEM((width, TILE), BF16)],
        )

    def turn_pieces(self, pieces, orders):
        width, tokens = self.width, self.tokens
        steps = tokens // TILE
        count = len(orders[0])
        rows = width // count

        def body(scalars, ins, outs, scratch):
            stacked, turned, made, in_sems, out_sems = scratch
            for copy in copies(self.placed(scalars, ins, stacked), in_sems):
                copy.wait()
            place = scalars[0][1]

            def store(step, number):
                return pltpu.make_async_copy(
                    made.at[number, step], outs[number].at[step], out_sems.at[number, step]
                )

            def one(step):
                turned[...] = stacked[pl.ds(pl.multiple_of(step * TILE, TILE), TILE), :].T
                for number, order in enumerate(orders):
                    for index, block in enumerate(order):
                        source = pl.multiple_of((place ^ block) * rows, rows)
                        made[number, step, index * rows : (index + 1) * rows, :] = turned[
                            pl.ds(source, rows), :
                        ]
                    store(step, number).start()

            each(steps, one)
            for number in range(len(orders)):
                each(steps, lambda step: store(step, number).wait())

        return self.chain.run(
            body,
            "turn_pieces",
            (1,),
            [(piece, ANYWHERE) for piece in pieces],
            [((steps, width, TILE), BF16, ANYWHERE)] * len(orders),
            [
                pltpu.VMEM((tokens, width), BF16),
                pltpu.VMEM((width, TILE), BF16),
                pltpu.VMEM((len(orders), steps, width, TILE), BF16),
                pltpu.SemaphoreType.DMA((len(pieces),)),
                pltpu.SemaphoreType.DMA((len(orders), steps)),
            ],
        )

    def shrink(self, pairs):
        tiles, rows, _ = pairs[0][0].shape
        width, hidden = self.width, self.hidden
        count = len(pairs)
        full = hidden // TILE
        lead = 2 * TILE

        def body(scalars, ins, outs, scratch):
            values, weights, acc, value_sems, weight_sems = scratch

            def loads(index, size):
                found = []
                for pair in range(count):
                    at = pl.multiple_of((pair * tiles + index) * TILE, TILE)
                    found.append(
                        pltpu.make_async_copy(
                            ins[2 * pair].at[index],
                            values.at[:, pl.ds(at, TILE)],
                            value_sems.at[index, pair],
                        )
                    )
                    found.append(
                        pltpu.make_async_copy(
                            ins[2 * pair + 1].at[pl.ds(pl.multiple_of(index * TILE, TILE), size)],
                            weights.at[pl.ds(at, size)],
                            weight_sems.at[index, pair],
                        )
                    )
                return found

            def begin(index):
                for copy in loads(index, TILE):
                    copy.start()

            each(full, begin)
            if full < tiles:
                rest = hidden - full * TILE
                for copy in loads(full, rest):
                    copy.start()
                for pair in range(count):
                    at = (pair * tiles + full) * TILE
                    weights[at + rest : at + TILE] = jnp.zeros((TILE - rest, width), BF16)
            acc[...] = jnp.zeros_like(acc)

            def add(index):
                for pair in range(count):
                    at = pl.ds(pl.multiple_of((pair * tiles + index) * TILE, TILE), TILE)
                    acc[...] += dot(values[:, at], weights[at, :lead])

            def one(index):
                for copy in loads(index, TILE):
                    copy.wait()
                add(index)

            each(full, one)
            if full < tiles:
                for copy in loads(full, hidden - full * TILE):
                    copy.wait()
                add(full)

            def put(value, at):
                for side in range(2):
                    outs[0][side, :, at] = value[side * (rows // 2) : (side + 1) * (rows // 2)].astype(BF16)

            put(acc, slice(0, lead))

            def wide(number):
                at = pl.ds(pl.multiple_of(lead + number * TILE, TILE), TILE)
                put(dot(values[...], weights[:, at]), at)

            each((width - lead) // TILE, wide)

        ins = []
        for value, weight in pairs:
            ins += [(value, ANYWHERE), (weight, ANYWHERE)]
        return self.chain.run(
            body,
            "ffn_shrink",
            (1,),
            ins,
            [((2, rows // 2, width), BF16, whole(2, rows // 2, width))],
            [
                pltpu.VMEM((rows, count * tiles * TILE), BF16),
                pltpu.VMEM((count * tiles * TILE, width), BF16),
                pltpu.VMEM((rows, lead), F32),
                pltpu.SemaphoreType.DMA((tiles, count)),
                pltpu.SemaphoreType.DMA((tiles, count)),
            ],
        )[0]

    def middle(self, hidden, own, gots, grad, small):
        half, width = self.half, self.width
        step = 128
        count = half // step
        rows = self.micro * half

        def body(scalars, ins, outs, scratch):
            state_ref, own_ref, *got_refs, grad_ref, small_ref = ins
            per = rows // step // len(gots)
            for index, ref in enumerate(got_refs):

                @pl.when(pl.program_id(0) // per == index)
                def _():
                    outs[0][...] = own_ref[...].astype(F32) + ref[...].astype(F32)

            incoming = outs[0][...]
            unit, inverse = unit_rows(state_ref[...])
            back = grad_ref[...].astype(F32) + norm_back(incoming, unit, inverse, self.gain_of(small_ref, 1))
            outs[0][...] = back
            outs[1][0] = back.astype(BF16)
            outs[1][1] = back.astype(BF16)
            part = jnp.sum(incoming * unit, axis=0, keepdims=True)

            @pl.when(pl.program_id(0) == 0)
            def _():
                outs[2][...] = part

            @pl.when(pl.program_id(0) > 0)
            def _():
                outs[2][...] += part

        block = pl.BlockSpec((step, width), lambda j, *_: (j, 0))
        return self.chain.run(
            body,
            "norm_two_back",
            (rows // step,),
            [
                (hidden, block),
                (own, block),
            ]
            + [
                (
                    got,
                    pl.BlockSpec(
                        (step, width),
                        lambda j, *_, index=index: (
                            jnp.clip(j - index * (rows // step // len(gots)), 0, rows // step // len(gots) - 1),
                            0,
                        ),
                    ),
                )
                for index, got in enumerate(gots)
            ]
            + [
                (
                    self.halves(grad),
                    pl.BlockSpec(
                        (None, None, step, width),
                        lambda j, place, *_: (j // count, place[0], j % count, 0),
                    ),
                ),
                (small, whole(1, small.shape[1])),
            ],
            [
                ((rows, width), F32, block),
                ((2, rows, width), BF16, pl.BlockSpec((2, step, width), lambda j, *_: (0, j, 0))),
                ((1, width), F32, whole(1, width)),
            ],
        )

    def back(self, front, segments, both, wo):
        seq_len, width, cols, half = self.seq_len, self.width, self.cols, self.half

        def body(scalars, ins, outs, scratch):
            q_ref, k_ref, v_ref, cos_ref, sin_ref, seg_ref, both_ref, wo_ref = ins
            dq_out, dkv_out = outs
            grad_all, dk_all, dv_all = scratch
            row = pl.program_id(0)
            length = scalars[1][row]
            for side in range(2):
                grad_all[side * half : (side + 1) * half, :] = outer_back(
                    both_ref[side], wo_ref[...]
                ).astype(BF16)
            seg_row = seg_ref[pl.ds(row, 1), :].astype(F32)
            dk_all[...] = jnp.zeros_like(dk_all)
            dv_all[...] = jnp.zeros_like(dv_all)
            for part in (0, 1):
                at = part * half
                keys = at + half
                allowed = allowed_pairs(seg_row, length, at, half, keys)
                key, value = k_ref[:keys], v_ref[:keys]
                for head in range(cols // HD):
                    span = slice(head * HD, (head + 1) * HD)
                    query = q_ref[at:keys, span]
                    grad = grad_all[at:keys, span]
                    weights = softmax_block(query, key, allowed)
                    weight_grad = outer_back(grad, value)
                    delta = jnp.sum(weights * weight_grad, axis=1, keepdims=True)
                    score_grad = (weights * (weight_grad - delta)).astype(BF16)
                    dq = dot(score_grad, key) * (HD**-0.5)
                    dq_out[at:keys, span] = unrotate(dq, cos_ref[at:keys], sin_ref[at:keys]).astype(BF16)
                    dk_all[:keys] += inner(score_grad, query)
                    dv_all[:keys] += inner(weights.astype(BF16), grad)
            for side in range(2):
                dkv_out[side, :, :HD] = (dk_all[...] * (HD**-0.5)).astype(BF16)
                dkv_out[side, :, HD:] = dv_all[...].astype(BF16)

        _, query, key, value, cosine, sine = front[:6]
        head = pl.BlockSpec((seq_len, HD), lambda j, *_: (j, 0))
        heads = pl.BlockSpec((seq_len, cols), lambda j, *_: (j, 0))
        return self.chain.run(
            body,
            "attention_back",
            (self.micro,),
            [
                (query, heads),
                (key, head),
                (value, head),
                (cosine, head),
                (sine, head),
                (segments, whole(*segments.shape)),
                (both, pl.BlockSpec((2, half, width), lambda j, *_: (0, j, 0))),
                (wo, whole(cols, width)),
            ],
            [
                ((self.tokens, cols), BF16, heads),
                ((2, self.tokens, 2 * HD), BF16, pl.BlockSpec((2, seq_len, 2 * HD), lambda j, *_: (0, j, 0))),
            ],
            [
                pltpu.VMEM((seq_len, cols), BF16),
                pltpu.VMEM((seq_len, HD), F32),
                pltpu.VMEM((seq_len, HD), F32),
            ],
        )

    def linear_back(self, front, dq, dkv, wq, wk, wv):
        seq_len, width, cols, half = self.seq_len, self.width, self.cols, self.half
        half_dim = HD // 2
        total = cols + HD

        def body(scalars, ins, outs, scratch):
            dq_ref, dkv_ref, cos_ref, sin_ref, wq_ref, wk_ref, wv_ref = ins
            lin_out, bias_out, parts = outs
            small_grad = scratch[0]
            core = scalars[0][0]
            both = dkv_ref[0].astype(F32) + dkv_ref[1].astype(F32)
            key = unrotate(both[:, :HD], cos_ref[...], sin_ref[...])
            value = both[:, HD:]
            low = lax.broadcasted_iota(jnp.int32, key.shape, 1) < half_dim
            first = jnp.where(low, key, pltpu.roll(value, half_dim, 1))
            second = jnp.where(low, pltpu.roll(key, half_dim, 1), value)
            own_kv = jnp.where(core == 0, first, second).astype(BF16)
            small_grad[...] = own_kv
            lin_out[:, :cols] = dq_ref[...]
            lin_out[:, cols:] = own_kv

            @pl.when(pl.program_id(0) == 0)
            def _():
                bias_out[...] = jnp.zeros_like(bias_out)

            bias_out[:, :cols] += jnp.sum(dq_ref[...].astype(F32), axis=0, keepdims=True)
            bias_out[:, cols:] += jnp.sum(own_kv.astype(F32), axis=0, keepdims=True)
            weight = jnp.concatenate([wk_ref[...], wv_ref[...]], axis=0)
            for side in range(2):
                span = slice(side * half, (side + 1) * half)
                piece = outer_back(dq_ref[span, :], wq_ref[...]) + dot(small_grad[span, :], weight)
                parts[side] = piece.astype(BF16)

        kv_rows = wk.shape[0]
        head = pl.BlockSpec((seq_len, HD), lambda j, *_: (j, 0))
        return self.chain.run(
            body,
            "linear_back",
            (self.micro,),
            [
                (dq, pl.BlockSpec((seq_len, cols), lambda j, *_: (j, 0))),
                (dkv, pl.BlockSpec((2, seq_len, 2 * HD), lambda j, *_: (0, j, 0))),
                (front[4], head),
                (front[5], head),
                (wq, whole(width, cols)),
                (wk, whole(kv_rows, width)),
                (wv, whole(kv_rows, width)),
            ],
            [
                ((self.tokens, total), BF16, pl.BlockSpec((seq_len, total), lambda j, *_: (j, 0))),
                ((1, total), F32, whole(1, total)),
                (
                    (2, self.micro * half, width),
                    BF16,
                    pl.BlockSpec((2, half, width), lambda j, *_: (0, j, 0)),
                ),
            ],
            [pltpu.VMEM((seq_len, HD), BF16)],
        )

    def last(self, inputs, own, got, hidden_grad, small):
        half, width = self.half, self.width
        step = 128
        count = half // step
        rows = self.micro * half

        def body(scalars, ins, outs, scratch):
            x_ref, own_ref, got_ref, grad_ref, small_ref = ins
            incoming = own_ref[...].astype(F32) + got_ref[...].astype(F32)
            unit, inverse = unit_rows(x_ref[...].astype(F32))
            back = grad_ref[...] + norm_back(incoming, unit, inverse, self.gain_of(small_ref, 0))
            outs[0][...] = back.astype(BF16)
            part = jnp.sum(incoming * unit, axis=0, keepdims=True)

            @pl.when(pl.program_id(0) == 0)
            def _():
                outs[1][...] = part

            @pl.when(pl.program_id(0) > 0)
            def _():
                outs[1][...] += part

        block = pl.BlockSpec((step, width), lambda j, *_: (j, 0))
        return self.chain.run(
            body,
            "norm_one_back",
            (rows // step,),
            [
                (
                    self.halves(inputs),
                    pl.BlockSpec(
                        (None, None, step, width),
                        lambda j, place, *_: (j // count, place[0], j % count, 0),
                    ),
                ),
                (own, block),
                (got, block),
                (hidden_grad, block),
                (small, whole(1, small.shape[1])),
            ],
            [((rows, width), BF16, block), ((1, width), F32, whole(1, width))],
        )

    def result(self, state, own, got):
        rows, width = state.shape
        step = 128
        block = pl.BlockSpec((step, width), lambda j, *_: (j, 0))

        def body(scalars, ins, outs, scratch):
            value = ins[0][...] + ins[1][...].astype(F32) + ins[2][...].astype(F32)
            outs[0][...] = value.astype(BF16)

        return self.chain.run(
            body,
            "result",
            (rows // step,),
            [(state, block), (own, block), (got, block)],
            [((rows, width), BF16, block)],
        )[0]


class Halving:
    def __init__(self, chain, left, right, masks, cols, columns=None, at=0, direct=False):
        self.chain, self.left, self.right, self.masks, self.cols = chain, left, right, masks, cols
        total = left.shape[1]
        levels = len(masks)
        self.sizes = [total >> (level + 1) for level in range(levels)] + [total >> levels]
        self.starts = [total - (total >> level) for level in range(levels + 1)]
        self.parts = []
        self.columns = right.shape[2] if columns is None else columns
        self.at = at
        self.direct = direct
        self.level = 0
        self.received = []
        self.result = None

    def product(self, first, last, into=()):
        parts, _, span = self.left.shape
        tiles, tokens, tile = self.right.shape
        sizes = self.sizes[first:last]
        offset = self.starts[first]
        rows = sum(sizes)
        column, columns = self.at, self.columns

        def body(scalars, refs, outs, scratch):
            left, right, made, left_sems, in_sems, out_sems = scratch
            lefts = copies(
                [
                    (refs[0].at[part, pl.ds(offset, rows)], left.at[:, pl.ds(part * span, span)])
                    for part in range(parts)
                ],
                left_sems,
            )

            def load(index):
                return pltpu.make_async_copy(refs[1].at[index], right.at[index], in_sems.at[index])

            def stores(index):
                at = 0
                found = []
                for number, size in enumerate(sizes):
                    found.append(
                        pltpu.make_async_copy(
                            made.at[index, pl.ds(at, size)],
                            outs[number].at[index, :, pl.ds(column, tile)],
                            out_sems.at[index, number],
                        )
                    )
                    at += size
                return found

            each(tiles, lambda index: load(index).start())
            for copy in lefts:
                copy.wait()

            def one(index):
                load(index).wait()

                made[index] = dot(left[...], right[index]).astype(BF16)
                for store in stores(index):
                    store.start()

            each(tiles, one)

            def end(index):
                for store in stores(index):
                    store.wait()

            each(tiles, end)

        self.parts += self.chain.run(
            body,
            "gradient_product",
            (1,),
            [(self.left, ANYWHERE), (self.right, ANYWHERE)],
            [((tiles, size, columns), BF16, ANYWHERE) for size in sizes],
            [
                pltpu.VMEM((rows, tokens), BF16),
                pltpu.VMEM((tiles, tokens, tile), BF16),
                pltpu.VMEM((tiles, rows, tile), BF16),
                pltpu.SemaphoreType.DMA((parts,)),
                pltpu.SemaphoreType.DMA((tiles,)),
                pltpu.SemaphoreType.DMA((tiles, len(sizes))),
            ],
            into=into,
        )
        return self

    def send(self):
        if self.level == len(self.masks):
            return self
        if self.direct and self.level == len(self.masks) - 2:
            return self.send_direct()
        value = self.parts[self.level]
        if self.received:
            tiles, size, tile = value.shape
            start = self.starts[self.level]
            ins = [(value, whole(tiles, size, tile))]
            for piece, base in self.received:
                at = (start - base) // size
                ins.append((piece, pl.BlockSpec((tiles, size, tile), lambda *_, at=at: (0, at, 0))))

            def body(scalars, refs, outs, scratch):
                def one(index):
                    total = refs[0][index].astype(F32)
                    for ref in refs[1:]:
                        total = total + ref[index].astype(F32)
                    outs[0][index] = total.astype(BF16)

                each(tiles, one)

            (value,) = self.chain.run(
                body, "gradient_add", (1,), ins, [((tiles, size, tile), BF16, whole(tiles, size, tile))]
            )
        after = self.starts[self.level + 1]
        self.received.append((swap(value, "wide", self.masks[self.level]), after))
        self.level += 1
        return self

    def send_direct(self):
        first, second = self.masks[-2:]
        pair, single = self.parts[self.level], self.parts[self.level + 1]
        tiles, rows, tile = single.shape
        start = self.starts[self.level]
        ins = [(pair, whole(tiles, 2 * rows, tile)), (single, whole(tiles, rows, tile))]
        for piece, base in self.received:
            for index in range(3):
                at = (start - base) // rows + index
                ins.append((piece, pl.BlockSpec((tiles, rows, tile), lambda *_, at=at: (0, at, 0))))

        def body(scalars, refs, outs, scratch):
            def one(index):
                for block in range(3):
                    if block < 2:
                        total = refs[0][index, block * rows : (block + 1) * rows].astype(F32)
                    else:
                        total = refs[1][index].astype(F32)
                    for ref in refs[2 + block :: 3]:
                        total = total + ref[index].astype(F32)
                    outs[block][index] = total.astype(BF16)

            each(tiles, one)

        shape = (tiles, rows, tile)
        values = self.chain.run(body, "gradient_add", (1,), ins, [(shape, BF16, whole(*shape))] * 3)
        for value, mask in zip(values, (first ^ second, first, second)):
            self.received.append((swap(value, "wide", mask), self.starts[-1]))
        self.level = len(self.masks)
        return self

    def total(self):
        if self.result is not None:
            return self.result
        while self.level < len(self.masks):
            self.send()
        rows, start = self.sizes[-1], self.starts[-1]
        tiles, tile = self.right.shape[0], self.columns
        cols = self.cols
        ins = [(self.parts[-1], whole(tiles, rows, tile))]
        for piece, base in self.received:
            at = (start - base) // rows
            ins.append((piece, pl.BlockSpec((tiles, rows, tile), lambda *_, at=at: (0, at, 0))))

        def body(scalars, refs, outs, scratch):
            for index in range(tiles):
                value = refs[0][index].astype(F32)
                for ref in refs[1:]:
                    value = value + ref[index].astype(F32)
                size = min(tile, cols - index * tile)
                outs[0][:, index * tile : index * tile + size] = value[:, :size]

        (self.result,) = self.chain.run(
            body, "gradient_total", (1,), ins, [((rows, cols), F32, whole(rows, cols))]
        )
        return self.result


def doubling_sum(value, axis, masks):
    for mask in masks:
        value = value + swap(value, axis, mask)
    return value


def body(
    inputs,
    out_grad,
    norm_gain,
    query_weight,
    query_bias,
    key_weight,
    key_bias,
    value_weight,
    value_bias,
    output_weight,
    ffn_gain,
    gate_weight,
    up_weight,
    down_weight,
    lengths,
    segments,
    positions,
):
    micro, seq_len, width = inputs.shape
    cols = query_weight.shape[1]
    hidden_units = gate_weight.shape[1]
    layer = Layer(inputs, cols, hidden_units)
    half, tokens = layer.half, layer.tokens
    place = jnp.stack([layer.core, lax.axis_index("wide")]).astype(jnp.int32)
    chain = Chain([place, lengths])
    layer.chain = chain
    wide_masks = masks_of("wide")
    down_masks, up_masks, gate_masks, joint_masks = [
        [wide_masks[int(place)] for place in places] + wide_masks[3:] for places in MASKS.split()
    ]
    key_rows, value_rows = key_weight.T, value_weight.T
    gate_rows, up_rows = gate_weight.T, up_weight.T
    small = jnp.concatenate([norm_gain, ffn_gain, query_bias, key_bias, value_bias]).astype(F32)[None]
    small_oth = swap(small, "narrow", 1)
    kv = (key_rows, value_rows, swap(key_rows, "narrow", 1), swap(value_rows, "narrow", 1))
    grad_flat = out_grad.reshape(tokens, width)
    halves_grad = layer.halves(out_grad)
    front = layer.front(inputs, small, small_oth, query_weight, kv, segments, positions, output_weight)
    pair = (front[6], swap(front[7], "narrow", 1))
    one_own, one_got = layer.to_other_chip(pair, sizes=(micro * half,))
    mixed = front[0]
    (grad_turned,) = layer.turn(
        [
            (
                halves_grad,
                pl.BlockSpec((None, None, TILE, width), lambda j, *_: (j % micro, j // micro, 0, 0)),
            )
        ],
        (block_order(down_masks),),
    )
    act_grad = layer.act_grad(out_grad, down_weight)
    (one_turned,) = layer.turn(
        [(inputs.reshape(tokens, width), pl.BlockSpec((TILE, width), lambda j, *_: (j, 0)))], (block_order(joint_masks),), small
    )
    state, normed = layer.hidden_state(inputs, small, one_own, one_got)
    normed = [normed, swap(normed, "narrow", 1)]
    act, dgate, dup = layer.expand(normed, gate_rows, up_rows, act_grad)
    levels = len(wide_masks)
    lin_cols = cols + HD
    made = {}
    down = Halving(chain, grad_turned, act, down_masks, hidden_units, direct="d" in DIRECT)

    def turn_two():
        made["two"] = layer.turn_pieces(normed, (block_order(gate_masks), block_order(up_masks)))

    def up_product():
        made["up"] = Halving(chain, made["two"][1], dup, up_masks, hidden_units, direct="u" in DIRECT).product(0, levels + 1)
        made["up"].send()

    def gate_product():
        made["gate"] = Halving(chain, made["two"][0], dgate, gate_masks, hidden_units, direct="g" in DIRECT).product(0, levels + 1)
        made["gate"].send()

    def shrink_two():
        made["two_sum"] = layer.across(layer.shrink([(dgate, gate_rows), (dup, up_rows)]))

    def shrink_ffn():
        made["ffn"] = layer.shrink([(act, down_weight)])

    def across_ffn():
        made["ffn_sum"] = layer.across(made["ffn"])

    def middle():
        made["hidden_grad"], branch, made["ffn_gain"] = layer.middle(state, *made["two_sum"], out_grad, small)
        made["branch"] = pair_exchange(branch)

    def back():
        made["dq"], made["dkv"] = layer.back(front, segments, made["branch"], output_weight)

    def linear():
        made["lin_grad"], made["bias"], parts = layer.linear_back(
            front, made["dq"], pair_exchange(made["dkv"]), query_weight, key_rows, value_rows
        )
        made["one_sum"] = layer.across(parts)

    def linear_product():
        right = made["lin_grad"][None]
        made["lin"] = Halving(chain, one_turned, right, joint_masks, lin_cols + cols, lin_cols + cols)
        made["lin"].product(0, levels + 1)

    def turn_branch():
        (made["branch_turned"],) = layer.turn_pieces([made["branch"].reshape(tokens, width)], (block_order(joint_masks),))

    def output_product():
        right = mixed.reshape(1, tokens, cols)
        both = lin_cols + cols
        made["joint"] = Halving(chain, made["branch_turned"], right, joint_masks, both, both, lin_cols, "l" in DIRECT)
        made["joint"].product(0, levels + 1, tuple(made["lin"].parts)).send()

    def result():
        own = layer.result(state, made["ffn_sum"][0], made["ffn_sum"][1][0])
        made["result"] = (own, swap(own, "narrow", 1))

    def last():
        own, made["norm_gain"] = layer.last(
            inputs, made["one_sum"][0], made["one_sum"][1][0], made["hidden_grad"], small
        )
        made["input"] = (own, swap(own, "narrow", 1))

    def pack():
        packed = share_wide(made["small"] + chain.token[:1, :1])
        made["packed"] = (packed, packed[0, cols + HD :])

    def pair_gains():
        gains = jnp.concatenate([made["norm_gain"], made["ffn_gain"]], axis=1)
        both = pair_exchange(jnp.broadcast_to(gains, (2, 2 * width)))
        small = jnp.concatenate([made["bias"], (both[0] + both[1])[None]], axis=1)
        (made["small"],) = chain.hold(small)

    def total(name):
        made[name + "_out"] = made[name].total()

    made["down"] = down
    steps = {
        "pk": pack,
        "gp": pair_gains,
        "pd1": lambda: down.product(0, 1).send(),
        "pdr": lambda: down.product(1, levels + 1),
        "tn": turn_two,
        "pu": up_product,
        "pg": gate_product,
        "s2": shrink_two,
        "sF": shrink_ffn,
        "xF": across_ffn,
        "mid": middle,
        "bk": back,
        "ln": linear,
        "plo": linear_product,
        "ta": turn_branch,
        "pout": output_product,
        "res": result,
        "last": last,
        "jr": lambda: made.update(result_out=layer.join(*made["result"])),
        "ji": lambda: made.update(input_out=layer.join(*made["input"])),
        "ad": lambda: down.send(),
        "au": lambda: made["up"].send(),
        "ag": lambda: made["gate"].send(),
        "al": lambda: made["joint"].send(),
        "td": lambda: total("down"),
        "tu": lambda: total("up"),
        "tg": lambda: total("gate"),
        "tl": lambda: total("joint"),
    }
    for name in " ".join(ORDER).split():
        if name.startswith("c"):
            chain.scale = 1e8 * int(name[1:])
        else:
            steps[name]()
    result, input_grad = made["result_out"], made["input_out"]
    down_out, up_out, gate_out = made["down_out"], made["up_out"], made["gate_out"]
    lin_out, output_out = made["joint_out"][:, :lin_cols], made["joint_out"][:, lin_cols:]
    packed, gain_out = made["packed"]
    part = HD // 2
    query_out, key_out, value_out = jnp.split(lin_out, [cols, cols + part], axis=1)
    query_bias_out, key_bias_out, value_bias_out, _ = jnp.split(
        packed[0], [cols, cols + part, cols + 2 * part]
    )
    norm_gain_out, ffn_gain_out = gain_out[:width], gain_out[width:]
    return (
        result,
        input_grad,
        norm_gain_out,
        query_out,
        query_bias_out,
        key_out,
        key_bias_out,
        value_out,
        value_bias_out,
        output_out.T,
        ffn_gain_out,
        gate_out,
        up_out,
        down_out.T,
    )


def solution(mesh):
    placed = (
        P("wide", None, None),
        P("wide", None, None),
        P(),
        P(None, "narrow"),
        P("narrow"),
        P(None, "narrow"),
        P("narrow"),
        P(None, "narrow"),
        P("narrow"),
        P("narrow", None),
        P(),
        P(None, "narrow"),
        P(None, "narrow"),
        P("narrow", None),
        P("wide"),
        P("wide", None),
        P("wide", None),
    )
    return jax.shard_map(
        body,
        mesh=mesh,
        in_specs=placed,
        out_specs=(
            P("wide", None, None),
            P("wide", None, None),
            P(),
            P("wide", "narrow"),
            P("narrow"),
            P("wide", "narrow"),
            P("narrow"),
            P("wide", "narrow"),
            P("narrow"),
            P("narrow", "wide"),
            P(),
            P("wide", "narrow"),
            P("wide", "narrow"),
            P("narrow", "wide"),
        ),
        check_vma=False,
    )
```

```python
import functools

import jax
import jax.numpy as jnp
from jax import lax
from jax.experimental import pallas as pl
from jax.experimental.pallas import tpu as pltpu
from jax.sharding import PartitionSpec as P

HD = 128


NORM_EPS = 1e-06
ROPE_BASE = 10000.0
NEG_FILL = -1e30
F32 = jnp.float32
BF16 = jnp.bfloat16
TILE = 256
VMEM_LIMIT = 64 << 20
ORDER = (
    "pd1 tn pu s2",
    "pg pdr sF mid",
    "ad au xF bk",
    "ad ln plo c4",
    "ag ta pout td",
    "au res last ag",
    "jr al ji al",
    "tu gp tg tl",
    "pk",
)
MASKS = "012 102 012 012"
DIRECT = ""


def swap(value, axis, mask):
    pairs = [(source, source ^ mask) for source in range(lax.axis_size(axis))]
    return lax.ppermute(value, axis, pairs)


def pair_exchange(value):
    size = lax.axis_size("narrow")
    pairs = [[first, first + 1] for first in range(0, size, 2)]
    return lax.all_to_all(value, "narrow", 0, 0, axis_index_groups=pairs, tiled=True)


def share_wide(value):
    count = lax.axis_size("wide")
    spread = jnp.broadcast_to(value, (count,) + value.shape[1:])
    return jnp.sum(lax.all_to_all(spread, "wide", 0, 0, tiled=True), axis=0, keepdims=True)


def swap_pieces(value, mask, count):
    return [swap(piece, "narrow", mask) for piece in jnp.split(value, count, axis=0)]


def swap_in_turn(value, axis, mask, sizes):
    if len(sizes) == 1:
        return swap(value, axis, mask)
    arrived = []
    last = 0
    for size in sizes:
        first, last = last, last + size
        piece = value[first:last]
        if arrived:
            arrived[-1], piece = lax.optimization_barrier((arrived[-1], piece))
        arrived.append(swap(piece, axis, mask))
    return jnp.concatenate(arrived, axis=0)


def masks_of(axis):
    return [1 << bit for bit in range(lax.axis_size(axis).bit_length() - 1)]


def block_order(masks):
    order = [0]
    for mask in reversed(masks):
        order = [mask ^ block for block in order] + order
    return order


def dot(left, right):
    return jnp.dot(left, right, preferred_element_type=F32)


def outer_back(left, right):
    return lax.dot_general(left, right, (((1,), (1,)), ((), ())), preferred_element_type=F32)


def inner(left, right):
    return lax.dot_general(left, right, (((0,), (0,)), ((), ())), preferred_element_type=F32)


def whole(*shape):
    return pl.BlockSpec(shape, lambda *_: (0,) * len(shape))


ANYWHERE = pl.BlockSpec(memory_space=pl.ANY)


TIMES = {
    "attention_back": 13,
    "linear_back": 7,
    "ffn_shrink": 13,
    "gradient_product": 8,
    "turn_pieces": 6,
    "norm_two_back": 8,
    "norm_one_back": 6,
    "gradient_add": 4,
    "gradient_total": 4,
    "result": 5,
    "join_tokens": 4,
}


class Chain:
    def __init__(self, scalars):
        self.scalars = scalars
        self.token = None
        self.scale = 0.0

    def hold(self, *values):
        self.token, *held = lax.optimization_barrier((self.token, *values))
        return held

    def run(self, body, name, grid, ins, outs, scratch=(), into=(), after=(), flops=1):
        extra = list(into) + ([] if self.token is None else [self.token]) + list(after)
        count, given, made = len(self.scalars), len(ins), len(outs)

        def kernel(*refs):
            scalars = refs[:count]
            used = refs[count : count + given]
            results = refs[count + given + len(extra) :]
            results[made][...] = jnp.zeros_like(results[made])
            body(scalars, used, results[:made], results[made + 1 :])

        results = pl.pallas_call(
            kernel,
            out_shape=[jax.ShapeDtypeStruct(shape, dtype) for shape, dtype, _ in outs]
            + [jax.ShapeDtypeStruct((8, 128), F32)],
            grid_spec=pltpu.PrefetchScalarGridSpec(
                num_scalar_prefetch=count,
                grid=grid,
                in_specs=[spec for _, spec in ins] + [ANYWHERE] * len(extra),
                out_specs=[spec for _, _, spec in outs] + [whole(8, 128)],
                scratch_shapes=list(scratch),
            ),
            input_output_aliases={count + given + index: index for index in range(len(into))},
            compiler_params=pltpu.CompilerParams(
                dimension_semantics=("arbitrary",) * len(grid), vmem_limit_bytes=VMEM_LIMIT
            ),
            cost_estimate=pl.CostEstimate(
                flops=int(self.scale * TIMES.get(name, 5)) + 1, bytes_accessed=1, transcendentals=0
            ),
            name=name,
        )(*self.scalars, *[array for array, _ in ins], *extra)
        self.token = results[-1]
        return results[:-1]


def copies(pairs, sems):
    started = []
    for index, (source, target) in enumerate(pairs):
        copy = pltpu.make_async_copy(source, target, sems.at[index])
        copy.start()
        started.append(copy)
    return started


class Tiles:
    def __init__(self, source, target, sems, total, tile):
        self.source, self.target, self.sems, self.tile = source, target, sems, tile
        self.full, self.rest = divmod(total, tile)

    def make(self, index, size):
        at = pl.multiple_of(index * self.tile, self.tile)
        return pltpu.make_async_copy(
            self.source.at[pl.ds(at, size)], self.target.at[index, pl.ds(0, size)], self.sems.at[index]
        )

    def start(self):
        for index in range(self.full):
            self.make(index, self.tile).start()
        if self.rest:
            self.make(self.full, self.rest).start()

    def wait(self, index):
        if not self.rest:
            self.make(index, self.tile).wait()
            return

        @pl.when(index < self.full)
        def _():
            self.make(index, self.tile).wait()

        @pl.when(index == self.full)
        def _():
            self.make(self.full, self.rest).wait()


def each(count, body):
    def run(index, carry):
        body(index)
        return carry

    lax.fori_loop(0, count, run, 0)


def unit_rows(values):
    inverse = lax.rsqrt(jnp.mean(values * values, axis=-1, keepdims=True) + NORM_EPS)
    return values * inverse, inverse


def norm_back(grad, unit, inverse, gain):
    grown = grad * gain
    return inverse * (grown - unit * jnp.mean(grown * unit, axis=-1, keepdims=True))


def rotate(values, cosine, sine):
    return values * cosine + pltpu.roll(values, HD // 2, 1) * sine


def unrotate(grads, cosine, sine):
    return grads * cosine + pltpu.roll(grads * sine, HD // 2, 1)


def down_rows(row, count):
    return jnp.broadcast_to(row, (128, count)).T


def allowed_pairs(seg_row, length, first, count, keys):
    turned = down_rows(seg_row[:, first : first + count], count)
    own = jnp.concatenate([turned] * (keys // 128), axis=1)
    rows = lax.broadcasted_iota(jnp.int32, (count, keys), 0) + first
    cols = lax.broadcasted_iota(jnp.int32, (count, keys), 1)
    same = own == jnp.broadcast_to(seg_row[:, :keys], (count, keys))
    return same & (cols <= rows) & ((cols < length) | (cols == rows))


def softmax_block(query, keys, allowed):
    scores = jnp.where(allowed, outer_back(query, keys) * (HD**-0.5), NEG_FILL)
    top = jnp.max(scores, axis=1, keepdims=True)
    grown = jnp.exp(scores - top)
    return grown * (1.0 / jnp.sum(grown, axis=1, keepdims=True))


class Layer:
    def __init__(self, inputs, cols, hidden):
        self.micro, self.seq_len, self.width = inputs.shape
        self.half = self.seq_len // 2
        self.tokens = self.micro * self.seq_len
        self.cols = cols
        self.hidden = hidden
        self.core = lax.axis_index("narrow") % 2
        self.even = self.core == 0
        self.narrow_masks = masks_of("narrow")
        self.chain = None

    def gain_of(self, small_ref, index):
        return small_ref[:, index * self.width : (index + 1) * self.width]

    def halves(self, value):
        return value.reshape(self.micro, 2, self.half, self.width)

    def across(self, parts, count=1, sizes=None):
        return self.to_other_chip(pair_exchange(parts), count, sizes)

    def to_other_chip(self, got, count=1, sizes=None):
        total = (got[0].astype(F32) + got[1].astype(F32)).astype(BF16)
        for mask in self.narrow_masks[1:-1]:
            total = (total.astype(F32) + swap(total, "narrow", mask).astype(F32)).astype(BF16)
        (total,) = self.chain.hold(total)
        if sizes is not None:
            return total, swap_in_turn(total, "narrow", self.narrow_masks[-1], sizes)
        return total, swap_pieces(total, self.narrow_masks[-1], count)

    def join(self, own, other):
        half, width, seq_len = self.half, self.width, self.seq_len
        block = pl.BlockSpec((half, width), lambda j, *_: (j, 0))

        def body(scalars, ins, outs, scratch):
            core = scalars[0][0]
            outs[0][pl.ds(pl.multiple_of(core * half, half), half), :] = ins[0][...]
            outs[0][pl.ds(pl.multiple_of((1 - core) * half, half), half), :] = ins[1][...]

        return self.chain.run(
            body,
            "join_tokens",
            (self.micro,),
            [(own, block), (other, block)],
            [
                (
                    (self.micro, seq_len, width),
                    BF16,
                    pl.BlockSpec((None, seq_len, width), lambda j, *_: (j, 0, 0)),
                )
            ],
        )[0]

    def front(self, inputs, small, small_oth, wq, kv, segments, positions, wo):
        seq_len, width, cols, half = self.seq_len, self.width, self.cols, self.half
        bias_at = 2 * width
        step = 128
        half_dim = HD // 2

        def body(scalars, ins, outs, scratch):
            x_ref, small_ref, oth_ref, wq_ref, wk_own, wv_own, wk_oth, wv_oth, seg_ref, pos_ref, wo_ref = ins
            mixed_out, q_out, k_out, v_out, cos_out, sin_out, part_own, part_oth = outs
            normed, mixed_all = scratch
            core = scalars[0][0]
            length = scalars[1][pl.program_id(0)]
            even = core == 0
            gain = self.gain_of(small_ref, 0)

            def norm_rows(index, carry):
                span = pl.ds(pl.multiple_of(index * step, step), step)
                unit, _ = unit_rows(x_ref[span, :].astype(F32))
                normed[span, :] = (unit * gain).astype(BF16)
                return carry

            lax.fori_loop(0, seq_len // step, norm_rows, 0)
            lane = lax.broadcasted_iota(jnp.int32, (1, HD), 1)
            exponent = jnp.where(lane < half_dim, lane, lane - half_dim).astype(F32) * (2.0 / HD)
            freq = jnp.exp(exponent * (-jnp.log(F32(ROPE_BASE))))
            place = down_rows(pos_ref[pl.ds(pl.program_id(0), 1), :].astype(F32), seq_len)
            angle = place * freq
            cosine = jnp.cos(angle)
            sine = jnp.where(lane < half_dim, -1.0, 1.0) * jnp.sin(angle)
            cos_out[...] = cosine
            sin_out[...] = sine
            rows = normed[...]
            first_k = jnp.where(even, wk_own[...], wk_oth[...])
            second_k = jnp.where(even, wk_oth[...], wk_own[...])
            first_v = jnp.where(even, wv_own[...], wv_oth[...])
            second_v = jnp.where(even, wv_oth[...], wv_own[...])
            kv = jnp.concatenate([first_k, second_k, first_v, second_v], axis=0)
            lin = outer_back(rows, kv)
            own_bias = small_ref[:, bias_at + cols : bias_at + cols + HD]
            oth_bias = oth_ref[:, bias_at + cols : bias_at + cols + HD]
            left = jnp.where(even, own_bias, oth_bias)
            right = jnp.where(even, oth_bias, own_bias)
            key_bias = jnp.where(lane < half_dim, left, pltpu.roll(right, half_dim, 1))
            value_bias = jnp.where(lane < half_dim, pltpu.roll(left, half_dim, 1), right)
            key = rotate(lin[:, :HD] + key_bias, cosine, sine).astype(BF16)
            value = (lin[:, HD:] + value_bias).astype(BF16)
            k_out[...] = key
            v_out[...] = value
            query_lin = dot(rows, wq_ref[...]) + small_ref[:, bias_at : bias_at + cols]
            seg_row = seg_ref[pl.ds(pl.program_id(0), 1), :].astype(F32)
            masks = [allowed_pairs(seg_row, length, at, half, at + half) for at in (0, half)]
            for head in range(cols // HD):
                span = slice(head * HD, (head + 1) * HD)
                query = rotate(query_lin[:, span], cosine, sine).astype(BF16)
                q_out[:, span] = query
                for part, allowed in enumerate(masks):
                    at = part * half
                    keys = at + half
                    weights = softmax_block(query[at:keys], key[:keys], allowed).astype(BF16)
                    mixed_all[at:keys, span] = dot(weights, value[:keys]).astype(BF16)
            for side in range(2):
                mixed_out[side] = mixed_all[side * half : (side + 1) * half, :]
            for side, part in ((core, part_own), (1 - core, part_oth)):
                some = mixed_all[pl.ds(pl.multiple_of(side * half, half), half), :]
                part[...] = dot(some, wo_ref[...]).astype(BF16)

        small_size = small.shape[1]
        kv_rows = kv[0].shape[0]
        return self.chain.run(
            body,
            "attention_front",
            (self.micro,),
            [
                (inputs, pl.BlockSpec((None, seq_len, width), lambda j, *_: (j, 0, 0))),
                (small, whole(1, small_size)),
                (small_oth, whole(1, small_size)),
                (wq, whole(width, cols)),
            ]
            + [(piece, whole(kv_rows, width)) for piece in kv]
            + [
                (segments, whole(*segments.shape)),
                (positions, whole(*positions.shape)),
                (wo, whole(cols, width)),
            ],
            [
                ((2, self.micro * half, cols), BF16, pl.BlockSpec((2, half, cols), lambda j, *_: (0, j, 0))),
                ((self.tokens, cols), BF16, pl.BlockSpec((seq_len, cols), lambda j, *_: (j, 0))),
                ((self.tokens, HD), BF16, pl.BlockSpec((seq_len, HD), lambda j, *_: (j, 0))),
                ((self.tokens, HD), BF16, pl.BlockSpec((seq_len, HD), lambda j, *_: (j, 0))),
                ((self.tokens, HD), F32, pl.BlockSpec((seq_len, HD), lambda j, *_: (j, 0))),
                ((self.tokens, HD), F32, pl.BlockSpec((seq_len, HD), lambda j, *_: (j, 0))),
                ((self.micro * half, width), BF16, pl.BlockSpec((half, width), lambda j, *_: (j, 0))),
                ((self.micro * half, width), BF16, pl.BlockSpec((half, width), lambda j, *_: (j, 0))),
            ],
            [pltpu.VMEM((seq_len, width), BF16), pltpu.VMEM((seq_len, cols), BF16)],
        )

    def act_grad(self, grad, wd):
        tokens, width, half, micro = self.tokens, self.width, self.half, self.micro
        hidden = self.hidden
        tiles = pl.cdiv(hidden, TILE)

        def body(scalars, ins, outs, scratch):
            grad_ref, wd_ref = ins
            rows, weights, made, row_sems, in_sems, out_sems = scratch
            lines = copies(
                [
                    (grad_ref.at[row, side], rows.at[pl.ds((side * micro + row) * half, half)])
                    for side in range(2)
                    for row in range(micro)
                ],
                row_sems,
            )
            loads = Tiles(wd_ref, weights, in_sems, hidden, TILE)
            loads.start()
            for copy in lines:
                copy.wait()

            def store(index):
                return pltpu.make_async_copy(made.at[index], outs[0].at[index], out_sems.at[index])

            def one(index):
                loads.wait(index)
                made[index] = outer_back(rows[...], weights[index]).astype(BF16)
                store(index).start()

            each(tiles, one)
            each(tiles, lambda index: store(index).wait())

        return self.chain.run(
            body,
            "activation_grad",
            (1,),
            [(self.halves(grad), ANYWHERE), (wd, ANYWHERE)],
            [((tiles, tokens, TILE), BF16, ANYWHERE)],
            [
                pltpu.VMEM((tokens, width), BF16),
                pltpu.VMEM((tiles, TILE, width), BF16),
                pltpu.VMEM((tiles, tokens, TILE), BF16),
                pltpu.SemaphoreType.DMA((2 * micro,)),
                pltpu.SemaphoreType.DMA((tiles,)),
                pltpu.SemaphoreType.DMA((tiles,)),
            ],
        )[0]

    def hidden_state(self, inputs, small, own, got):
        half, width = self.half, self.width
        step = 128
        count = half // step
        rows = self.micro * half

        def body(scalars, ins, outs, scratch):
            x_ref, small_ref, own_ref, got_ref = ins
            branch = own_ref[...].astype(F32) + got_ref[...].astype(F32)
            state = x_ref[...].astype(F32) + branch
            outs[0][...] = state
            unit, _ = unit_rows(state)
            outs[1][...] = (unit * self.gain_of(small_ref, 1)).astype(BF16)

        part = pl.BlockSpec((step, width), lambda j, *_: (j, 0))
        return self.chain.run(
            body,
            "hidden_norm",
            (rows // step,),
            [
                (
                    self.halves(inputs),
                    pl.BlockSpec(
                        (None, None, step, width), lambda j, place, *_: (j // count, place[0], j % count, 0)
                    ),
                ),
                (small, whole(1, small.shape[1])),
                (own, part),
                (got, part),
            ],
            [((rows, width), F32, part), ((rows, width), BF16, part)],
        )

    def placed(self, scalars, refs, target):
        core = scalars[0][0]
        rows = refs[0].shape[0]
        if len(refs) == 1:
            return [(refs[0], target)]
        spots = [pl.multiple_of(side * rows, rows) for side in (core, 1 - core)]
        return [(ref, target.at[pl.ds(spot, rows)]) for ref, spot in zip(refs, spots)]

    def expand(self, rows_in, wg, wu, act_grad):
        width, hidden, tokens = self.width, self.hidden, self.tokens
        tiles = pl.cdiv(hidden, TILE)

        def body(scalars, ins, outs, scratch):
            *row_refs, wg_ref, wu_ref, grad_ref = ins
            rows, gates, ups, grads, made, row_sems, gate_sems, up_sems, grad_sems, out_sems = scratch
            sides = copies(self.placed(scalars, row_refs, rows), row_sems)
            first = Tiles(wg_ref, gates, gate_sems, hidden, TILE)
            second = Tiles(wu_ref, ups, up_sems, hidden, TILE)
            first.start()
            second.start()

            def grad_loads(index):
                return [pltpu.make_async_copy(grad_ref.at[index], grads.at[index], grad_sems.at[index])]

            def store(index, kind):
                return pltpu.make_async_copy(
                    made.at[index % 2, kind], outs[kind].at[index], out_sems.at[index % 2, kind]
                )

            def begin(index):
                for copy in grad_loads(index):
                    copy.start()

            each(tiles, begin)
            for copy in sides:
                copy.wait()
            lane = lax.broadcasted_iota(jnp.int32, (1, TILE), 1)

            def one(index):
                first.wait(index)
                second.wait(index)
                for copy in grad_loads(index):
                    copy.wait()

                @pl.when(index >= 2)
                def _():
                    for kind in range(3):
                        store(index - 2, kind).wait()

                def part(number):
                    span = slice(number, tokens)
                    gate = outer_back(rows[span, :], gates[index])
                    upper = outer_back(rows[span, :], ups[index])
                    grad = grads[index, span, :].astype(F32)
                    sig = 0.5 * jnp.tanh(0.5 * gate) + 0.5
                    silu = gate * sig
                    slot = index % 2
                    made[slot, 0, span, :] = (silu * upper).astype(BF16)
                    made[slot, 1, span, :] = (grad * upper * (sig + silu * (1.0 - sig))).astype(BF16)
                    made[slot, 2, span, :] = (grad * silu).astype(BF16)

                part(0)
                if hidden % TILE:

                    @pl.when(index == tiles - 1)
                    def _():
                        slot = (tiles - 1) % 2
                        blank = jnp.zeros((3, tokens, TILE // 2), BF16)
                        spare = lane[:, TILE // 2 :] < hidden % TILE
                        if hidden % TILE <= TILE // 2:
                            made[slot, :, :, TILE // 2 :] = blank
                            spare = lane[:, : TILE // 2] < hidden % TILE
                            made[slot, :, :, : TILE // 2] = jnp.where(
                                spare, made[slot, :, :, : TILE // 2], blank
                            )
                        else:
                            made[slot, :, :, TILE // 2 :] = jnp.where(
                                spare, made[slot, :, :, TILE // 2 :], blank
                            )

                for kind in range(3):
                    store(index, kind).start()

            each(tiles, one)
            for index in range(max(tiles - 2, 0), tiles):
                for kind in range(3):
                    store(index, kind).wait()

        return self.chain.run(
            body,
            "ffn_expand",
            (1,),
            [(piece, ANYWHERE) for piece in rows_in]
            + [(wg, ANYWHERE), (wu, ANYWHERE), (act_grad, ANYWHERE)],
            [((tiles, tokens, TILE), BF16, ANYWHERE)] * 3,
            [
                pltpu.VMEM((tokens, width), BF16),
                pltpu.VMEM((tiles, TILE, width), BF16),
                pltpu.VMEM((tiles, TILE, width), BF16),
                pltpu.VMEM((tiles, tokens, TILE), BF16),
                pltpu.VMEM((2, 3, tokens, TILE), BF16),
                pltpu.SemaphoreType.DMA((len(rows_in),)),
                pltpu.SemaphoreType.DMA((tiles,)),
                pltpu.SemaphoreType.DMA((tiles,)),
                pltpu.SemaphoreType.DMA((tiles,)),
                pltpu.SemaphoreType.DMA((2, 3)),
            ],
        )

    def turn(self, blocks, orders, small=None):
        width = self.width
        arrays = [entry[:2] for entry in blocks]
        steps = self.tokens // TILE
        count = len(orders[0])
        rows = width // count

        def body(scalars, ins, outs, scratch):
            turned = scratch[0]
            if small is not None:
                unit, _ = unit_rows(ins[0][...].astype(F32))
                turned[...] = (unit * self.gain_of(ins[1], 0)).astype(BF16).T
            elif len(ins) == 1:
                turned[...] = ins[0][...].T
            else:
                for index, ref in enumerate(ins):
                    @pl.when((pl.program_id(0) >= blocks[index][2]) & (pl.program_id(0) < blocks[index][3]))
                    def _():
                        turned[...] = ref[...].T
            place = scalars[0][1]
            for order, out in zip(orders, outs):
                for index, block in enumerate(order):
                    source = pl.multiple_of((place ^ block) * rows, rows)
                    out[0, index * rows : (index + 1) * rows, :] = turned[pl.ds(source, rows), :]

        ins = arrays + ([] if small is None else [(small, whole(1, small.shape[1]))])
        return self.chain.run(
            body,
            "turn_blocks",
            (steps,),
            ins,
            [((steps, width, TILE), BF16, pl.BlockSpec((1, width, TILE), lambda j, *_: (j, 0, 0)))] * len(orders),
            [pltpu.VMEM((width, TILE), BF16)],
        )

    def turn_pieces(self, pieces, orders):
        width, tokens = self.width, self.tokens
        steps = tokens // TILE
        count = len(orders[0])
        rows = width // count

        def body(scalars, ins, outs, scratch):
            stacked, turned, made, in_sems, out_sems = scratch
            for copy in copies(self.placed(scalars, ins, stacked), in_sems):
                copy.wait()
            place = scalars[0][1]

            def store(step, number):
                return pltpu.make_async_copy(
                    made.at[number, step], outs[number].at[step], out_sems.at[number, step]
                )

            def one(step):
                turned[...] = stacked[pl.ds(pl.multiple_of(step * TILE, TILE), TILE), :].T
                for number, order in enumerate(orders):
                    for index, block in enumerate(order):
                        source = pl.multiple_of((place ^ block) * rows, rows)
                        made[number, step, index * rows : (index + 1) * rows, :] = turned[
                            pl.ds(source, rows), :
                        ]
                    store(step, number).start()

            each(steps, one)
            for number in range(len(orders)):
                each(steps, lambda step: store(step, number).wait())

        return self.chain.run(
            body,
            "turn_pieces",
            (1,),
            [(piece, ANYWHERE) for piece in pieces],
            [((steps, width, TILE), BF16, ANYWHERE)] * len(orders),
            [
                pltpu.VMEM((tokens, width), BF16),
                pltpu.VMEM((width, TILE), BF16),
                pltpu.VMEM((len(orders), steps, width, TILE), BF16),
                pltpu.SemaphoreType.DMA((len(pieces),)),
                pltpu.SemaphoreType.DMA((len(orders), steps)),
            ],
        )

    def shrink(self, pairs):
        tiles, rows, _ = pairs[0][0].shape
        width, hidden = self.width, self.hidden
        count = len(pairs)
        full = hidden // TILE
        lead = 2 * TILE

        def body(scalars, ins, outs, scratch):
            values, weights, acc, value_sems, weight_sems = scratch

            def loads(index, size):
                found = []
                for pair in range(count):
                    at = pl.multiple_of((pair * tiles + index) * TILE, TILE)
                    found.append(
                        pltpu.make_async_copy(
                            ins[2 * pair].at[index],
                            values.at[:, pl.ds(at, TILE)],
                            value_sems.at[index, pair],
                        )
                    )
                    found.append(
                        pltpu.make_async_copy(
                            ins[2 * pair + 1].at[pl.ds(pl.multiple_of(index * TILE, TILE), size)],
                            weights.at[pl.ds(at, size)],
                            weight_sems.at[index, pair],
                        )
                    )
                return found

            def begin(index):
                for copy in loads(index, TILE):
                    copy.start()

            each(full, begin)
            if full < tiles:
                rest = hidden - full * TILE
                for copy in loads(full, rest):
                    copy.start()
                for pair in range(count):
                    at = (pair * tiles + full) * TILE
                    weights[at + rest : at + TILE] = jnp.zeros((TILE - rest, width), BF16)
            acc[...] = jnp.zeros_like(acc)

            def add(index):
                for pair in range(count):
                    at = pl.ds(pl.multiple_of((pair * tiles + index) * TILE, TILE), TILE)
                    acc[...] += dot(values[:, at], weights[at, :lead])

            def one(index):
                for copy in loads(index, TILE):
                    copy.wait()
                add(index)

            each(full, one)
            if full < tiles:
                for copy in loads(full, hidden - full * TILE):
                    copy.wait()
                add(full)

            def put(value, at):
                for side in range(2):
                    outs[0][side, :, at] = value[side * (rows // 2) : (side + 1) * (rows // 2)].astype(BF16)

            put(acc, slice(0, lead))

            def wide(number):
                at = pl.ds(pl.multiple_of(lead + number * TILE, TILE), TILE)
                put(dot(values[...], weights[:, at]), at)

            each((width - lead) // TILE, wide)

        ins = []
        for value, weight in pairs:
            ins += [(value, ANYWHERE), (weight, ANYWHERE)]
        return self.chain.run(
            body,
            "ffn_shrink",
            (1,),
            ins,
            [((2, rows // 2, width), BF16, whole(2, rows // 2, width))],
            [
                pltpu.VMEM((rows, count * tiles * TILE), BF16),
                pltpu.VMEM((count * tiles * TILE, width), BF16),
                pltpu.VMEM((rows, lead), F32),
                pltpu.SemaphoreType.DMA((tiles, count)),
                pltpu.SemaphoreType.DMA((tiles, count)),
            ],
        )[0]

    def middle(self, hidden, own, gots, grad, small):
        half, width = self.half, self.width
        step = 128
        count = half // step
        rows = self.micro * half

        def body(scalars, ins, outs, scratch):
            state_ref, own_ref, *got_refs, grad_ref, small_ref = ins
            per = rows // step // len(gots)
            for index, ref in enumerate(got_refs):

                @pl.when(pl.program_id(0) // per == index)
                def _():
                    outs[0][...] = own_ref[...].astype(F32) + ref[...].astype(F32)

            incoming = outs[0][...]
            unit, inverse = unit_rows(state_ref[...])
            back = grad_ref[...].astype(F32) + norm_back(incoming, unit, inverse, self.gain_of(small_ref, 1))
            outs[0][...] = back
            outs[1][0] = back.astype(BF16)
            outs[1][1] = back.astype(BF16)
            part = jnp.sum(incoming * unit, axis=0, keepdims=True)

            @pl.when(pl.program_id(0) == 0)
            def _():
                outs[2][...] = part

            @pl.when(pl.program_id(0) > 0)
            def _():
                outs[2][...] += part

        block = pl.BlockSpec((step, width), lambda j, *_: (j, 0))
        return self.chain.run(
            body,
            "norm_two_back",
            (rows // step,),
            [
                (hidden, block),
                (own, block),
            ]
            + [
                (
                    got,
                    pl.BlockSpec(
                        (step, width),
                        lambda j, *_, index=index: (
                            jnp.clip(j - index * (rows // step // len(gots)), 0, rows // step // len(gots) - 1),
                            0,
                        ),
                    ),
                )
                for index, got in enumerate(gots)
            ]
            + [
                (
                    self.halves(grad),
                    pl.BlockSpec(
                        (None, None, step, width),
                        lambda j, place, *_: (j // count, place[0], j % count, 0),
                    ),
                ),
                (small, whole(1, small.shape[1])),
            ],
            [
                ((rows, width), F32, block),
                ((2, rows, width), BF16, pl.BlockSpec((2, step, width), lambda j, *_: (0, j, 0))),
                ((1, width), F32, whole(1, width)),
            ],
        )

    def back(self, front, segments, both, wo):
        seq_len, width, cols, half = self.seq_len, self.width, self.cols, self.half

        def body(scalars, ins, outs, scratch):
            q_ref, k_ref, v_ref, cos_ref, sin_ref, seg_ref, both_ref, wo_ref = ins
            dq_out, dkv_out = outs
            grad_all, dk_all, dv_all = scratch
            row = pl.program_id(0)
            length = scalars[1][row]
            for side in range(2):
                grad_all[side * half : (side + 1) * half, :] = outer_back(
                    both_ref[side], wo_ref[...]
                ).astype(BF16)
            seg_row = seg_ref[pl.ds(row, 1), :].astype(F32)
            dk_all[...] = jnp.zeros_like(dk_all)
            dv_all[...] = jnp.zeros_like(dv_all)
            for part in (0, 1):
                at = part * half
                keys = at + half
                allowed = allowed_pairs(seg_row, length, at, half, keys)
                key, value = k_ref[:keys], v_ref[:keys]
                for head in range(cols // HD):
                    span = slice(head * HD, (head + 1) * HD)
                    query = q_ref[at:keys, span]
                    grad = grad_all[at:keys, span]
                    weights = softmax_block(query, key, allowed)
                    weight_grad = outer_back(grad, value)
                    delta = jnp.sum(weights * weight_grad, axis=1, keepdims=True)
                    score_grad = (weights * (weight_grad - delta)).astype(BF16)
                    dq = dot(score_grad, key) * (HD**-0.5)
                    dq_out[at:keys, span] = unrotate(dq, cos_ref[at:keys], sin_ref[at:keys]).astype(BF16)
                    dk_all[:keys] += inner(score_grad, query)
                    dv_all[:keys] += inner(weights.astype(BF16), grad)
            for side in range(2):
                dkv_out[side, :, :HD] = (dk_all[...] * (HD**-0.5)).astype(BF16)
                dkv_out[side, :, HD:] = dv_all[...].astype(BF16)

        _, query, key, value, cosine, sine = front[:6]
        head = pl.BlockSpec((seq_len, HD), lambda j, *_: (j, 0))
        heads = pl.BlockSpec((seq_len, cols), lambda j, *_: (j, 0))
        return self.chain.run(
            body,
            "attention_back",
            (self.micro,),
            [
                (query, heads),
                (key, head),
                (value, head),
                (cosine, head),
                (sine, head),
                (segments, whole(*segments.shape)),
                (both, pl.BlockSpec((2, half, width), lambda j, *_: (0, j, 0))),
                (wo, whole(cols, width)),
            ],
            [
                ((self.tokens, cols), BF16, heads),
                ((2, self.tokens, 2 * HD), BF16, pl.BlockSpec((2, seq_len, 2 * HD), lambda j, *_: (0, j, 0))),
            ],
            [
                pltpu.VMEM((seq_len, cols), BF16),
                pltpu.VMEM((seq_len, HD), F32),
                pltpu.VMEM((seq_len, HD), F32),
            ],
        )

    def linear_back(self, front, dq, dkv, wq, wk, wv):
        seq_len, width, cols, half = self.seq_len, self.width, self.cols, self.half
        half_dim = HD // 2
        total = cols + HD

        def body(scalars, ins, outs, scratch):
            dq_ref, dkv_ref, cos_ref, sin_ref, wq_ref, wk_ref, wv_ref = ins
            lin_out, bias_out, parts = outs
            small_grad = scratch[0]
            core = scalars[0][0]
            both = dkv_ref[0].astype(F32) + dkv_ref[1].astype(F32)
            key = unrotate(both[:, :HD], cos_ref[...], sin_ref[...])
            value = both[:, HD:]
            low = lax.broadcasted_iota(jnp.int32, key.shape, 1) < half_dim
            first = jnp.where(low, key, pltpu.roll(value, half_dim, 1))
            second = jnp.where(low, pltpu.roll(key, half_dim, 1), value)
            own_kv = jnp.where(core == 0, first, second).astype(BF16)
            small_grad[...] = own_kv
            lin_out[:, :cols] = dq_ref[...]
            lin_out[:, cols:] = own_kv

            @pl.when(pl.program_id(0) == 0)
            def _():
                bias_out[...] = jnp.zeros_like(bias_out)

            bias_out[:, :cols] += jnp.sum(dq_ref[...].astype(F32), axis=0, keepdims=True)
            bias_out[:, cols:] += jnp.sum(own_kv.astype(F32), axis=0, keepdims=True)
            weight = jnp.concatenate([wk_ref[...], wv_ref[...]], axis=0)
            for side in range(2):
                span = slice(side * half, (side + 1) * half)
                piece = outer_back(dq_ref[span, :], wq_ref[...]) + dot(small_grad[span, :], weight)
                parts[side] = piece.astype(BF16)

        kv_rows = wk.shape[0]
        head = pl.BlockSpec((seq_len, HD), lambda j, *_: (j, 0))
        return self.chain.run(
            body,
            "linear_back",
            (self.micro,),
            [
                (dq, pl.BlockSpec((seq_len, cols), lambda j, *_: (j, 0))),
                (dkv, pl.BlockSpec((2, seq_len, 2 * HD), lambda j, *_: (0, j, 0))),
                (front[4], head),
                (front[5], head),
                (wq, whole(width, cols)),
                (wk, whole(kv_rows, width)),
                (wv, whole(kv_rows, width)),
            ],
            [
                ((self.tokens, total), BF16, pl.BlockSpec((seq_len, total), lambda j, *_: (j, 0))),
                ((1, total), F32, whole(1, total)),
                (
                    (2, self.micro * half, width),
                    BF16,
                    pl.BlockSpec((2, half, width), lambda j, *_: (0, j, 0)),
                ),
            ],
            [pltpu.VMEM((seq_len, HD), BF16)],
        )

    def last(self, inputs, own, got, hidden_grad, small):
        half, width = self.half, self.width
        step = 128
        count = half // step
        rows = self.micro * half

        def body(scalars, ins, outs, scratch):
            x_ref, own_ref, got_ref, grad_ref, small_ref = ins
            incoming = own_ref[...].astype(F32) + got_ref[...].astype(F32)
            unit, inverse = unit_rows(x_ref[...].astype(F32))
            back = grad_ref[...] + norm_back(incoming, unit, inverse, self.gain_of(small_ref, 0))
            outs[0][...] = back.astype(BF16)
            part = jnp.sum(incoming * unit, axis=0, keepdims=True)

            @pl.when(pl.program_id(0) == 0)
            def _():
                outs[1][...] = part

            @pl.when(pl.program_id(0) > 0)
            def _():
                outs[1][...] += part

        block = pl.BlockSpec((step, width), lambda j, *_: (j, 0))
        return self.chain.run(
            body,
            "norm_one_back",
            (rows // step,),
            [
                (
                    self.halves(inputs),
                    pl.BlockSpec(
                        (None, None, step, width),
                        lambda j, place, *_: (j // count, place[0], j % count, 0),
                    ),
                ),
                (own, block),
                (got, block),
                (hidden_grad, block),
                (small, whole(1, small.shape[1])),
            ],
            [((rows, width), BF16, block), ((1, width), F32, whole(1, width))],
        )

    def result(self, state, own, got):
        rows, width = state.shape
        step = 128
        block = pl.BlockSpec((step, width), lambda j, *_: (j, 0))

        def body(scalars, ins, outs, scratch):
            value = ins[0][...] + ins[1][...].astype(F32) + ins[2][...].astype(F32)
            outs[0][...] = value.astype(BF16)

        return self.chain.run(
            body,
            "result",
            (rows // step,),
            [(state, block), (own, block), (got, block)],
            [((rows, width), BF16, block)],
        )[0]


class Halving:
    def __init__(self, chain, left, right, masks, cols, columns=None, at=0, direct=False):
        self.chain, self.left, self.right, self.masks, self.cols = chain, left, right, masks, cols
        total = left.shape[1]
        levels = len(masks)
        self.sizes = [total >> (level + 1) for level in range(levels)] + [total >> levels]
        self.starts = [total - (total >> level) for level in range(levels + 1)]
        self.parts = []
        self.columns = right.shape[2] if columns is None else columns
        self.at = at
        self.direct = direct
        self.level = 0
        self.received = []
        self.result = None

    def product(self, first, last, into=()):
        parts, _, span = self.left.shape
        tiles, tokens, tile = self.right.shape
        sizes = self.sizes[first:last]
        offset = self.starts[first]
        rows = sum(sizes)
        column, columns = self.at, self.columns

        def body(scalars, refs, outs, scratch):
            left, right, made, left_sems, in_sems, out_sems = scratch
            lefts = copies(
                [
                    (refs[0].at[part, pl.ds(offset, rows)], left.at[:, pl.ds(part * span, span)])
                    for part in range(parts)
                ],
                left_sems,
            )

            def load(index):
                return pltpu.make_async_copy(refs[1].at[index], right.at[index], in_sems.at[index])

            def stores(index):
                at = 0
                found = []
                for number, size in enumerate(sizes):
                    found.append(
                        pltpu.make_async_copy(
                            made.at[index, pl.ds(at, size)],
                            outs[number].at[index, :, pl.ds(column, tile)],
                            out_sems.at[index, number],
                        )
                    )
                    at += size
                return found

            each(tiles, lambda index: load(index).start())
            for copy in lefts:
                copy.wait()

            def one(index):
                load(index).wait()

                made[index] = dot(left[...], right[index]).astype(BF16)
                for store in stores(index):
                    store.start()

            each(tiles, one)

            def end(index):
                for store in stores(index):
                    store.wait()

            each(tiles, end)

        self.parts += self.chain.run(
            body,
            "gradient_product",
            (1,),
            [(self.left, ANYWHERE), (self.right, ANYWHERE)],
            [((tiles, size, columns), BF16, ANYWHERE) for size in sizes],
            [
                pltpu.VMEM((rows, tokens), BF16),
                pltpu.VMEM((tiles, tokens, tile), BF16),
                pltpu.VMEM((tiles, rows, tile), BF16),
                pltpu.SemaphoreType.DMA((parts,)),
                pltpu.SemaphoreType.DMA((tiles,)),
                pltpu.SemaphoreType.DMA((tiles, len(sizes))),
            ],
            into=into,
        )
        return self

    def send(self):
        if self.level == len(self.masks):
            return self
        if self.direct and self.level == len(self.masks) - 2:
            return self.send_direct()
        value = self.parts[self.level]
        if self.received:
            tiles, size, tile = value.shape
            start = self.starts[self.level]
            ins = [(value, whole(tiles, size, tile))]
            for piece, base in self.received:
                at = (start - base) // size
                ins.append((piece, pl.BlockSpec((tiles, size, tile), lambda *_, at=at: (0, at, 0))))

            def body(scalars, refs, outs, scratch):
                def one(index):
                    total = refs[0][index].astype(F32)
                    for ref in refs[1:]:
                        total = total + ref[index].astype(F32)
                    outs[0][index] = total.astype(BF16)

                each(tiles, one)

            (value,) = self.chain.run(
                body, "gradient_add", (1,), ins, [((tiles, size, tile), BF16, whole(tiles, size, tile))]
            )
        after = self.starts[self.level + 1]
        self.received.append((swap(value, "wide", self.masks[self.level]), after))
        self.level += 1
        return self

    def send_direct(self):
        first, second = self.masks[-2:]
        pair, single = self.parts[self.level], self.parts[self.level + 1]
        tiles, rows, tile = single.shape
        start = self.starts[self.level]
        ins = [(pair, whole(tiles, 2 * rows, tile)), (single, whole(tiles, rows, tile))]
        for piece, base in self.received:
            for index in range(3):
                at = (start - base) // rows + index
                ins.append((piece, pl.BlockSpec((tiles, rows, tile), lambda *_, at=at: (0, at, 0))))

        def body(scalars, refs, outs, scratch):
            def one(index):
                for block in range(3):
                    if block < 2:
                        total = refs[0][index, block * rows : (block + 1) * rows].astype(F32)
                    else:
                        total = refs[1][index].astype(F32)
                    for ref in refs[2 + block :: 3]:
                        total = total + ref[index].astype(F32)
                    outs[block][index] = total.astype(BF16)

            each(tiles, one)

        shape = (tiles, rows, tile)
        values = self.chain.run(body, "gradient_add", (1,), ins, [(shape, BF16, whole(*shape))] * 3)
        for value, mask in zip(values, (first ^ second, first, second)):
            self.received.append((swap(value, "wide", mask), self.starts[-1]))
        self.level = len(self.masks)
        return self

    def total(self):
        if self.result is not None:
            return self.result
        while self.level < len(self.masks):
            self.send()
        rows, start = self.sizes[-1], self.starts[-1]
        tiles, tile = self.right.shape[0], self.columns
        cols = self.cols
        ins = [(self.parts[-1], whole(tiles, rows, tile))]
        for piece, base in self.received:
            at = (start - base) // rows
            ins.append((piece, pl.BlockSpec((tiles, rows, tile), lambda *_, at=at: (0, at, 0))))

        def body(scalars, refs, outs, scratch):
            for index in range(tiles):
                value = refs[0][index].astype(F32)
                for ref in refs[1:]:
                    value = value + ref[index].astype(F32)
                size = min(tile, cols - index * tile)
                outs[0][:, index * tile : index * tile + size] = value[:, :size]

        (self.result,) = self.chain.run(
            body, "gradient_total", (1,), ins, [((rows, cols), F32, whole(rows, cols))]
        )
        return self.result


def doubling_sum(value, axis, masks):
    for mask in masks:
        value = value + swap(value, axis, mask)
    return value


def body(
    inputs,
    out_grad,
    norm_gain,
    query_weight,
    query_bias,
    key_weight,
    key_bias,
    value_weight,
    value_bias,
    output_weight,
    ffn_gain,
    gate_weight,
    up_weight,
    down_weight,
    lengths,
    segments,
    positions,
):
    micro, seq_len, width = inputs.shape
    cols = query_weight.shape[1]
    hidden_units = gate_weight.shape[1]
    layer = Layer(inputs, cols, hidden_units)
    half, tokens = layer.half, layer.tokens
    place = jnp.stack([layer.core, lax.axis_index("wide")]).astype(jnp.int32)
    chain = Chain([place, lengths])
    layer.chain = chain
    wide_masks = masks_of("wide")
    down_masks, up_masks, gate_masks, joint_masks = [
        [wide_masks[int(place)] for place in places] + wide_masks[3:] for places in MASKS.split()
    ]
    key_rows, value_rows = key_weight.T, value_weight.T
    gate_rows, up_rows = gate_weight.T, up_weight.T
    small = jnp.concatenate([norm_gain, ffn_gain, query_bias, key_bias, value_bias]).astype(F32)[None]
    small_oth = swap(small, "narrow", 1)
    kv = (key_rows, value_rows, swap(key_rows, "narrow", 1), swap(value_rows, "narrow", 1))
    grad_flat = out_grad.reshape(tokens, width)
    halves_grad = layer.halves(out_grad)
    front = layer.front(inputs, small, small_oth, query_weight, kv, segments, positions, output_weight)
    pair = (front[6], swap(front[7], "narrow", 1))
    one_own, one_got = layer.to_other_chip(pair, sizes=(micro * half,))
    mixed = front[0]
    (grad_turned,) = layer.turn(
        [
            (
                halves_grad,
                pl.BlockSpec((None, None, TILE, width), lambda j, *_: (j % micro, j // micro, 0, 0)),
            )
        ],
        (block_order(down_masks),),
    )
    act_grad = layer.act_grad(out_grad, down_weight)
    (one_turned,) = layer.turn(
        [(inputs.reshape(tokens, width), pl.BlockSpec((TILE, width), lambda j, *_: (j, 0)))], (block_order(joint_masks),), small
    )
    state, normed = layer.hidden_state(inputs, small, one_own, one_got)
    normed = [normed, swap(normed, "narrow", 1)]
    act, dgate, dup = layer.expand(normed, gate_rows, up_rows, act_grad)
    levels = len(wide_masks)
    lin_cols = cols + HD
    made = {}
    down = Halving(chain, grad_turned, act, down_masks, hidden_units, direct="d" in DIRECT)

    def turn_two():
        made["two"] = layer.turn_pieces(normed, (block_order(gate_masks), block_order(up_masks)))

    def up_product():
        made["up"] = Halving(chain, made["two"][1], dup, up_masks, hidden_units, direct="u" in DIRECT).product(0, levels + 1)
        made["up"].send()

    def gate_product():
        made["gate"] = Halving(chain, made["two"][0], dgate, gate_masks, hidden_units, direct="g" in DIRECT).product(0, levels + 1)
        made["gate"].send()

    def shrink_two():
        made["two_sum"] = layer.across(layer.shrink([(dgate, gate_rows), (dup, up_rows)]))

    def shrink_ffn():
        made["ffn"] = layer.shrink([(act, down_weight)])

    def across_ffn():
        made["ffn_sum"] = layer.across(made["ffn"])

    def middle():
        made["hidden_grad"], branch, made["ffn_gain"] = layer.middle(state, *made["two_sum"], out_grad, small)
        made["branch"] = pair_exchange(branch)

    def back():
        made["dq"], made["dkv"] = layer.back(front, segments, made["branch"], output_weight)

    def linear():
        made["lin_grad"], made["bias"], parts = layer.linear_back(
            front, made["dq"], pair_exchange(made["dkv"]), query_weight, key_rows, value_rows
        )
        made["one_sum"] = layer.across(parts)

    def linear_product():
        right = made["lin_grad"][None]
        made["lin"] = Halving(chain, one_turned, right, joint_masks, lin_cols + cols, lin_cols + cols)
        made["lin"].product(0, levels + 1)

    def turn_branch():
        (made["branch_turned"],) = layer.turn_pieces([made["branch"].reshape(tokens, width)], (block_order(joint_masks),))

    def output_product():
        right = mixed.reshape(1, tokens, cols)
        both = lin_cols + cols
        made["joint"] = Halving(chain, made["branch_turned"], right, joint_masks, both, both, lin_cols, "l" in DIRECT)
        made["joint"].product(0, levels + 1, tuple(made["lin"].parts)).send()

    def result():
        own = layer.result(state, made["ffn_sum"][0], made["ffn_sum"][1][0])
        made["result"] = (own, swap(own, "narrow", 1))

    def last():
        own, made["norm_gain"] = layer.last(
            inputs, made["one_sum"][0], made["one_sum"][1][0], made["hidden_grad"], small
        )
        made["input"] = (own, swap(own, "narrow", 1))

    def pack():
        packed = share_wide(made["small"] + chain.token[:1, :1])
        made["packed"] = (packed, packed[0, cols + HD :])

    def pair_gains():
        gains = jnp.concatenate([made["norm_gain"], made["ffn_gain"]], axis=1)
        both = pair_exchange(jnp.broadcast_to(gains, (2, 2 * width)))
        small = jnp.concatenate([made["bias"], (both[0] + both[1])[None]], axis=1)
        (made["small"],) = chain.hold(small)

    def total(name):
        made[name + "_out"] = made[name].total()

    made["down"] = down
    steps = {
        "pk": pack,
        "gp": pair_gains,
        "pd1": lambda: down.product(0, 1).send(),
        "pdr": lambda: down.product(1, levels + 1),
        "tn": turn_two,
        "pu": up_product,
        "pg": gate_product,
        "s2": shrink_two,
        "sF": shrink_ffn,
        "xF": across_ffn,
        "mid": middle,
        "bk": back,
        "ln": linear,
        "plo": linear_product,
        "ta": turn_branch,
        "pout": output_product,
        "res": result,
        "last": last,
        "jr": lambda: made.update(result_out=layer.join(*made["result"])),
        "ji": lambda: made.update(input_out=layer.join(*made["input"])),
        "ad": lambda: down.send(),
        "au": lambda: made["up"].send(),
        "ag": lambda: made["gate"].send(),
        "al": lambda: made["joint"].send(),
        "td": lambda: total("down"),
        "tu": lambda: total("up"),
        "tg": lambda: total("gate"),
        "tl": lambda: total("joint"),
    }
    for name in " ".join(ORDER).split():
        if name.startswith("c"):
            chain.scale = 1e8 * int(name[1:])
        else:
            steps[name]()
    result, input_grad = made["result_out"], made["input_out"]
    down_out, up_out, gate_out = made["down_out"], made["up_out"], made["gate_out"]
    lin_out, output_out = made["joint_out"][:, :lin_cols], made["joint_out"][:, lin_cols:]
    packed, gain_out = made["packed"]
    part = HD // 2
    query_out, key_out, value_out = jnp.split(lin_out, [cols, cols + part], axis=1)
    query_bias_out, key_bias_out, value_bias_out, _ = jnp.split(
        packed[0], [cols, cols + part, cols + 2 * part]
    )
    norm_gain_out, ffn_gain_out = gain_out[:width], gain_out[width:]
    return (
        result,
        input_grad,
        norm_gain_out,
        query_out,
        query_bias_out,
        key_out,
        key_bias_out,
        value_out,
        value_bias_out,
        output_out.T,
        ffn_gain_out,
        gate_out,
        up_out,
        down_out.T,
    )


def solution(mesh):
    placed = (
        P("wide", None, None),
        P("wide", None, None),
        P(),
        P(None, "narrow"),
        P("narrow"),
        P(None, "narrow"),
        P("narrow"),
        P(None, "narrow"),
        P("narrow"),
        P("narrow", None),
        P(),
        P(None, "narrow"),
        P(None, "narrow"),
        P("narrow", None),
        P("wide"),
        P("wide", None),
        P("wide", None),
    )
    return jax.shard_map(
        body,
        mesh=mesh,
        in_specs=placed,
        out_specs=(
            P("wide", None, None),
            P("wide", None, None),
            P(),
            P("wide", "narrow"),
            P("narrow"),
            P("wide", "narrow"),
            P("narrow"),
            P("wide", "narrow"),
            P("narrow"),
            P("narrow", "wide"),
            P(),
            P("wide", "narrow"),
            P("wide", "narrow"),
            P("narrow", "wide"),
        ),
        check_vma=False,
    )
```
